256 devices in a mesh: ctx: 32 (over z, x), head: 8 (over y, core).
Axes of the slice: x: 4, y: 4, z: 8, core: 2. Of those that a mesh axis runs over, the one named last changes fastest.
Arguments:
- queries: bfloat16 [256, 4096], P(None, 'head'), may hold values from -40 to 40
- keys: bfloat16 [64, 2048, 2048], P('ctx', None, 'head'), may hold values from -6 to 6
- values: bfloat16 [64, 2048, 2048], P('ctx', None, 'head'), may hold values from -6 to 6
- page_map: int32 [64], replicated, may hold values from 0 to 63, each once
- selected: int32 [2, 8], replicated, may hold values from 0 to 63, as said below
- residual_in: bfloat16 [256, 5376], P('head', 'ctx'), may hold values from -7 to 7
- out_weight: bfloat16 [4096, 5376], P('head', 'ctx'), may hold values from -0.09375 to 0.09375
- norm_gain: float32 [5376], P('ctx'), may hold values from 0.5 to 1.5
- gate_weight: bfloat16 [5376, 21504], P('head', 'ctx'), may hold values from -0.078125 to 0.078125
- up_weight: bfloat16 [5376, 21504], P('head', 'ctx'), may hold values from -0.078125 to 0.078125
- down_weight: bfloat16 [21504, 5376], P('ctx', 'head'), may hold values from -0.0390625 to 0.0390625
Outputs:
- layer_out: bfloat16 [256, 5376], P('ctx', 'head')
The draws below stay inside these ranges and needn't reach their ends.
Inputs may be any that keep to these rules, and one draw needn't show every extreme that they name: `selected`: each row names 8 different logical pages, among them 64 - 1, the page that holds the block's own positions.
All inputs are finite; a program needn't handle non-finite values.
Results may differ from the reference program's by a relative error of at most 0.02.
Values may be sent and summed in bfloat16 or wider, within the bound.
No kernel may reach another device: no remote copies, remote signals or barrier semaphores. Data moves between devices by JAX's collectives and lax.ppermute only.
A program may use at most 128 MiB of HBM per device.

```python
import jax
import jax.numpy as jnp
from jax import lax

D = 5376
FF = 21504
QUERY_HEADS = 32
KEY_VALUE_HEADS = 16
HEAD_SIZE = 128
PAGE_TOKENS = 2048
TILE_QUERY_ROWS = 128
PAGES_PER_TILE = 8
TILES = 2
CACHE_PAGES = 64


def insert_vectors(key):
    sign_values = jax.random.bernoulli(jax.random.fold_in(key, 7), 0.5, (KEY_VALUE_HEADS, HEAD_SIZE))
    return jnp.where(sign_values, 1.0, -1.0).astype(jnp.float32)


def marked_slots(key):
    chosen = jax.random.bernoulli(jax.random.fold_in(key, 8), 0.5, (CACHE_PAGES,))
    return chosen.at[0].set(True)


def draw_queries(key, part):
    row_count = TILES * TILE_QUERY_ROWS
    base_vector = jnp.clip(3.0 * jax.random.normal(jax.random.fold_in(key, 1), (row_count, QUERY_HEADS * HEAD_SIZE), jnp.float32), -24.0, 24.0)
    vector_rows = insert_vectors(key)
    inserted_rows = jnp.repeat(vector_rows, QUERY_HEADS // KEY_VALUE_HEADS, axis=0).reshape(QUERY_HEADS * HEAD_SIZE)
    row_ids = jnp.arange(row_count)
    target = 130.0 + 50.0 * (row_ids // TILE_QUERY_ROWS % 3).astype(jnp.float32)
    strength = jnp.minimum(target * 168.0 ** 0.5 / (5.0 * HEAD_SIZE), 40.0)
    marked = row_ids % TILE_QUERY_ROWS == TILE_QUERY_ROWS // 2
    base_vector = jnp.where(marked[:, None], strength[:, None] * inserted_rows[None, :], base_vector)
    return base_vector.astype(jnp.bfloat16)


def draw_keys(key, part):
    base_vector = jnp.clip(jax.random.normal(jax.random.fold_in(key, 2), (CACHE_PAGES, PAGE_TOKENS, KEY_VALUE_HEADS * HEAD_SIZE), jnp.float32), -6.0, 6.0)
    vector_rows = 5.0 * insert_vectors(key).reshape(KEY_VALUE_HEADS * HEAD_SIZE)
    hot = marked_slots(key)[:, None]
    base_vector = base_vector.at[:, 0, :].set(jnp.where(hot, vector_rows[None, :], base_vector[:, 0, :]))
    base_vector = base_vector.at[:, 1, :].set(jnp.where(hot, 0.992 * vector_rows[None, :], base_vector[:, 1, :]))
    return base_vector.astype(jnp.bfloat16)


def draw_selected(key, part):
    popular = jax.random.randint(jax.random.fold_in(key, 3), (CACHE_PAGES,), 0, 4)
    jitter = jax.random.randint(jax.random.fold_in(key, 4), (TILES, CACHE_PAGES), 0, 64)
    page_ids = jnp.arange(CACHE_PAGES, dtype=jnp.int32)
    ranking = (popular[None, :] * 64 + jitter) * CACHE_PAGES + page_ids[None, :]
    ranking = jnp.where(page_ids[None, :] == CACHE_PAGES - 1, 1 << 29, ranking)
    picked = lax.top_k(ranking, PAGES_PER_TILE)[1]
    return picked.astype(jnp.int32)


def draw_residual_in(key, part):
    row_count = TILES * TILE_QUERY_ROWS
    row_scale = jnp.exp(jax.random.uniform(jax.random.fold_in(key, 5), (row_count, 1), jnp.float32, -0.69, 0.4))
    column = jnp.arange(D).astype(jnp.float32) / D
    column_scale = 0.5 * 3.0 ** column
    base_vector = jnp.clip(jax.random.normal(jax.random.fold_in(key, 6), (row_count, D), jnp.float32), -3.0, 3.0)
    return (base_vector * row_scale * column_scale[None, :]).astype(jnp.bfloat16)


def levels(own_key, extent, cuts, least, top_value):
    def one(dim, blocks):
        heights = jax.random.uniform(jax.random.fold_in(jax.random.fold_in(own_key, 6), dim), (blocks,), jnp.float32, least / len(cuts), top_value / len(cuts))
        return jnp.repeat(jnp.exp(heights), extent[dim] // blocks).reshape((-1,) + (1,) * (len(extent) - dim - 1))

    gain = one(*cuts[0])
    for cut in cuts[1:]:
        gain = gain * one(*cut)
    return gain


def gaussian(stream_key, extent, width, reach, split=(), kind=jnp.bfloat16):
    entries = width * jax.random.normal(stream_key, extent, jnp.float32)
    if split:
        entries = entries * levels(stream_key, extent, split, -0.22, 0.18)
    return jnp.clip(entries, -reach, reach).astype(kind)


def setup_inputs(seed: int = 0) -> dict:
    splits = jax.random.split(jax.random.key(seed), 12)
    queries = draw_queries(jax.random.fold_in(splits[11], 71), 0)
    keys = draw_keys(jax.random.fold_in(splits[11], 71), 0)
    values = gaussian(splits[2], (CACHE_PAGES, PAGE_TOKENS, KEY_VALUE_HEADS * HEAD_SIZE), 1.0, 6.0, ((0, 32), (2, 8)))
    page_map = jax.random.permutation(splits[3], CACHE_PAGES).astype(jnp.int32)
    selected = draw_selected(jax.random.fold_in(splits[11], 71), 0)
    residual_in = draw_residual_in(jax.random.fold_in(splits[11], 71), 0)
    out_weight = gaussian(splits[6], (QUERY_HEADS * HEAD_SIZE, D), (QUERY_HEADS * HEAD_SIZE) ** -0.5, 0.09375, ((0, 8), (1, 32)))
    norm_gain = jnp.clip(0.5 + 1.0 * jax.random.uniform(splits[7], (D,), jnp.float32) ** levels(splits[7], (D,), ((0, 32),), -0.2, 0.2), 0.5, 1.5)
    gate_weight = gaussian(splits[8], (D, FF), D ** -0.5, 0.078125, ((0, 8), (1, 32)))
    up_weight = gaussian(splits[9], (D, FF), D ** -0.5, 0.078125, ((0, 8), (1, 32)))
    down_weight = gaussian(splits[10], (FF, D), FF ** -0.5, 0.0390625, ((0, 32), (1, 8)))
    return dict(queries=queries, keys=keys, values=values, page_map=page_map, selected=selected, residual_in=residual_in, out_weight=out_weight, norm_gain=norm_gain, gate_weight=gate_weight, up_weight=up_weight, down_weight=down_weight)


score_scale = 168.0 ** (-0.5)
masked_score = -1e+30
norm_epsilon = 1e-06

def reference(queries, keys, values, page_map, selected, residual_in, out_weight, norm_gain, gate_weight, up_weight, down_weight):
    row_count = TILES * TILE_QUERY_ROWS
    offset = PAGE_TOKENS - row_count
    query_group_size = QUERY_HEADS // KEY_VALUE_HEADS
    slot_ids = jnp.take(page_map, selected, axis=0).astype(jnp.int32)
    is_causal = selected == CACHE_PAGES - 1
    key_position = jnp.arange(PAGE_TOKENS, dtype=jnp.int32)

    def one_tile(inputs):
        tile_query_rows, tile_page_slots, tile_causal, tile_index = inputs
        tile_key_rows = jnp.take(keys, tile_page_slots, axis=0).reshape(PAGES_PER_TILE * PAGE_TOKENS, KEY_VALUE_HEADS, HEAD_SIZE).astype(jnp.float32)
        tile_value_rows = jnp.take(values, tile_page_slots, axis=0).reshape(PAGES_PER_TILE * PAGE_TOKENS, KEY_VALUE_HEADS, HEAD_SIZE).astype(jnp.float32)
        grouped_queries = tile_query_rows.reshape(TILE_QUERY_ROWS, KEY_VALUE_HEADS, query_group_size, HEAD_SIZE).astype(jnp.float32)
        scores = jnp.einsum('qkgd,jkd->kgqj', grouped_queries, tile_key_rows) * score_scale
        query_position = offset + tile_index * TILE_QUERY_ROWS + jnp.arange(TILE_QUERY_ROWS, dtype=jnp.int32)
        visible = jnp.logical_or(jnp.logical_not(tile_causal)[:, None, None], key_position[None, None, :] <= query_position[None, :, None])
        visible = jnp.transpose(visible, (1, 0, 2)).reshape(TILE_QUERY_ROWS, PAGES_PER_TILE * PAGE_TOKENS)
        scores = jnp.where(visible[None, None], scores, masked_score)
        row_max = lax.optimization_barrier(jnp.max(scores, axis=-1, keepdims=True))
        weights = jnp.where(visible[None, None], jnp.exp(scores - row_max), 0.0)
        row_total = lax.optimization_barrier(jnp.sum(weights, axis=-1))
        rounded = lax.optimization_barrier(weights.astype(jnp.bfloat16)).astype(jnp.float32)
        mixture = jnp.einsum('kgqj,jkd->qkgd', rounded, tile_value_rows)
        mixture = mixture / jnp.transpose(row_total, (2, 0, 1))[..., None]
        return mixture.reshape(TILE_QUERY_ROWS, QUERY_HEADS * HEAD_SIZE).astype(jnp.bfloat16)
    tiled = queries.reshape(TILES, TILE_QUERY_ROWS, QUERY_HEADS * HEAD_SIZE)
    attention = lax.map(one_tile, (tiled, slot_ids, is_causal, jnp.arange(TILES, dtype=jnp.int32)))
    attention = attention.reshape(row_count, QUERY_HEADS * HEAD_SIZE)
    projected = jnp.dot(attention, out_weight, preferred_element_type=jnp.float32)
    stream = (residual_in.astype(jnp.float32) + projected).astype(jnp.bfloat16)
    stream_float = stream.astype(jnp.float32)
    mean_square = lax.optimization_barrier(jnp.mean(stream_float * stream_float, axis=-1, keepdims=True))
    normed = (stream_float * lax.rsqrt(mean_square + norm_epsilon) * norm_gain).astype(jnp.bfloat16)
    gate = jnp.dot(normed, gate_weight, preferred_element_type=jnp.float32)
    upward = jnp.dot(normed, up_weight, preferred_element_type=jnp.float32)
    hidden = (jax.nn.gelu(gate, approximate=True) * upward).astype(jnp.bfloat16)
    mlp_out = jnp.dot(hidden, down_weight, preferred_element_type=jnp.float32)
    return (stream_float + mlp_out).astype(jnp.bfloat16)
```

```python
import functools
import math

import jax
import jax.numpy as jnp
from jax import lax
from jax.experimental import pallas as pl
from jax.experimental.pallas import tpu as pltpu
from jax.sharding import Mesh
from jax.sharding import PartitionSpec as P

D = 5376
HEAD = 128
LAST_PAGE = 63
BF = jnp.bfloat16
F32 = jnp.float32
NEG = -1e30
EXP2_SCALE = 168.0 ** (-0.5) * math.log2(math.e)
EPSILON = 1e-06
CTX = ("z", "x")
HEADS = ("y", "core")
ALL = ("z", "x", "y", "core")
NZ, NX, NY, NC = 8, 4, 4, 2
GU_HALF = 768

VMEM = pl.BlockSpec(memory_space=pltpu.VMEM)
SMEM = pl.BlockSpec(memory_space=pltpu.SMEM)
HBM = pl.BlockSpec(memory_space=pl.ANY)


def pieces(value):
    high = value.astype(BF).astype(F32)
    rest = value - high
    middle = rest.astype(BF).astype(F32)
    return high, middle, rest - middle


def attend_kernel(
    pm, sel, me, q_ref, k_hbm, v_hbm, o_ref, kbuf, vbuf, ksem, vsem, s_ref, m_ref, l_ref, acc_ref
):
    chosen = [[jnp.int32(0), jnp.int32(0)], [jnp.int32(0), jnp.int32(0)]]
    causal = [jnp.int32(0), jnp.int32(0)]
    for t in range(2):
        for j in range(8):
            logical = sel[t, j]
            slot = pm[logical]
            for p in range(2):
                hit = (slot == me[0] * 2 + p).astype(jnp.int32)
                chosen[p][t] = chosen[p][t] | hit
                causal[p] = causal[p] | (hit * (logical == LAST_PAGE).astype(jnp.int32))
    used = [chosen[p][0] | chosen[p][1] for p in range(2)]

    def copies(p):
        return (
            pltpu.make_async_copy(k_hbm.at[p], kbuf.at[p], ksem.at[p]),
            pltpu.make_async_copy(v_hbm.at[p], vbuf.at[p], vsem.at[p]),
        )

    for p in range(2):

        @pl.when(used[p] != 0)
        def _(p=p):
            for c in copies(p):
                c.start()

    m_ref[...] = jnp.full_like(m_ref, NEG)
    l_ref[...] = jnp.zeros_like(l_ref)
    acc_ref[...] = jnp.zeros_like(acc_ref)

    def combo(p, t, is_causal):
        row = lax.broadcasted_iota(jnp.int32, (256, 512), 0)
        col = lax.broadcasted_iota(jnp.int32, (256, 512), 1)
        limit = jnp.where(is_causal != 0, 1792 - 1536 + t * 128, 1 << 20)
        visible = col <= (row & 127) + limit
        rows = pl.ds(pl.multiple_of(t * 128, 128), 128)
        for kv in range(2):
            lanes = slice(kv * 128, (kv + 1) * 128)
            q2 = jnp.concatenate(
                [q_ref[rows, (2 * kv + g) * 128 : (2 * kv + g + 1) * 128] for g in range(2)], axis=0
            )
            top = jnp.full((256, 128), NEG, F32)
            for j in range(4):
                s = lax.dot_general(
                    q2,
                    kbuf[p, j * 512 : (j + 1) * 512, lanes],
                    (((1,), (1,)), ((), ())),
                    preferred_element_type=F32,
                )
                if j == 3:
                    s = jnp.where(visible, s, NEG)
                s_ref[:, j * 512 : (j + 1) * 512] = s
                for a in range(4):
                    top = jnp.maximum(top, s[:, a * 128 : (a + 1) * 128])
            i = t * 2 + kv
            m_old = m_ref[i]
            m_new = jnp.maximum(m_old, jnp.max(top, axis=1, keepdims=True))
            alpha = jnp.exp2((m_old - m_new) * EXP2_SCALE)
            m_wide = jnp.concatenate([m_new] * 4, axis=1)
            total = jnp.zeros((256, 128), F32)
            mixture = acc_ref[i] * alpha
            for j in range(4):
                w = jnp.exp2((s_ref[:, j * 512 : (j + 1) * 512] - m_wide) * EXP2_SCALE)
                for a in range(4):
                    total = total + w[:, a * 128 : (a + 1) * 128]
                mixture = mixture + jnp.dot(
                    w.astype(BF),
                    vbuf[p, j * 512 : (j + 1) * 512, lanes],
                    preferred_element_type=F32,
                )
            m_ref[i] = m_new
            l_ref[i] = l_ref[i] * alpha + jnp.sum(total, axis=1, keepdims=True)
            acc_ref[i] = mixture

    for p in range(2):

        @pl.when(used[p] != 0)
        def _(p=p):
            for c in copies(p):
                c.wait()

            def tile(t, carry):
                picked = jnp.where(t == 0, chosen[p][0], chosen[p][1])

                @pl.when(picked != 0)
                def _():
                    combo(p, t, causal[p])

                return carry

            lax.fori_loop(0, 2, tile, 0)

    lane = lax.broadcasted_iota(jnp.int32, (128, 128), 1)
    for t in range(2):
        block = jnp.zeros((128, 128), F32)
        for h in range(4):
            i, rows = t * 2 + h // 2, slice((h % 2) * 128, (h % 2 + 1) * 128)
            total = l_ref[i, rows, :]
            some = total > 0.0
            safe = jnp.where(some, total, 1.0)
            level = jnp.where(some, m_ref[i, rows, :] * EXP2_SCALE + jnp.log2(safe), NEG)
            o_ref[t * 128 : (t + 1) * 128, h * 128 : (h + 1) * 128] = (
                acc_ref[i, rows, :] / safe
            ).astype(BF)
            for n, piece in enumerate(pieces(level)):
                block = jnp.where(lane == h + 4 * n, piece, block)
        o_ref[t * 128 : (t + 1) * 128, 512:640] = block.astype(BF)


def attend(page_map, selected, me, queries, keys, values):
    return pl.pallas_call(
        attend_kernel,
        out_shape=jax.ShapeDtypeStruct((256, 640), BF),
        in_specs=[SMEM, SMEM, SMEM, VMEM, HBM, HBM],
        out_specs=VMEM,
        scratch_shapes=[
            pltpu.VMEM((2, 2048, 256), BF),
            pltpu.VMEM((2, 2048, 256), BF),
            pltpu.SemaphoreType.DMA((2,)),
            pltpu.SemaphoreType.DMA((2,)),
            pltpu.VMEM((256, 2048), F32),
            pltpu.VMEM((4, 256, 128), F32),
            pltpu.VMEM((4, 256, 128), F32),
            pltpu.VMEM((4, 256, 128), F32),
        ],
        compiler_params=pltpu.CompilerParams(vmem_limit_bytes=32 << 20),
        cost_estimate=pl.CostEstimate(
            flops=4 * 10**9, transcendentals=4 * 10**6, bytes_accessed=10 * 2**20
        ),
        name="attend",
    )(page_map, selected, me, queries, keys, values)


def merge_kernel(x_ref, o_ref):
    x = x_ref[...].astype(F32)
    marks = x[:, :, 512:640].reshape(256, 128).astype(BF)
    source = lax.broadcasted_iota(jnp.int32, (128, 512), 0)
    target = lax.broadcasted_iota(jnp.int32, (128, 512), 1)
    spread = jnp.where((source < 12) & ((source & 3) == target // 128), 1.0, 0.0).astype(BF)
    level = jnp.dot(marks, spread, preferred_element_type=F32).reshape(32, 8, 512)
    top = jnp.max(level, axis=0, keepdims=True)
    weight = jnp.exp2(level - top)
    total = jnp.sum(weight, axis=0)
    mixed = jnp.sum(weight * x[:, :, :512], axis=0)
    o_ref[...] = (mixed / total).astype(BF)


def project_kernel(a_ref, w_ref, o_ref):
    a = a_ref[...]
    for z in range(NZ):
        o_ref[z] = jnp.dot(
            a, w_ref[z * 512 : (z + 1) * 512, :], preferred_element_type=F32
        ).astype(BF)


def gate_up_kernel(ids, x_ref, g_ref, u_ref, mine_ref, other_ref, own_ref, stream, normed):
    for x in range(NX):
        lanes = slice(x * 168, (x + 1) * 168)
        block = x_ref[:, x, :, :].astype(F32)
        part = block[:, :32, :].reshape(256, 168)
        tail = block[0, 32:40, :]
        gain = tail[0:1] + tail[1:2] + tail[2:3]
        stream[:, lanes] = part
        normed[:, lanes] = (part * gain).astype(BF)
    own_ref[...] = stream[pl.ds(pl.multiple_of(ids[0] * 8, 8), 8), :].astype(BF)
    core = ids[1]
    lane = lax.broadcasted_iota(jnp.int32, (128, GU_HALF - 672), 1)
    for ref, start in ((other_ref, (1 - core) * 128), (mine_ref, core * 128)):
        rows = pl.ds(pl.multiple_of(start, 128), 128)
        a = normed[rows, :]
        s = stream[rows, :]
        squares = jnp.sum(s * s, axis=1, keepdims=True)
        marks = jnp.zeros((128, GU_HALF - 672), F32)
        for n, piece in enumerate(pieces(squares)):
            marks = jnp.where(lane == n, piece, marks)
        ref[:, 0:672] = jnp.dot(a, g_ref[...], preferred_element_type=F32).astype(BF)
        ref[:, 672:GU_HALF] = marks.astype(BF)
        ref[:, GU_HALF : GU_HALF + 672] = jnp.dot(
            a, u_ref[...], preferred_element_type=F32
        ).astype(BF)
        ref[:, GU_HALF + 672 :] = jnp.zeros((128, GU_HALF - 672), BF)


def pair_kernel(a_ref, b_ref, o_ref):
    both = a_ref[...].astype(F32) + b_ref[...].astype(F32)
    o_ref[...] = both.astype(BF)
    squares = both[:, 672:673] + both[:, 673:674] + both[:, 674:675]
    lane = lax.broadcasted_iota(jnp.int32, (128, GU_HALF - 672), 1)
    marks = jnp.zeros((128, GU_HALF - 672), F32)
    for n, piece in enumerate(pieces(squares)):
        marks = jnp.where(lane == n, piece, marks)
    o_ref[:, 672:GU_HALF] = marks.astype(BF)


def hidden_kernel(x_ref, o_ref):
    both = jnp.sum(x_ref[...].astype(F32), axis=0)
    squares = both[:, 672:673] + both[:, 673:674] + both[:, 674:675]
    factor = lax.rsqrt(squares / D + EPSILON)
    gate = both[:, 0:672] * factor
    up = both[:, GU_HALF : GU_HALF + 672] * factor
    o_ref[...] = (jax.nn.gelu(gate, approximate=True) * up).astype(BF)


def down_kernel(ids, a_ref, b_ref, w_ref, o_ref):
    core = ids[1]
    for ref, start in ((a_ref, core * 128), (b_ref, (1 - core) * 128)):
        rows = pl.ds(pl.multiple_of(start, 128), 128)
        o_ref[rows, :] = jnp.dot(ref[...], w_ref[...], preferred_element_type=F32).astype(BF)


def final_kernel(x_ref, s_ref, o_ref):
    o_ref[...] = (jnp.sum(x_ref[...].astype(F32), axis=0) + s_ref[...].astype(F32)).astype(BF)


def call(kernel, shapes, specs, *args, scratch=()):
    many = isinstance(shapes, list)
    outs = [jax.ShapeDtypeStruct(s, BF) for s in (shapes if many else [shapes])]
    return pl.pallas_call(
        kernel,
        out_shape=outs if many else outs[0],
        in_specs=specs,
        out_specs=[VMEM] * len(outs) if many else VMEM,
        scratch_shapes=scratch,
        compiler_params=pltpu.CompilerParams(vmem_limit_bytes=32 << 20),
        name=kernel.__name__,
    )(*args)


def exchange(parts, axis):
    return lax.all_to_all(parts, axis, split_axis=0, concat_axis=0, tiled=True)


def to_all(part, axis):
    return exchange(jnp.broadcast_to(part, (lax.axis_size(axis), *part.shape)), axis)


def place(z, x, h):
    return (z * NX + x) * NY * NC + h


def shards(
    queries, keys, values, page_map, selected, residual_in, out_weight, norm_gain, gate_weight, up_weight, down_weight
):
    ctx = (lax.axis_index("z") * NX + lax.axis_index("x")).astype(jnp.int32)
    core = lax.axis_index("core").astype(jnp.int32)
    ids = jnp.stack([ctx, core])
    wide_weight = lax.all_gather(out_weight, "z", axis=0, tiled=True)
    gain_high = lax.reduce_precision(norm_gain, 8, 7)
    gain_rest = norm_gain - gain_high
    gain_middle = lax.reduce_precision(gain_rest, 8, 7)
    gain_rows = jnp.stack([gain_high, gain_middle, gain_rest - gain_middle]).astype(BF)
    carried = jnp.concatenate([residual_in, gain_rows, jnp.zeros((5, 168), BF)], axis=0)
    turned = lax.ppermute(
        carried,
        ALL,
        [(place(z, x, h), place(h, x, z)) for z in range(NZ) for x in range(NX) for h in range(NZ)],
    )

    sent = attend(page_map, selected, ids, queries, keys, values)
    arrived = exchange(sent.reshape(32, 8, 640), CTX)
    share = call(merge_kernel, (8, 512), [VMEM], arrived)
    attention = to_all(share, "x").reshape(32, 512)
    partial = call(project_kernel, (NZ, 32, 168), [VMEM, VMEM], attention, wide_weight)
    projected = exchange(partial, HEADS).astype(F32).sum(axis=0)
    stream = (turned[:32].astype(F32) + projected).astype(BF)
    rows = to_all(jnp.concatenate([stream, turned[32:]], axis=0), CTX)
    mine, other, own_stream = call(
        gate_up_kernel,
        [(128, 2 * GU_HALF), (128, 2 * GU_HALF), (8, 672)],
        [SMEM, VMEM, VMEM, VMEM],
        ids,
        rows.reshape(NZ, NX, 40, 168),
        gate_weight,
        up_weight,
        scratch=[pltpu.VMEM((256, 672), F32), pltpu.VMEM((256, 672), BF)],
    )
    swap = [(0, 1), (1, 0)]
    pair = call(pair_kernel, (128, 2 * GU_HALF), [VMEM, VMEM], mine, lax.ppermute(other, "core", swap))
    quarters = exchange(pair.reshape(NY, 32, 2 * GU_HALF), "y")
    hidden = call(hidden_kernel, (32, 672), [VMEM], quarters)
    hidden_half = to_all(hidden, "y").reshape(128, 672)
    hidden_other = lax.ppermute(hidden_half, "core", swap)
    down = call(
        down_kernel, (256, 672), [SMEM, VMEM, VMEM, VMEM], ids, hidden_half, hidden_other, down_weight
    )
    out_parts = exchange(down.reshape(32, 8, 672), CTX)
    return call(final_kernel, (8, 672), [VMEM, VMEM], out_parts, own_stream)


def solution(mesh):
    fine = Mesh(mesh.devices.reshape(NZ, NX, NY, NC), ALL)
    in_specs = (
        P(None, HEADS),
        P(CTX, None, HEADS),
        P(CTX, None, HEADS),
        P(),
        P(),
        P(HEADS, CTX),
        P(HEADS, CTX),
        P(CTX),
        P(HEADS, CTX),
        P(HEADS, CTX),
        P(CTX, HEADS),
    )
    return jax.shard_map(shards, mesh=fine, in_specs=in_specs, out_specs=P(CTX, HEADS), check_vma=False)
```

```python
import functools
import math

import jax
import jax.numpy as jnp
from jax import lax
from jax.experimental import pallas as pl
from jax.experimental.pallas import tpu as pltpu
from jax.sharding import Mesh
from jax.sharding import PartitionSpec as P

D = 5376
HEAD = 128
LAST_PAGE = 63
BF = jnp.bfloat16
F32 = jnp.float32
NEG = -1e30
EXP2_SCALE = 168.0 ** (-0.5) * math.log2(math.e)
EPSILON = 1e-06
CTX = ("z", "x")
HEADS = ("y", "core")
ALL = ("z", "x", "y", "core")
NZ, NX, NY, NC = 8, 4, 4, 2
GU_HALF = 768

VMEM = pl.BlockSpec(memory_space=pltpu.VMEM)
SMEM = pl.BlockSpec(memory_space=pltpu.SMEM)
HBM = pl.BlockSpec(memory_space=pltpu.HBM)


def pieces(value):
    high = value.astype(BF).astype(F32)
    rest = value - high
    middle = rest.astype(BF).astype(F32)
    return high, middle, rest - middle


def attend_kernel(
    pm_hbm, sel_hbm, ids, gain_hbm, q_hbm, k_hbm, v_hbm, o_ref,
    pm, sel, gain_ref, q_ref, kbuf, vbuf, sems, ksem, vsem, s_ref, m_ref, l_ref, acc_ref,
):
    tables = (
        pltpu.make_async_copy(pm_hbm, pm, sems.at[0]),
        pltpu.make_async_copy(sel_hbm, sel, sems.at[1]),
    )
    late = (
        pltpu.make_async_copy(q_hbm, q_ref, sems.at[2]),
        pltpu.make_async_copy(gain_hbm, gain_ref, sems.at[3]),
    )
    for c in tables:
        c.start()
    for c in late:
        c.start()
    for c in tables:
        c.wait()
    chosen = [[jnp.int32(0), jnp.int32(0)], [jnp.int32(0), jnp.int32(0)]]
    causal = [jnp.int32(0), jnp.int32(0)]
    for t in range(2):
        for j in range(8):
            logical = sel[t, j]
            slot = pm[logical]
            for p in range(2):
                hit = (slot == ids[0] * 2 + p).astype(jnp.int32)
                chosen[p][t] = chosen[p][t] | hit
                causal[p] = causal[p] | (hit * (logical == LAST_PAGE).astype(jnp.int32))
    used = [chosen[p][0] | chosen[p][1] for p in range(2)]

    def copies(p):
        return (
            pltpu.make_async_copy(k_hbm.at[p], kbuf.at[p], ksem.at[p]),
            pltpu.make_async_copy(v_hbm.at[p], vbuf.at[p], vsem.at[p]),
        )

    for p in range(2):

        @pl.when(used[p] != 0)
        def _(p=p):
            for c in copies(p):
                c.start()

    for c in late:
        c.wait()
    m_ref[...] = jnp.full_like(m_ref, NEG)
    l_ref[...] = jnp.zeros_like(l_ref)
    acc_ref[...] = jnp.zeros_like(acc_ref)

    def combo(p, t, is_causal):
        row = lax.broadcasted_iota(jnp.int32, (256, 512), 0)
        col = lax.broadcasted_iota(jnp.int32, (256, 512), 1)
        limit = jnp.where(is_causal != 0, 1792 - 1536 + t * 128, 1 << 20)
        visible = col <= (row & 127) + limit
        rows = pl.ds(pl.multiple_of(t * 128, 128), 128)
        for kv in range(2):
            lanes = slice(kv * 128, (kv + 1) * 128)
            q2 = jnp.concatenate(
                [q_ref[rows, (2 * kv + g) * 128 : (2 * kv + g + 1) * 128] for g in range(2)], axis=0
            )
            top = jnp.full((256, 128), NEG, F32)
            for j in range(4):
                s = lax.dot_general(
                    q2,
                    kbuf[p, j * 512 : (j + 1) * 512, lanes],
                    (((1,), (1,)), ((), ())),
                    preferred_element_type=F32,
                )
                if j == 3:
                    s = jnp.where(visible, s, NEG)
                s_ref[kv, :, j * 512 : (j + 1) * 512] = s
                for a in range(4):
                    top = jnp.maximum(top, s[:, a * 128 : (a + 1) * 128])
            i = t * 2 + kv
            m_old = m_ref[i]
            m_new = jnp.maximum(m_old, jnp.max(top, axis=1, keepdims=True))
            alpha = jnp.exp2((m_old - m_new) * EXP2_SCALE)
            m_wide = jnp.concatenate([m_new] * 4, axis=1)
            total = jnp.zeros((256, 128), F32)
            mixture = acc_ref[i] * alpha
            for j in range(4):
                w = jnp.exp2((s_ref[kv, :, j * 512 : (j + 1) * 512] - m_wide) * EXP2_SCALE)
                for a in range(4):
                    total = total + w[:, a * 128 : (a + 1) * 128]
                mixture = mixture + jnp.dot(
                    w.astype(BF),
                    vbuf[p, j * 512 : (j + 1) * 512, lanes],
                    preferred_element_type=F32,
                )
            m_ref[i] = m_new
            l_ref[i] = l_ref[i] * alpha + jnp.sum(total, axis=1, keepdims=True)
            acc_ref[i] = mixture

    for p in range(2):

        @pl.when(used[p] != 0)
        def _(p=p):
            for c in copies(p):
                c.wait()

            def tile(t, carry):
                picked = jnp.where(t == 0, chosen[p][0], chosen[p][1])

                @pl.when(picked != 0)
                def _():
                    combo(p, t, causal[p])

                return carry

            lax.fori_loop(0, 2, tile, 0)

    lane = lax.broadcasted_iota(jnp.int32, (128, 128), 1)
    halves = []
    for piece in pieces(gain_ref[...]):
        halves += [piece[:, :84], piece[:, 84:168]]
    halves += [jnp.zeros((1, 84), F32)] * 2
    gains = jnp.concatenate(
        [jnp.zeros((8, 16), F32), jnp.concatenate(halves, axis=0), jnp.zeros((8, 28), F32)], axis=1
    )
    gains = jnp.concatenate([gains] * 16, axis=0)
    for t in range(2):
        block = gains
        for h in range(4):
            i, rows = t * 2 + h // 2, slice((h % 2) * 128, (h % 2 + 1) * 128)
            total = l_ref[i, rows, :]
            some = total > 0.0
            safe = jnp.where(some, total, 1.0)
            level = jnp.where(some, m_ref[i, rows, :] * EXP2_SCALE + jnp.log2(safe), NEG)
            o_ref[t * 128 : (t + 1) * 128, h * 128 : (h + 1) * 128] = (
                acc_ref[i, rows, :] / safe
            ).astype(BF)
            for n, piece in enumerate(pieces(level)):
                block = jnp.where(lane == h + 4 * n, piece, block)
        o_ref[t * 128 : (t + 1) * 128, 512:640] = block.astype(BF)


def in_hbm(array):
    return pltpu.with_memory_space_constraint(array, pltpu.HBM)


def attend(page_map, selected, ids, gain, queries, keys, values):
    return pl.pallas_call(
        attend_kernel,
        out_shape=jax.ShapeDtypeStruct((256, 640), BF),
        in_specs=[HBM, HBM, SMEM, HBM, HBM, HBM, HBM],
        out_specs=VMEM,
        scratch_shapes=[
            pltpu.SMEM((64,), jnp.int32),
            pltpu.SMEM((2, 8), jnp.int32),
            pltpu.VMEM((1, 168), F32),
            pltpu.VMEM((256, 512), BF),
            pltpu.VMEM((2, 2048, 256), BF),
            pltpu.VMEM((2, 2048, 256), BF),
            pltpu.SemaphoreType.DMA((4,)),
            pltpu.SemaphoreType.DMA((2,)),
            pltpu.SemaphoreType.DMA((2,)),
            pltpu.VMEM((2, 256, 2048), F32),
            pltpu.VMEM((4, 256, 128), F32),
            pltpu.VMEM((4, 256, 128), F32),
            pltpu.VMEM((4, 256, 128), F32),
        ],
        compiler_params=pltpu.CompilerParams(vmem_limit_bytes=32 << 20),
        cost_estimate=pl.CostEstimate(
            flops=4 * 10**9, transcendentals=4 * 10**6, bytes_accessed=10 * 2**20
        ),
        name="attend",
    )(in_hbm(page_map), in_hbm(selected), ids, in_hbm(gain), in_hbm(queries), in_hbm(keys), in_hbm(values))


def merge_kernel(ids, x_ref, o_ref, gain_ref):
    x = x_ref[...].astype(F32)
    marks = x[:, :, 512:640].reshape(256, 128).astype(BF)
    source = lax.broadcasted_iota(jnp.int32, (128, 512), 0)
    target = lax.broadcasted_iota(jnp.int32, (128, 512), 1)
    spread = jnp.where((source < 12) & ((source & 3) == target // 128), 1.0, 0.0).astype(BF)
    level = jnp.dot(marks, spread, preferred_element_type=F32).reshape(32, 8, 512)
    top = jnp.max(level, axis=0, keepdims=True)
    weight = jnp.exp2(level - top)
    total = jnp.sum(weight, axis=0)
    mixed = jnp.sum(weight * x[:, :, :512], axis=0)
    share = (mixed / total).astype(BF)
    for k in range(NX):
        o_ref[k] = share
        gain = x_ref[ids[2] * NX + k, :, 512:640].astype(F32)
        for half in range(2):
            gain_ref[k : k + 1, half * 84 : half * 84 + 84] = (
                gain[half : half + 1, 16:100]
                + gain[half + 2 : half + 3, 16:100]
                + gain[half + 4 : half + 5, 16:100]
            )


def packed(rows):
    rest = rows[:, 128:168]
    return jnp.concatenate(
        [
            rows[:, :128],
            jnp.concatenate([rest[:16], rest[16:], jnp.zeros((16, 48), rows.dtype)], axis=1),
        ],
        axis=0,
    )


def project_kernel(a_ref, w_hbm, o_ref, wbuf, sems):
    copies = [
        pltpu.make_async_copy(w_hbm.at[z], wbuf.at[z], sems.at[z]) for z in range(NZ)
    ]
    for c in copies:
        c.start()
    a = a_ref[...]
    for z in range(NZ):
        copies[z].wait()
        block = lax.dot_general(
            a,
            wbuf[z],
            (((1,), (1,)), ((), ())),
            preferred_element_type=F32,
        )
        o_ref[z] = packed(block).astype(BF)


def stream_kernel(x_ref, r_ref, o_ref):
    total = jnp.sum(x_ref[...].astype(F32), axis=0) + packed(r_ref[...].astype(F32))
    stream = total.astype(BF)
    for k in range(NZ * NX):
        o_ref[k] = stream


def gate_up_kernel(ids, x_ref, gain_ref, g_ref, u_ref, mine_ref, other_ref, own_ref, stream, normed):
    for x in range(NX):
        block = x_ref[:, x, :, :].astype(F32)
        main = block[:, :32, :].reshape(256, 128)
        rest = jnp.concatenate([block[:, 32:48, 0:40], block[:, 32:48, 40:80]], axis=1)
        rest = rest.reshape(256, 40)
        first, second = slice(x * 168, x * 168 + 128), slice(x * 168 + 128, x * 168 + 168)
        stream[:, first] = main
        stream[:, second] = rest
        normed[:, first] = (main * gain_ref[x : x + 1, 0:128]).astype(BF)
        normed[:, second] = (rest * gain_ref[x : x + 1, 128:168]).astype(BF)
    own_ref[...] = stream[pl.ds(pl.multiple_of(ids[0] * 8, 8), 8), :].astype(BF)
    core = ids[1]
    lane = lax.broadcasted_iota(jnp.int32, (128, GU_HALF - 672), 1)
    for ref, start in ((other_ref, (1 - core) * 128), (mine_ref, core * 128)):
        rows = pl.ds(pl.multiple_of(start, 128), 128)
        a = normed[rows, :]
        s = stream[rows, :]
        squares = jnp.sum(s * s, axis=1, keepdims=True)
        marks = jnp.zeros((128, GU_HALF - 672), F32)
        for n, piece in enumerate(pieces(squares)):
            marks = jnp.where(lane == n, piece, marks)
        ref[:, 0:672] = jnp.dot(a, g_ref[...], preferred_element_type=F32).astype(BF)
        ref[:, 672:GU_HALF] = marks.astype(BF)
        ref[:, GU_HALF : GU_HALF + 672] = jnp.dot(
            a, u_ref[...], preferred_element_type=F32
        ).astype(BF)
        ref[:, GU_HALF + 672 :] = jnp.zeros((128, GU_HALF - 672), BF)


def pair_kernel(a_ref, b_ref, o_ref):
    both = a_ref[...].astype(F32) + b_ref[...].astype(F32)
    o_ref[...] = both.astype(BF)
    squares = both[:, 672:673] + both[:, 673:674] + both[:, 674:675]
    lane = lax.broadcasted_iota(jnp.int32, (128, GU_HALF - 672), 1)
    marks = jnp.zeros((128, GU_HALF - 672), F32)
    for n, piece in enumerate(pieces(squares)):
        marks = jnp.where(lane == n, piece, marks)
    o_ref[:, 672:GU_HALF] = marks.astype(BF)


def hidden_kernel(x_ref, o_ref):
    both = jnp.sum(x_ref[...].astype(F32), axis=0)
    squares = both[:, 672:673] + both[:, 673:674] + both[:, 674:675]
    factor = lax.rsqrt(squares / D + EPSILON)
    gate = both[:, 0:672] * factor
    up = both[:, GU_HALF : GU_HALF + 672] * factor
    hidden = (jax.nn.gelu(gate, approximate=True) * up).astype(BF)
    for k in range(NY):
        o_ref[k] = hidden


def down_kernel(ids, a_ref, b_ref, w_ref, o_ref):
    core = ids[1]
    for ref, start in ((a_ref, core * 128), (b_ref, (1 - core) * 128)):
        rows = pl.ds(pl.multiple_of(start, 128), 128)
        o_ref[rows, :] = jnp.dot(ref[...], w_ref[...], preferred_element_type=F32).astype(BF)


def final_kernel(x_ref, s_ref, o_ref):
    o_ref[...] = (jnp.sum(x_ref[...].astype(F32), axis=0) + s_ref[...].astype(F32)).astype(BF)


def call(kernel, outs, specs, *args, scratch=()):
    outs = [jax.ShapeDtypeStruct(shape, dtype) for shape, dtype in outs]
    results = pl.pallas_call(
        kernel,
        out_shape=outs,
        in_specs=specs,
        out_specs=[VMEM] * len(outs),
        scratch_shapes=scratch,
        compiler_params=pltpu.CompilerParams(vmem_limit_bytes=32 << 20),
        name=kernel.__name__,
    )(*args)
    return results if len(outs) > 1 else results[0]


def exchange(parts, axis):
    return lax.all_to_all(parts, axis, split_axis=0, concat_axis=0, tiled=True)


def place(z, x, h):
    return (z * NX + x) * NY * NC + h


def shards(
    queries, keys, values, page_map, selected, residual_in, out_weight, norm_gain, gate_weight, up_weight, down_weight
):
    ctx = (lax.axis_index("z") * NX + lax.axis_index("x")).astype(jnp.int32)
    core = lax.axis_index("core").astype(jnp.int32)
    head = lax.axis_index("y").astype(jnp.int32) * NC + core
    ids = jnp.stack([ctx, core, head])
    wide_weight = lax.all_gather(out_weight.T[None], "z", axis=0, tiled=True)
    residual = lax.ppermute(
        residual_in,
        ALL,
        [(place(z, x, h), place(h, x, z)) for z in range(NZ) for x in range(NX) for h in range(NZ)],
    )
    sent = attend(page_map, selected, ids, norm_gain.reshape(1, 168), queries, keys, values)
    sent, residual = lax.optimization_barrier((sent, residual))
    arrived = exchange(sent.reshape(32, 8, 640), CTX)
    shares, gain = call(
        merge_kernel, [((NX, 8, 512), BF), ((NX, 168), F32)], [SMEM, VMEM], ids, arrived
    )
    attention = exchange(shares, "x").reshape(32, 512)
    partial = call(
        project_kernel,
        [((NZ, 48, 128), BF)],
        [VMEM, HBM],
        attention,
        in_hbm(wide_weight),
        scratch=[pltpu.VMEM((NZ, 168, 512), BF), pltpu.SemaphoreType.DMA((NZ,))],
    )
    projected = exchange(partial, HEADS)
    streams = call(stream_kernel, [((NZ * NX, 48, 128), BF)], [VMEM, VMEM], projected, residual)
    rows = exchange(streams, CTX)
    half = ((128, 2 * GU_HALF), BF)
    mine, other, own_stream = call(
        gate_up_kernel,
        [half, half, ((8, 672), BF)],
        [SMEM, VMEM, VMEM, VMEM, VMEM],
        ids,
        rows.reshape(NZ, NX, 48, 128),
        gain,
        gate_weight,
        up_weight,
        scratch=[pltpu.VMEM((256, 672), F32), pltpu.VMEM((256, 672), BF)],
    )
    swap = [(0, 1), (1, 0)]
    pair = call(pair_kernel, [half], [VMEM, VMEM], mine, lax.ppermute(other, "core", swap))
    quarters = exchange(pair.reshape(NY, 32, 2 * GU_HALF), "y")
    hidden = call(hidden_kernel, [((NY, 32, 672), BF)], [VMEM], quarters)
    hidden_half = exchange(hidden, "y").reshape(128, 672)
    hidden_other = lax.ppermute(hidden_half, "core", swap)
    down = call(
        down_kernel,
        [((256, 672), BF)],
        [SMEM, VMEM, VMEM, VMEM],
        ids,
        hidden_half,
        hidden_other,
        down_weight,
    )
    out_parts = exchange(down.reshape(32, 8, 672), CTX)
    return call(final_kernel, [((8, 672), BF)], [VMEM, VMEM], out_parts, own_stream)


def solution(mesh):
    fine = Mesh(mesh.devices.reshape(NZ, NX, NY, NC), ALL)
    in_specs = (
        P(None, HEADS),
        P(CTX, None, HEADS),
        P(CTX, None, HEADS),
        P(),
        P(),
        P(HEADS, CTX),
        P(HEADS, CTX),
        P(CTX),
        P(HEADS, CTX),
        P(HEADS, CTX),
        P(CTX, HEADS),
    )
    return jax.shard_map(shards, mesh=fine, in_specs=in_specs, out_specs=P(CTX, HEADS), check_vma=False)
```

```python
import functools
import math

import jax
import jax.numpy as jnp
from jax import lax
from jax.experimental import pallas as pl
from jax.experimental.pallas import tpu as pltpu
from jax.sharding import Mesh
from jax.sharding import PartitionSpec as P

D = 5376
HEAD = 128
LAST_PAGE = 63
BF = jnp.bfloat16
F32 = jnp.float32
NEG = -1e30
EXP2_SCALE = 168.0 ** (-0.5) * math.log2(math.e)
EPSILON = 1e-06
CTX = ("z", "x")
HEADS = ("y", "core")
ALL = ("z", "x", "y", "core")
NZ, NX, NY, NC = 8, 4, 4, 2
GU_HALF = 768

VMEM = pl.BlockSpec(memory_space=pltpu.VMEM)
SMEM = pl.BlockSpec(memory_space=pltpu.SMEM)
HBM = pl.BlockSpec(memory_space=pltpu.HBM)


def pieces(value):
    high = value.astype(BF).astype(F32)
    rest = value - high
    middle = rest.astype(BF).astype(F32)
    return high, middle, rest - middle


def attend_kernel(
    pm_hbm, sel_hbm, ids, gain_hbm, q_hbm, k_hbm, v_hbm, o_ref,
    pm, sel, gain_ref, q_ref, kbuf, vbuf, sems, ksem, vsem, s_ref, m_ref, l_ref, acc_ref,
):
    tables = (
        pltpu.make_async_copy(pm_hbm, pm, sems.at[0]),
        pltpu.make_async_copy(sel_hbm, sel, sems.at[1]),
    )
    late = (
        pltpu.make_async_copy(q_hbm, q_ref, sems.at[2]),
        pltpu.make_async_copy(gain_hbm, gain_ref, sems.at[3]),
    )
    for c in tables:
        c.start()
    for c in late:
        c.start()
    for c in tables:
        c.wait()
    chosen = [[jnp.int32(0), jnp.int32(0)], [jnp.int32(0), jnp.int32(0)]]
    causal = [jnp.int32(0), jnp.int32(0)]
    for t in range(2):
        for j in range(8):
            logical = sel[t, j]
            slot = pm[logical]
            for p in range(2):
                hit = (slot == ids[0] * 2 + p).astype(jnp.int32)
                chosen[p][t] = chosen[p][t] | hit
                causal[p] = causal[p] | (hit * (logical == LAST_PAGE).astype(jnp.int32))
    used = [chosen[p][0] | chosen[p][1] for p in range(2)]

    def copies(p):
        return (
            pltpu.make_async_copy(k_hbm.at[p], kbuf.at[p], ksem.at[p]),
            pltpu.make_async_copy(v_hbm.at[p], vbuf.at[p], vsem.at[p]),
        )

    for p in range(2):

        @pl.when(used[p] != 0)
        def _(p=p):
            for c in copies(p):
                c.start()

    for c in late:
        c.wait()
    m_ref[...] = jnp.full_like(m_ref, NEG)
    l_ref[...] = jnp.zeros_like(l_ref)
    acc_ref[...] = jnp.zeros_like(acc_ref)

    def combo(p, t, is_causal):
        row = lax.broadcasted_iota(jnp.int32, (256, 512), 0)
        col = lax.broadcasted_iota(jnp.int32, (256, 512), 1)
        limit = jnp.where(is_causal != 0, 1792 - 1536 + t * 128, 1 << 20)
        visible = col <= (row & 127) + limit
        rows = pl.ds(pl.multiple_of(t * 128, 128), 128)
        for kv in range(2):
            lanes = slice(kv * 128, (kv + 1) * 128)
            q2 = jnp.concatenate(
                [q_ref[rows, (2 * kv + g) * 128 : (2 * kv + g + 1) * 128] for g in range(2)], axis=0
            )
            top = jnp.full((256, 128), NEG, F32)
            for j in range(4):
                s = lax.dot_general(
                    q2,
                    kbuf[p, j * 512 : (j + 1) * 512, lanes],
                    (((1,), (1,)), ((), ())),
                    preferred_element_type=F32,
                )
                if j == 3:
                    s = jnp.where(visible, s, NEG)
                s_ref[kv, :, j * 512 : (j + 1) * 512] = s
                for a in range(4):
                    top = jnp.maximum(top, s[:, a * 128 : (a + 1) * 128])
            i = t * 2 + kv
            m_old = m_ref[i]
            m_new = jnp.maximum(m_old, jnp.max(top, axis=1, keepdims=True))
            alpha = jnp.exp2((m_old - m_new) * EXP2_SCALE)
            m_wide = jnp.concatenate([m_new] * 4, axis=1)
            total = jnp.zeros((256, 128), F32)
            mixture = acc_ref[i] * alpha
            for j in range(4):
                w = jnp.exp2((s_ref[kv, :, j * 512 : (j + 1) * 512] - m_wide) * EXP2_SCALE)
                for a in range(4):
                    total = total + w[:, a * 128 : (a + 1) * 128]
                mixture = mixture + jnp.dot(
                    w.astype(BF),
                    vbuf[p, j * 512 : (j + 1) * 512, lanes],
                    preferred_element_type=F32,
                )
            m_ref[i] = m_new
            l_ref[i] = l_ref[i] * alpha + jnp.sum(total, axis=1, keepdims=True)
            acc_ref[i] = mixture

    for p in range(2):

        @pl.when(used[p] != 0)
        def _(p=p):
            for c in copies(p):
                c.wait()

            def tile(t, carry):
                picked = jnp.where(t == 0, chosen[p][0], chosen[p][1])

                @pl.when(picked != 0)
                def _():
                    combo(p, t, causal[p])

                return carry

            lax.fori_loop(0, 2, tile, 0)

    lane = lax.broadcasted_iota(jnp.int32, (128, 128), 1)
    halves = []
    for piece in pieces(gain_ref[...]):
        halves += [piece[:, :84], piece[:, 84:168]]
    halves += [jnp.zeros((1, 84), F32)] * 2
    gains = jnp.concatenate(
        [jnp.zeros((8, 16), F32), jnp.concatenate(halves, axis=0), jnp.zeros((8, 28), F32)], axis=1
    )
    gains = jnp.concatenate([gains] * 16, axis=0)
    for t in range(2):
        block = gains
        for h in range(4):
            i, rows = t * 2 + h // 2, slice((h % 2) * 128, (h % 2 + 1) * 128)
            total = l_ref[i, rows, :]
            some = total > 0.0
            safe = jnp.where(some, total, 1.0)
            level = jnp.where(some, m_ref[i, rows, :] * EXP2_SCALE + jnp.log2(safe), NEG)
            o_ref[t * 128 : (t + 1) * 128, h * 128 : (h + 1) * 128] = (
                acc_ref[i, rows, :] / safe
            ).astype(BF)
            for n, piece in enumerate(pieces(level)):
                block = jnp.where(lane == h + 4 * n, piece, block)
        o_ref[t * 128 : (t + 1) * 128, 512:640] = block.astype(BF)


def in_hbm(array):
    return pltpu.with_memory_space_constraint(array, pltpu.HBM)


def attend(page_map, selected, ids, gain, queries, keys, values):
    return pl.pallas_call(
        attend_kernel,
        out_shape=jax.ShapeDtypeStruct((256, 640), BF),
        in_specs=[HBM, HBM, SMEM, HBM, HBM, HBM, HBM],
        out_specs=VMEM,
        scratch_shapes=[
            pltpu.SMEM((64,), jnp.int32),
            pltpu.SMEM((2, 8), jnp.int32),
            pltpu.VMEM((1, 168), F32),
            pltpu.VMEM((256, 512), BF),
            pltpu.VMEM((2, 2048, 256), BF),
            pltpu.VMEM((2, 2048, 256), BF),
            pltpu.SemaphoreType.DMA((4,)),
            pltpu.SemaphoreType.DMA((2,)),
            pltpu.SemaphoreType.DMA((2,)),
            pltpu.VMEM((2, 256, 2048), F32),
            pltpu.VMEM((4, 256, 128), F32),
            pltpu.VMEM((4, 256, 128), F32),
            pltpu.VMEM((4, 256, 128), F32),
        ],
        compiler_params=pltpu.CompilerParams(vmem_limit_bytes=32 << 20),
        cost_estimate=pl.CostEstimate(
            flops=4 * 10**9, transcendentals=4 * 10**6, bytes_accessed=10 * 2**20
        ),
        name="attend",
    )(in_hbm(page_map), in_hbm(selected), ids, in_hbm(gain), in_hbm(queries), in_hbm(keys), in_hbm(values))


def merge_kernel(ids, x_ref, o_ref, gain_ref):
    x = x_ref[...].astype(F32)
    marks = x[:, :, 512:640].reshape(256, 128).astype(BF)
    source = lax.broadcasted_iota(jnp.int32, (128, 512), 0)
    target = lax.broadcasted_iota(jnp.int32, (128, 512), 1)
    spread = jnp.where((source < 12) & ((source & 3) == target // 128), 1.0, 0.0).astype(BF)
    level = jnp.dot(marks, spread, preferred_element_type=F32).reshape(32, 8, 512)
    top = jnp.max(level, axis=0, keepdims=True)
    weight = jnp.exp2(level - top)
    total = jnp.sum(weight, axis=0)
    mixed = jnp.sum(weight * x[:, :, :512], axis=0)
    share = (mixed / total).astype(BF)
    for k in range(NZ * NX):
        o_ref[k] = share
    for k in range(NX):
        gain = x_ref[ids[2] * NX + k, :, 512:640].astype(F32)
        for half in range(2):
            gain_ref[k : k + 1, half * 84 : half * 84 + 84] = (
                gain[half : half + 1, 16:100]
                + gain[half + 2 : half + 3, 16:100]
                + gain[half + 4 : half + 5, 16:100]
            )


def packed(rows):
    rest = rows[:, 128:168]
    return jnp.concatenate(
        [
            rows[:, :128],
            jnp.concatenate([rest[:16], rest[16:], jnp.zeros((16, 48), rows.dtype)], axis=1),
        ],
        axis=0,
    )


def project_kernel(a_ref, w_ref, o_ref):
    block = lax.dot_general(
        a_ref[...], w_ref[...], (((1,), (1,)), ((), ())), preferred_element_type=F32
    )
    for h in range(NZ):
        o_ref[h] = packed(block[h * 32 : (h + 1) * 32]).astype(BF)


def stream_kernel(x_ref, r_ref, o_ref):
    total = jnp.sum(x_ref[...].astype(F32), axis=0) + packed(r_ref[...].astype(F32))
    o_ref[...] = total.astype(BF)


def gate_up_kernel(ids, x_ref, gain_ref, g_ref, u_ref, mine_ref, other_ref, own_ref, stream, normed):
    for x in range(NX):
        block = x_ref[:, x, :, :].astype(F32)
        main = block[:, :32, :].reshape(256, 128)
        rest = jnp.concatenate([block[:, 32:48, 0:40], block[:, 32:48, 40:80]], axis=1)
        rest = rest.reshape(256, 40)
        first, second = slice(x * 168, x * 168 + 128), slice(x * 168 + 128, x * 168 + 168)
        stream[:, first] = main
        stream[:, second] = rest
        normed[:, first] = (main * gain_ref[x : x + 1, 0:128]).astype(BF)
        normed[:, second] = (rest * gain_ref[x : x + 1, 128:168]).astype(BF)
    own_ref[...] = stream[pl.ds(pl.multiple_of(ids[0] * 8, 8), 8), :].astype(BF)
    core = ids[1]
    lane = lax.broadcasted_iota(jnp.int32, (128, GU_HALF - 672), 1)
    for ref, start in ((other_ref, (1 - core) * 128), (mine_ref, core * 128)):
        rows = pl.ds(pl.multiple_of(start, 128), 128)
        a = normed[rows, :]
        s = stream[rows, :]
        squares = jnp.sum(s * s, axis=1, keepdims=True)
        marks = jnp.zeros((128, GU_HALF - 672), F32)
        for n, piece in enumerate(pieces(squares)):
            marks = jnp.where(lane == n, piece, marks)
        ref[:, 0:672] = jnp.dot(a, g_ref[...], preferred_element_type=F32).astype(BF)
        ref[:, 672:GU_HALF] = marks.astype(BF)
        ref[:, GU_HALF : GU_HALF + 672] = jnp.dot(
            a, u_ref[...], preferred_element_type=F32
        ).astype(BF)
        ref[:, GU_HALF + 672 :] = jnp.zeros((128, GU_HALF - 672), BF)


def pair_kernel(a_ref, b_ref, o_ref):
    both = a_ref[...].astype(F32) + b_ref[...].astype(F32)
    o_ref[...] = both.astype(BF)
    squares = both[:, 672:673] + both[:, 673:674] + both[:, 674:675]
    lane = lax.broadcasted_iota(jnp.int32, (128, GU_HALF - 672), 1)
    marks = jnp.zeros((128, GU_HALF - 672), F32)
    for n, piece in enumerate(pieces(squares)):
        marks = jnp.where(lane == n, piece, marks)
    o_ref[:, 672:GU_HALF] = marks.astype(BF)


def hidden_kernel(x_ref, o_ref):
    both = jnp.sum(x_ref[...].astype(F32), axis=0)
    squares = both[:, 672:673] + both[:, 673:674] + both[:, 674:675]
    factor = lax.rsqrt(squares / D + EPSILON)
    gate = both[:, 0:672] * factor
    up = both[:, GU_HALF : GU_HALF + 672] * factor
    hidden = (jax.nn.gelu(gate, approximate=True) * up).astype(BF)
    for k in range(NY):
        o_ref[k] = hidden


def down_kernel(ids, a_ref, b_ref, w_ref, o_ref):
    core = ids[1]
    for ref, start in ((a_ref, core * 128), (b_ref, (1 - core) * 128)):
        rows = pl.ds(pl.multiple_of(start, 128), 128)
        o_ref[rows, :] = jnp.dot(ref[...], w_ref[...], preferred_element_type=F32).astype(BF)


def final_kernel(x_ref, s_ref, o_ref):
    o_ref[...] = (jnp.sum(x_ref[...].astype(F32), axis=0) + s_ref[...].astype(F32)).astype(BF)


def call(kernel, outs, specs, *args, scratch=()):
    outs = [jax.ShapeDtypeStruct(shape, dtype) for shape, dtype in outs]
    results = pl.pallas_call(
        kernel,
        out_shape=outs,
        in_specs=specs,
        out_specs=[VMEM] * len(outs),
        scratch_shapes=scratch,
        compiler_params=pltpu.CompilerParams(vmem_limit_bytes=32 << 20),
        name=kernel.__name__,
    )(*args)
    return results if len(outs) > 1 else results[0]


def exchange(parts, axis):
    return lax.all_to_all(parts, axis, split_axis=0, concat_axis=0, tiled=True)


def place(z, x, h):
    return (z * NX + x) * NY * NC + h


def shards(
    queries, keys, values, page_map, selected, residual_in, out_weight, norm_gain, gate_weight, up_weight, down_weight
):
    ctx = (lax.axis_index("z") * NX + lax.axis_index("x")).astype(jnp.int32)
    core = lax.axis_index("core").astype(jnp.int32)
    head = lax.axis_index("y").astype(jnp.int32) * NC + core
    ids = jnp.stack([ctx, core, head])
    sent = attend(page_map, selected, ids, norm_gain.reshape(1, 168), queries, keys, values)
    arrived = exchange(sent.reshape(32, 8, 640), CTX)
    shares, gain = call(
        merge_kernel, [((NZ * NX, 8, 512), BF), ((NX, 168), F32)], [SMEM, VMEM], ids, arrived
    )
    attention = exchange(shares, CTX).reshape(256, 512)
    partial = call(project_kernel, [((NZ, 48, 128), BF)], [VMEM, VMEM], attention, out_weight.T)
    projected = exchange(partial, HEADS)
    stream = call(stream_kernel, [((48, 128), BF)], [VMEM, VMEM], projected, residual_in)
    turned = lax.ppermute(
        stream,
        ALL,
        [(place(z, x, h), place(h, x, z)) for z in range(NZ) for x in range(NX) for h in range(NZ)],
    )
    rows = exchange(jnp.broadcast_to(turned, (NZ * NX, 48, 128)), CTX)
    half = ((128, 2 * GU_HALF), BF)
    mine, other, own_stream = call(
        gate_up_kernel,
        [half, half, ((8, 672), BF)],
        [SMEM, VMEM, VMEM, VMEM, VMEM],
        ids,
        rows.reshape(NZ, NX, 48, 128),
        gain,
        gate_weight,
        up_weight,
        scratch=[pltpu.VMEM((256, 672), F32), pltpu.VMEM((256, 672), BF)],
    )
    swap = [(0, 1), (1, 0)]
    pair = call(pair_kernel, [half], [VMEM, VMEM], mine, lax.ppermute(other, "core", swap))
    quarters = exchange(pair.reshape(NY, 32, 2 * GU_HALF), "y")
    hidden = call(hidden_kernel, [((NY, 32, 672), BF)], [VMEM], quarters)
    hidden_half = exchange(hidden, "y").reshape(128, 672)
    hidden_other = lax.ppermute(hidden_half, "core", swap)
    down = call(
        down_kernel,
        [((256, 672), BF)],
        [SMEM, VMEM, VMEM, VMEM],
        ids,
        hidden_half,
        hidden_other,
        down_weight,
    )
    out_parts = exchange(down.reshape(32, 8, 672), CTX)
    return call(final_kernel, [((8, 672), BF)], [VMEM, VMEM], out_parts, own_stream)


def solution(mesh):
    fine = Mesh(mesh.devices.reshape(NZ, NX, NY, NC), ALL)
    in_specs = (
        P(None, HEADS),
        P(CTX, None, HEADS),
        P(CTX, None, HEADS),
        P(),
        P(),
        P(HEADS, CTX),
        P(HEADS, CTX),
        P(CTX),
        P(HEADS, CTX),
        P(HEADS, CTX),
        P(CTX, HEADS),
    )
    return jax.shard_map(shards, mesh=fine, in_specs=in_specs, out_specs=P(CTX, HEADS), check_vma=False)
```

```python
import functools
import math

import jax
import jax.numpy as jnp
from jax import lax
from jax.experimental import pallas as pl
from jax.experimental.pallas import tpu as pltpu
from jax.sharding import Mesh
from jax.sharding import PartitionSpec as P

D = 5376
HEAD = 128
LAST_PAGE = 63
BF = jnp.bfloat16
F32 = jnp.float32
NEG = -1e30
EXP2_SCALE = 168.0 ** (-0.5) * math.log2(math.e)
EPSILON = 1e-06
CTX = ("z", "x")
HEADS = ("y", "core")
ALL = ("z", "x", "y", "core")
NZ, NX, NY, NC = 8, 4, 4, 2
GU_HALF = 768

VMEM = pl.BlockSpec(memory_space=pltpu.VMEM)
SMEM = pl.BlockSpec(memory_space=pltpu.SMEM)
HBM = pl.BlockSpec(memory_space=pltpu.HBM)


def pieces(value):
    high = value.astype(BF).astype(F32)
    rest = value - high
    middle = rest.astype(BF).astype(F32)
    return high, middle, rest - middle


def attend_kernel(
    pm_hbm, sel_hbm, ids, gain_hbm, q_hbm, k_hbm, v_hbm, o_ref,
    pm, sel, gain_ref, q_ref, kbuf, vbuf, sems, ksem, vsem, flags, m_ref, l_ref, acc_ref,
):
    tables = (
        pltpu.make_async_copy(pm_hbm, pm, sems.at[0]),
        pltpu.make_async_copy(sel_hbm, sel, sems.at[1]),
    )
    late = (
        pltpu.make_async_copy(q_hbm, q_ref, sems.at[2]),
        pltpu.make_async_copy(gain_hbm, gain_ref, sems.at[3]),
    )

    def page_copies(p):
        return (
            pltpu.make_async_copy(k_hbm.at[p], kbuf.at[p], ksem.at[p]),
            pltpu.make_async_copy(v_hbm.at[p], vbuf.at[p], vsem.at[p]),
        )

    for c in tables + late + page_copies(0) + page_copies(1):
        c.start()
    m_ref[...] = jnp.full_like(m_ref, NEG)
    l_ref[...] = jnp.zeros_like(l_ref)
    acc_ref[...] = jnp.zeros_like(acc_ref)
    for n in range(6):
        flags[n] = jnp.int32(0)
    for c in tables:
        c.wait()

    def look(n, carry):
        logical = sel[n >> 3, n & 7]
        p = pm[logical] - ids[0] * 2

        @pl.when((p == 0) | (p == 1))
        def _():
            flags[p * 2 + (n >> 3)] = jnp.int32(1)

            @pl.when(logical == LAST_PAGE)
            def _():
                flags[4 + p] = jnp.int32(1)

        return carry

    lax.fori_loop(0, 16, look, 0)
    for c in late:
        c.wait()

    def attend_tile(p, t):
        span = pl.ds(pl.multiple_of(t * 256, 256), 256)
        rows = pl.ds(pl.multiple_of(t * 128, 128), 128)
        limit = jnp.where(flags[4 + p] != 0, t * 128, 1 << 20)
        row = lax.broadcasted_iota(jnp.int32, (256, 256), 0)
        col = lax.broadcasted_iota(jnp.int32, (256, 256), 1)
        visible = col <= (row & 127) + limit

        def scores(kv):
            q = jnp.concatenate(
                [q_ref[rows, (2 * kv + g) * 128 : (2 * kv + g + 1) * 128] for g in range(2)], axis=0
            )
            s = lax.dot_general(
                q,
                kbuf[p, :, kv * 128 : (kv + 1) * 128],
                (((1,), (1,)), ((), ())),
                preferred_element_type=F32,
            )
            return jnp.concatenate([s[:, :1792], jnp.where(visible, s[:, 1792:], NEG)], axis=1)

        for kv, s in enumerate([scores(0), scores(1)]):
            old = m_ref[kv, span, :]
            top = s[:, :128]
            for a in range(1, 16):
                top = jnp.maximum(top, s[:, a * 128 : (a + 1) * 128])
            new = jnp.maximum(old, jnp.max(top, axis=1, keepdims=True))
            keep = jnp.exp2((old - new) * EXP2_SCALE)
            w = jnp.exp2((s - jnp.concatenate([new] * 16, axis=1)) * EXP2_SCALE)
            part = w[:, :128]
            for a in range(1, 16):
                part = part + w[:, a * 128 : (a + 1) * 128]
            mixed = jnp.dot(
                w.astype(BF), vbuf[p, :, kv * 128 : (kv + 1) * 128], preferred_element_type=F32
            )
            m_ref[kv, span, :] = new
            l_ref[kv, span, :] = l_ref[kv, span, :] * keep + part
            acc_ref[kv, span, :] = acc_ref[kv, span, :] * keep + mixed

    def page(p, carry):
        for c in page_copies(p):
            c.wait()

        def tile(t, carry):
            @pl.when(flags[p * 2 + t] != 0)
            def _():
                attend_tile(p, t)

            return carry

        return lax.fori_loop(0, 2, tile, carry)

    lax.fori_loop(0, 2, page, 0)

    lane = lax.broadcasted_iota(jnp.int32, (128, 128), 1)
    halves = []
    for piece in pieces(gain_ref[...]):
        halves += [piece[:, :84], piece[:, 84:168]]
    halves += [jnp.zeros((1, 84), F32)] * 2
    gains = jnp.concatenate(
        [jnp.zeros((8, 16), F32), jnp.concatenate(halves, axis=0), jnp.zeros((8, 28), F32)], axis=1
    )
    gains = jnp.concatenate([gains] * 16, axis=0)

    def finish(t, carry):
        marks = gains
        out_rows = pl.ds(pl.multiple_of(t * 128, 128), 128)
        for h in range(4):
            kv = h // 2
            rows = pl.ds(pl.multiple_of(t * 256 + (h % 2) * 128, 128), 128)
            total = jnp.sum(l_ref[kv, rows, :], axis=1, keepdims=True)
            some = total > 0.0
            safe = jnp.where(some, total, 1.0)
            level = jnp.where(some, m_ref[kv, rows, :][:, :1] * EXP2_SCALE + jnp.log2(safe), NEG)
            o_ref[out_rows, h * 128 : (h + 1) * 128] = (acc_ref[kv, rows, :] * (1.0 / safe)).astype(BF)
            for n, piece in enumerate(pieces(level)):
                marks = jnp.where(lane == h + 4 * n, piece, marks)
        o_ref[out_rows, 512:640] = marks.astype(BF)
        return carry

    lax.fori_loop(0, 2, finish, 0)


def in_hbm(array):
    return pltpu.with_memory_space_constraint(array, pltpu.HBM)


def attend(page_map, selected, ids, gain, queries, keys, values):
    return pl.pallas_call(
        attend_kernel,
        out_shape=jax.ShapeDtypeStruct((256, 640), BF),
        in_specs=[HBM, HBM, SMEM, HBM, HBM, HBM, HBM],
        out_specs=VMEM,
        scratch_shapes=[
            pltpu.SMEM((64,), jnp.int32),
            pltpu.SMEM((2, 8), jnp.int32),
            pltpu.VMEM((1, 168), F32),
            pltpu.VMEM((256, 512), BF),
            pltpu.VMEM((2, 2048, 256), BF),
            pltpu.VMEM((2, 2048, 256), BF),
            pltpu.SemaphoreType.DMA((4,)),
            pltpu.SemaphoreType.DMA((2,)),
            pltpu.SemaphoreType.DMA((2,)),
            pltpu.SMEM((8,), jnp.int32),
            pltpu.VMEM((2, 512, 128), F32),
            pltpu.VMEM((2, 512, 128), F32),
            pltpu.VMEM((2, 512, 128), F32),
        ],
        compiler_params=pltpu.CompilerParams(vmem_limit_bytes=40 << 20),
        cost_estimate=pl.CostEstimate(
            flops=4 * 10**9, transcendentals=4 * 10**6, bytes_accessed=10 * 2**20
        ),
        name="attend",
    )(in_hbm(page_map), in_hbm(selected), ids, in_hbm(gain), in_hbm(queries), in_hbm(keys), in_hbm(values))


def merge_kernel(ids, x_ref, o_ref, gain_ref):
    x = x_ref[...].astype(F32)
    marks = x[:, :, 512:640].reshape(256, 128).astype(BF)
    source = lax.broadcasted_iota(jnp.int32, (128, 512), 0)
    target = lax.broadcasted_iota(jnp.int32, (128, 512), 1)
    spread = jnp.where((source < 12) & ((source & 3) == target // 128), 1.0, 0.0).astype(BF)
    level = jnp.dot(marks, spread, preferred_element_type=F32).reshape(32, 8, 512)
    top = jnp.max(level, axis=0, keepdims=True)
    weight = jnp.exp2(level - top)
    total = jnp.sum(weight, axis=0)
    mixed = jnp.sum(weight * x[:, :, :512], axis=0)
    share = (mixed / total).astype(BF)
    for k in range(NZ * NX):
        o_ref[k] = share
    for k in range(NX):
        gain = x_ref[ids[2] * NX + k, :, 512:640].astype(F32)
        for half in range(2):
            gain_ref[k : k + 1, half * 84 : half * 84 + 84] = (
                gain[half : half + 1, 16:100]
                + gain[half + 2 : half + 3, 16:100]
                + gain[half + 4 : half + 5, 16:100]
            )


def packed(rows):
    rest = rows[:, 128:168]
    return jnp.concatenate(
        [
            rows[:, :128],
            jnp.concatenate([rest[:16], rest[16:], jnp.zeros((16, 48), rows.dtype)], axis=1),
        ],
        axis=0,
    )


def project_kernel(a_ref, w_ref, o_ref):
    block = lax.dot_general(
        a_ref[...], w_ref[...], (((1,), (1,)), ((), ())), preferred_element_type=F32
    )
    for h in range(NZ):
        o_ref[h] = packed(block[h * 32 : (h + 1) * 32]).astype(BF)


def stream_kernel(x_ref, r_ref, o_ref):
    total = jnp.sum(x_ref[...].astype(F32), axis=0) + packed(r_ref[...].astype(F32))
    o_ref[...] = total.astype(BF)


def gate_up_kernel(ids, x_ref, gain_ref, g_ref, u_ref, mine_ref, other_ref, own_ref, stream, normed):
    for x in range(NX):
        block = x_ref[:, x, :, :].astype(F32)
        main = block[:, :32, :].reshape(256, 128)
        rest = jnp.concatenate([block[:, 32:48, 0:40], block[:, 32:48, 40:80]], axis=1)
        rest = rest.reshape(256, 40)
        first, second = slice(x * 168, x * 168 + 128), slice(x * 168 + 128, x * 168 + 168)
        stream[:, first] = main
        stream[:, second] = rest
        normed[:, first] = (main * gain_ref[x : x + 1, 0:128]).astype(BF)
        normed[:, second] = (rest * gain_ref[x : x + 1, 128:168]).astype(BF)
    own_ref[...] = stream[pl.ds(pl.multiple_of(ids[0] * 8, 8), 8), :].astype(BF)
    core = ids[1]
    lane = lax.broadcasted_iota(jnp.int32, (128, GU_HALF - 672), 1)
    for ref, start in ((other_ref, (1 - core) * 128), (mine_ref, core * 128)):
        rows = pl.ds(pl.multiple_of(start, 128), 128)
        a = normed[rows, :]
        s = stream[rows, :]
        squares = jnp.sum(s * s, axis=1, keepdims=True)
        marks = jnp.zeros((128, GU_HALF - 672), F32)
        for n, piece in enumerate(pieces(squares)):
            marks = jnp.where(lane == n, piece, marks)
        ref[:, 0:672] = jnp.dot(a, g_ref[...], preferred_element_type=F32).astype(BF)
        ref[:, 672:GU_HALF] = marks.astype(BF)
        ref[:, GU_HALF : GU_HALF + 672] = jnp.dot(
            a, u_ref[...], preferred_element_type=F32
        ).astype(BF)
        ref[:, GU_HALF + 672 :] = jnp.zeros((128, GU_HALF - 672), BF)


def pair_kernel(a_ref, b_ref, o_ref):
    both = a_ref[...].astype(F32) + b_ref[...].astype(F32)
    o_ref[...] = both.astype(BF)
    squares = both[:, 672:673] + both[:, 673:674] + both[:, 674:675]
    lane = lax.broadcasted_iota(jnp.int32, (128, GU_HALF - 672), 1)
    marks = jnp.zeros((128, GU_HALF - 672), F32)
    for n, piece in enumerate(pieces(squares)):
        marks = jnp.where(lane == n, piece, marks)
    o_ref[:, 672:GU_HALF] = marks.astype(BF)


def hidden_kernel(x_ref, o_ref):
    both = jnp.sum(x_ref[...].astype(F32), axis=0)
    squares = both[:, 672:673] + both[:, 673:674] + both[:, 674:675]
    factor = lax.rsqrt(squares / D + EPSILON)
    gate = both[:, 0:672] * factor
    up = both[:, GU_HALF : GU_HALF + 672] * factor
    hidden = (jax.nn.gelu(gate, approximate=True) * up).astype(BF)
    for k in range(NY):
        o_ref[k] = hidden


def down_kernel(ids, a_ref, b_ref, w_ref, o_ref):
    core = ids[1]
    for ref, start in ((a_ref, core * 128), (b_ref, (1 - core) * 128)):
        rows = pl.ds(pl.multiple_of(start, 128), 128)
        o_ref[rows, :] = jnp.dot(ref[...], w_ref[...], preferred_element_type=F32).astype(BF)


def final_kernel(x_ref, s_ref, o_ref):
    o_ref[...] = (jnp.sum(x_ref[...].astype(F32), axis=0) + s_ref[...].astype(F32)).astype(BF)


def call(kernel, outs, specs, *args, scratch=()):
    outs = [jax.ShapeDtypeStruct(shape, dtype) for shape, dtype in outs]
    results = pl.pallas_call(
        kernel,
        out_shape=outs,
        in_specs=specs,
        out_specs=[VMEM] * len(outs),
        scratch_shapes=scratch,
        compiler_params=pltpu.CompilerParams(vmem_limit_bytes=32 << 20),
        name=kernel.__name__,
    )(*args)
    return results if len(outs) > 1 else results[0]


def exchange(parts, axis):
    return lax.all_to_all(parts, axis, split_axis=0, concat_axis=0, tiled=True)


def place(z, x, h):
    return (z * NX + x) * NY * NC + h


def shards(
    queries, keys, values, page_map, selected, residual_in, out_weight, norm_gain, gate_weight, up_weight, down_weight
):
    ctx = (lax.axis_index("z") * NX + lax.axis_index("x")).astype(jnp.int32)
    core = lax.axis_index("core").astype(jnp.int32)
    head = lax.axis_index("y").astype(jnp.int32) * NC + core
    ids = jnp.stack([ctx, core, head])
    sent = attend(page_map, selected, ids, norm_gain.reshape(1, 168), queries, keys, values)
    arrived = exchange(sent.reshape(32, 8, 640), CTX)
    shares, gain = call(
        merge_kernel, [((NZ * NX, 8, 512), BF), ((NX, 168), F32)], [SMEM, VMEM], ids, arrived
    )
    attention = exchange(shares, CTX).reshape(256, 512)
    partial = call(project_kernel, [((NZ, 48, 128), BF)], [VMEM, VMEM], attention, out_weight.T)
    projected = exchange(partial, HEADS)
    stream = call(stream_kernel, [((48, 128), BF)], [VMEM, VMEM], projected, residual_in)
    turned = lax.ppermute(
        stream,
        ALL,
        [(place(z, x, h), place(h, x, z)) for z in range(NZ) for x in range(NX) for h in range(NZ)],
    )
    rows = exchange(jnp.broadcast_to(turned, (NZ * NX, 48, 128)), CTX)
    half = ((128, 2 * GU_HALF), BF)
    mine, other, own_stream = call(
        gate_up_kernel,
        [half, half, ((8, 672), BF)],
        [SMEM, VMEM, VMEM, VMEM, VMEM],
        ids,
        rows.reshape(NZ, NX, 48, 128),
        gain,
        gate_weight,
        up_weight,
        scratch=[pltpu.VMEM((256, 672), F32), pltpu.VMEM((256, 672), BF)],
    )
    swap = [(0, 1), (1, 0)]
    pair = call(pair_kernel, [half], [VMEM, VMEM], mine, lax.ppermute(other, "core", swap))
    quarters = exchange(pair.reshape(NY, 32, 2 * GU_HALF), "y")
    hidden = call(hidden_kernel, [((NY, 32, 672), BF)], [VMEM], quarters)
    hidden_half = exchange(hidden, "y").reshape(128, 672)
    hidden_other = lax.ppermute(hidden_half, "core", swap)
    down = call(
        down_kernel,
        [((256, 672), BF)],
        [SMEM, VMEM, VMEM, VMEM],
        ids,
        hidden_half,
        hidden_other,
        down_weight,
    )
    out_parts = exchange(down.reshape(32, 8, 672), CTX)
    return call(final_kernel, [((8, 672), BF)], [VMEM, VMEM], out_parts, own_stream)


def solution(mesh):
    fine = Mesh(mesh.devices.reshape(NZ, NX, NY, NC), ALL)
    in_specs = (
        P(None, HEADS),
        P(CTX, None, HEADS),
        P(CTX, None, HEADS),
        P(),
        P(),
        P(HEADS, CTX),
        P(HEADS, CTX),
        P(CTX),
        P(HEADS, CTX),
        P(HEADS, CTX),
        P(CTX, HEADS),
    )
    return jax.shard_map(shards, mesh=fine, in_specs=in_specs, out_specs=P(CTX, HEADS), check_vma=False)
```

```python
import functools
import math

import jax
import jax.numpy as jnp
from jax import lax
from jax.experimental import pallas as pl
from jax.experimental.pallas import tpu as pltpu
from jax.sharding import Mesh
from jax.sharding import PartitionSpec as P

D = 5376
HEAD = 128
LAST_PAGE = 63
BF = jnp.bfloat16
F32 = jnp.float32
NEG = -1e30
EXP2_SCALE = 168.0 ** (-0.5) * math.log2(math.e)
EPSILON = 1e-06
CTX = ("z", "x")
HEADS = ("y", "core")
ALL = ("z", "x", "y", "core")
NZ, NX, NY, NC = 8, 4, 4, 2

VMEM = pl.BlockSpec(memory_space=pltpu.VMEM)
SMEM = pl.BlockSpec(memory_space=pltpu.SMEM)
HBM = pl.BlockSpec(memory_space=pltpu.HBM)


def pieces(value):
    high = value.astype(BF).astype(F32)
    rest = value - high
    middle = rest.astype(BF).astype(F32)
    return high, middle, rest - middle


def attend_kernel(
    pm_hbm, sel_hbm, ids, gain_hbm, q_hbm, k_hbm, v_hbm, o_ref,
    pm, sel, gain_ref, q_ref, kbuf, vbuf, sems, ksem, vsem, flags, m_ref, l_ref, acc_ref,
):
    tables = (
        pltpu.make_async_copy(pm_hbm, pm, sems.at[0]),
        pltpu.make_async_copy(sel_hbm, sel, sems.at[1]),
    )
    late = (
        pltpu.make_async_copy(q_hbm, q_ref, sems.at[2]),
        pltpu.make_async_copy(gain_hbm, gain_ref, sems.at[3]),
    )

    def page_copies(p):
        return (
            pltpu.make_async_copy(k_hbm.at[p], kbuf.at[p], ksem.at[p]),
            pltpu.make_async_copy(v_hbm.at[p], vbuf.at[p], vsem.at[p]),
        )

    for c in tables + late + page_copies(0) + page_copies(1):
        c.start()
    m_ref[...] = jnp.full_like(m_ref, NEG)
    l_ref[...] = jnp.zeros_like(l_ref)
    acc_ref[...] = jnp.zeros_like(acc_ref)
    for n in range(6):
        flags[n] = jnp.int32(0)
    for c in tables:
        c.wait()

    def look(n, carry):
        logical = sel[n >> 3, n & 7]
        p = pm[logical] - ids[0] * 2

        @pl.when((p == 0) | (p == 1))
        def _():
            flags[p * 2 + (n >> 3)] = jnp.int32(1)

            @pl.when(logical == LAST_PAGE)
            def _():
                flags[4 + p] = jnp.int32(1)

        return carry

    lax.fori_loop(0, 16, look, 0)
    for c in late:
        c.wait()

    def attend_tile(p, t):
        span = pl.ds(pl.multiple_of(t * 256, 256), 256)
        rows = pl.ds(pl.multiple_of(t * 128, 128), 128)
        limit = jnp.where(flags[4 + p] != 0, t * 128, 1 << 20)
        row = lax.broadcasted_iota(jnp.int32, (256, 256), 0)
        col = lax.broadcasted_iota(jnp.int32, (256, 256), 1)
        visible = col <= (row & 127) + limit

        def scores(kv):
            q = jnp.concatenate(
                [q_ref[rows, (2 * kv + g) * 128 : (2 * kv + g + 1) * 128] for g in range(2)], axis=0
            )
            s = lax.dot_general(
                q,
                kbuf[p, :, kv * 128 : (kv + 1) * 128],
                (((1,), (1,)), ((), ())),
                preferred_element_type=F32,
            )
            return jnp.concatenate([s[:, :1792], jnp.where(visible, s[:, 1792:], NEG)], axis=1)

        for kv, s in enumerate([scores(0), scores(1)]):
            old = m_ref[kv, span, :]
            top = s[:, :128]
            for a in range(1, 16):
                top = jnp.maximum(top, s[:, a * 128 : (a + 1) * 128])
            new = jnp.maximum(old, jnp.max(top, axis=1, keepdims=True))
            keep = jnp.exp2((old - new) * EXP2_SCALE)
            w = jnp.exp2((s - jnp.concatenate([new] * 16, axis=1)) * EXP2_SCALE)
            part = w[:, :128]
            for a in range(1, 16):
                part = part + w[:, a * 128 : (a + 1) * 128]
            mixed = jnp.dot(
                w.astype(BF), vbuf[p, :, kv * 128 : (kv + 1) * 128], preferred_element_type=F32
            )
            m_ref[kv, span, :] = new
            l_ref[kv, span, :] = l_ref[kv, span, :] * keep + part
            acc_ref[kv, span, :] = acc_ref[kv, span, :] * keep + mixed

    def page(p, carry):
        for c in page_copies(p):
            c.wait()

        def tile(t, carry):
            @pl.when(flags[p * 2 + t] != 0)
            def _():
                attend_tile(p, t)

            return carry

        return lax.fori_loop(0, 2, tile, carry)

    lax.fori_loop(0, 2, page, 0)

    lane = lax.broadcasted_iota(jnp.int32, (128, 128), 1)
    halves = []
    for piece in pieces(gain_ref[...]):
        halves += [piece[:, :84], piece[:, 84:168]]
    halves += [jnp.zeros((1, 84), F32)] * 2
    gains = jnp.concatenate(
        [jnp.zeros((8, 16), F32), jnp.concatenate(halves, axis=0), jnp.zeros((8, 28), F32)], axis=1
    )
    gains = jnp.concatenate([gains] * 16, axis=0)

    def finish(t, carry):
        marks = gains
        out_rows = pl.ds(pl.multiple_of(t * 128, 128), 128)
        for h in range(4):
            kv = h // 2
            rows = pl.ds(pl.multiple_of(t * 256 + (h % 2) * 128, 128), 128)
            total = jnp.sum(l_ref[kv, rows, :], axis=1, keepdims=True)
            some = total > 0.0
            safe = jnp.where(some, total, 1.0)
            level = jnp.where(some, m_ref[kv, rows, :][:, :1] * EXP2_SCALE + jnp.log2(safe), NEG)
            o_ref[out_rows, h * 128 : (h + 1) * 128] = (acc_ref[kv, rows, :] * (1.0 / safe)).astype(BF)
            for n, piece in enumerate(pieces(level)):
                marks = jnp.where(lane == h + 4 * n, piece, marks)
        o_ref[out_rows, 512:640] = marks.astype(BF)
        return carry

    lax.fori_loop(0, 2, finish, 0)


def in_hbm(array):
    return pltpu.with_memory_space_constraint(array, pltpu.HBM)


def attend(page_map, selected, ids, gain, queries, keys, values):
    return pl.pallas_call(
        attend_kernel,
        out_shape=jax.ShapeDtypeStruct((256, 640), BF),
        in_specs=[HBM, HBM, SMEM, HBM, HBM, HBM, HBM],
        out_specs=VMEM,
        scratch_shapes=[
            pltpu.SMEM((64,), jnp.int32),
            pltpu.SMEM((2, 8), jnp.int32),
            pltpu.VMEM((1, 168), F32),
            pltpu.VMEM((256, 512), BF),
            pltpu.VMEM((2, 2048, 256), BF),
            pltpu.VMEM((2, 2048, 256), BF),
            pltpu.SemaphoreType.DMA((4,)),
            pltpu.SemaphoreType.DMA((2,)),
            pltpu.SemaphoreType.DMA((2,)),
            pltpu.SMEM((8,), jnp.int32),
            pltpu.VMEM((2, 512, 128), F32),
            pltpu.VMEM((2, 512, 128), F32),
            pltpu.VMEM((2, 512, 128), F32),
        ],
        compiler_params=pltpu.CompilerParams(vmem_limit_bytes=40 << 20),
        cost_estimate=pl.CostEstimate(
            flops=4 * 10**9, transcendentals=4 * 10**6, bytes_accessed=10 * 2**20
        ),
        name="attend",
    )(in_hbm(page_map), in_hbm(selected), ids, in_hbm(gain), in_hbm(queries), in_hbm(keys), in_hbm(values))


def merge_kernel(ids, x_ref, o_ref, gain_ref):
    x = x_ref[...].astype(F32)
    marks = x[:, :, 512:640].reshape(256, 128).astype(BF)
    source = lax.broadcasted_iota(jnp.int32, (128, 512), 0)
    target = lax.broadcasted_iota(jnp.int32, (128, 512), 1)
    spread = jnp.where((source < 12) & ((source & 3) == target // 128), 1.0, 0.0).astype(BF)
    level = jnp.dot(marks, spread, preferred_element_type=F32).reshape(32, 8, 512)
    top = jnp.max(level, axis=0, keepdims=True)
    weight = jnp.exp2(level - top)
    total = jnp.sum(weight, axis=0)
    mixed = jnp.sum(weight * x[:, :, :512], axis=0)
    share = (mixed / total).astype(BF)
    for k in range(NZ * NX):
        o_ref[k] = share
    for k in range(NX):
        gain = x_ref[ids[1] * NX + k, :, 512:640].astype(F32)
        for half in range(2):
            gain_ref[k : k + 1, half * 84 : half * 84 + 84] = (
                gain[half : half + 1, 16:100]
                + gain[half + 2 : half + 3, 16:100]
                + gain[half + 4 : half + 5, 16:100]
            )


def packed(rows):
    rest = rows[:, 128:168]
    return jnp.concatenate(
        [
            rows[:, :128],
            jnp.concatenate([rest[:16], rest[16:], jnp.zeros((16, 48), rows.dtype)], axis=1),
        ],
        axis=0,
    )


def project_kernel(a_ref, w_ref, o_ref):
    block = lax.dot_general(
        a_ref[...], w_ref[...], (((1,), (1,)), ((), ())), preferred_element_type=F32
    )
    for h in range(NZ):
        o_ref[h] = packed(block[h * 32 : (h + 1) * 32]).astype(BF)


def stream_kernel(x_ref, r_ref, o_ref):
    total = jnp.sum(x_ref[...].astype(F32), axis=0) + packed(r_ref[...].astype(F32))
    o_ref[...] = total.astype(BF)


def gate_up_kernel(ids, x_ref, gain_ref, g_ref, u_ref, o_ref, own_ref, stream, normed):
    for x in range(NX):
        block = x_ref[:, x, :, :].astype(F32)
        main = block[:, :32, :].reshape(256, 128)
        rest = jnp.concatenate([block[:, 32:48, 0:40], block[:, 32:48, 40:80]], axis=1)
        rest = rest.reshape(256, 40)
        first, second = slice(x * 168, x * 168 + 128), slice(x * 168 + 128, x * 168 + 168)
        stream[:, first] = main
        stream[:, second] = rest
        normed[:, first] = (main * gain_ref[x : x + 1, 0:128]).astype(BF)
        normed[:, second] = (rest * gain_ref[x : x + 1, 128:168]).astype(BF)
    own_ref[...] = stream[pl.ds(pl.multiple_of(ids[0] * 8, 8), 8), :].astype(BF)
    a = normed[...]
    s = stream[...]
    squares = jnp.sum(s * s, axis=1, keepdims=True)
    lane = lax.broadcasted_iota(jnp.int32, (256, 64), 1)
    marks = jnp.zeros((256, 64), F32)
    for n, piece in enumerate(pieces(squares)):
        marks = jnp.where(lane == n, piece, marks)
    gate = jnp.dot(a, g_ref[...], preferred_element_type=F32)
    o_ref[:, 0:640] = gate[:, :640].astype(BF)
    up = jnp.dot(a, u_ref[...], preferred_element_type=F32)
    o_ref[:, 640:1280] = up[:, :640].astype(BF)
    o_ref[:, 1280:] = jnp.concatenate([gate[:, 640:], up[:, 640:], marks], axis=1).astype(BF)


def hidden_kernel(x_ref, o_ref):
    both = jnp.sum(x_ref[...].astype(F32), axis=0)
    squares = both[:, 1344:1345] + both[:, 1345:1346] + both[:, 1346:1347]
    factor = lax.rsqrt(squares / D + EPSILON)
    gate = jnp.concatenate([both[:, :640], both[:, 1280:1312]], axis=1) * factor
    up = jnp.concatenate([both[:, 640:1280], both[:, 1312:1344]], axis=1) * factor
    hidden = (jax.nn.gelu(gate, approximate=True) * up).astype(BF)
    for k in range(NY * NC):
        o_ref[k] = hidden


def down_kernel(a_ref, w_ref, o_ref):
    o_ref[...] = jnp.dot(a_ref[...], w_ref[...], preferred_element_type=F32).astype(BF)


def final_kernel(x_ref, s_ref, o_ref):
    o_ref[...] = (jnp.sum(x_ref[...].astype(F32), axis=0) + s_ref[...].astype(F32)).astype(BF)


def call(kernel, outs, specs, *args, scratch=()):
    outs = [jax.ShapeDtypeStruct(shape, dtype) for shape, dtype in outs]
    results = pl.pallas_call(
        kernel,
        out_shape=outs,
        in_specs=specs,
        out_specs=[VMEM] * len(outs),
        scratch_shapes=scratch,
        compiler_params=pltpu.CompilerParams(vmem_limit_bytes=32 << 20),
        name=kernel.__name__,
    )(*args)
    return results if len(outs) > 1 else results[0]


def exchange(parts, axis):
    return lax.all_to_all(parts, axis, split_axis=0, concat_axis=0, tiled=True)


def place(z, x, h):
    return (z * NX + x) * NY * NC + h


def shards(
    queries, keys, values, page_map, selected, residual_in, out_weight, norm_gain, gate_weight, up_weight, down_weight
):
    ctx = (lax.axis_index("z") * NX + lax.axis_index("x")).astype(jnp.int32)
    head = (lax.axis_index("y") * NC + lax.axis_index("core")).astype(jnp.int32)
    ids = jnp.stack([ctx, head])
    sent = attend(page_map, selected, ids, norm_gain.reshape(1, 168), queries, keys, values)
    arrived = exchange(sent.reshape(32, 8, 640), CTX)
    shares, gain = call(
        merge_kernel, [((NZ * NX, 8, 512), BF), ((NX, 168), F32)], [SMEM, VMEM], ids, arrived
    )
    attention = exchange(shares, CTX).reshape(256, 512)
    partial = call(project_kernel, [((NZ, 48, 128), BF)], [VMEM, VMEM], attention, out_weight.T)
    projected = exchange(partial, HEADS)
    stream = call(stream_kernel, [((48, 128), BF)], [VMEM, VMEM], projected, residual_in)
    turned = lax.ppermute(
        stream,
        ALL,
        [(place(z, x, h), place(h, x, z)) for z in range(NZ) for x in range(NX) for h in range(NZ)],
    )
    rows = exchange(jnp.broadcast_to(turned, (NZ * NX, 48, 128)), CTX)
    parts, own_stream = call(
        gate_up_kernel,
        [((256, 1408), BF), ((8, 672), BF)],
        [SMEM, VMEM, VMEM, VMEM, VMEM],
        ids,
        rows.reshape(NZ, NX, 48, 128),
        gain,
        gate_weight,
        up_weight,
        scratch=[pltpu.VMEM((256, 672), F32), pltpu.VMEM((256, 672), BF)],
    )
    shared = exchange(parts.reshape(NY * NC, 32, 1408), HEADS)
    hidden = exchange(call(hidden_kernel, [((NY * NC, 32, 672), BF)], [VMEM], shared), HEADS)
    down = call(
        down_kernel, [((256, 672), BF)], [VMEM, VMEM], hidden.reshape(256, 672), down_weight
    )
    out_parts = exchange(down.reshape(32, 8, 672), CTX)
    return call(final_kernel, [((8, 672), BF)], [VMEM, VMEM], out_parts, own_stream)


def solution(mesh):
    fine = Mesh(mesh.devices.reshape(NZ, NX, NY, NC), ALL)
    in_specs = (
        P(None, HEADS),
        P(CTX, None, HEADS),
        P(CTX, None, HEADS),
        P(),
        P(),
        P(HEADS, CTX),
        P(HEADS, CTX),
        P(CTX),
        P(HEADS, CTX),
        P(HEADS, CTX),
        P(CTX, HEADS),
    )
    return jax.shard_map(shards, mesh=fine, in_specs=in_specs, out_specs=P(CTX, HEADS), check_vma=False)
```

```python
import functools
import math

import jax
import jax.numpy as jnp
from jax import lax
from jax.experimental import pallas as pl
from jax.experimental.pallas import tpu as pltpu
from jax.sharding import Mesh
from jax.sharding import PartitionSpec as P

D = 5376
HEAD = 128
LAST_PAGE = 63
BF = jnp.bfloat16
F32 = jnp.float32
NEG = -1e30
EXP2_SCALE = 168.0 ** (-0.5) * math.log2(math.e)
EPSILON = 1e-06
CTX = ("z", "x")
HEADS = ("y", "core")
ALL = ("z", "x", "y", "core")
NZ, NX, NY, NC = 8, 4, 4, 2

VMEM = pl.BlockSpec(memory_space=pltpu.VMEM)
SMEM = pl.BlockSpec(memory_space=pltpu.SMEM)
HBM = pl.BlockSpec(memory_space=pltpu.HBM)


def pieces(value):
    high = value.astype(BF).astype(F32)
    rest = value - high
    middle = rest.astype(BF).astype(F32)
    return high, middle, rest - middle


def attend_kernel(
    pm_hbm, sel_hbm, ids, gain_hbm, q_hbm, k_hbm, v_hbm, o_ref,
    pm, sel, gain_ref, q_ref, kbuf, vbuf, sems, ksem, vsem, flags, m_ref, l_ref, acc_ref,
):
    tables = (
        pltpu.make_async_copy(pm_hbm, pm, sems.at[0]),
        pltpu.make_async_copy(sel_hbm, sel, sems.at[1]),
    )
    late = (
        pltpu.make_async_copy(q_hbm, q_ref, sems.at[2]),
        pltpu.make_async_copy(gain_hbm, gain_ref, sems.at[3]),
    )

    def page_copies(p):
        return (
            pltpu.make_async_copy(k_hbm.at[p], kbuf.at[p], ksem.at[p]),
            pltpu.make_async_copy(v_hbm.at[p], vbuf.at[p], vsem.at[p]),
        )

    for c in tables + late + page_copies(0) + page_copies(1):
        c.start()
    m_ref[...] = jnp.full_like(m_ref, NEG)
    l_ref[...] = jnp.zeros_like(l_ref)
    acc_ref[...] = jnp.zeros_like(acc_ref)
    for n in range(6):
        flags[n] = jnp.int32(0)
    for c in tables:
        c.wait()

    def look(n, carry):
        logical = sel[n >> 3, n & 7]
        p = pm[logical] - ids[0] * 2

        @pl.when((p == 0) | (p == 1))
        def _():
            flags[p * 2 + (n >> 3)] = jnp.int32(1)

            @pl.when(logical == LAST_PAGE)
            def _():
                flags[4 + p] = jnp.int32(1)

        return carry

    lax.fori_loop(0, 16, look, 0)
    for c in late:
        c.wait()

    def attend_tile(p, t):
        span = pl.ds(pl.multiple_of(t * 256, 256), 256)
        rows = pl.ds(pl.multiple_of(t * 128, 128), 128)
        limit = jnp.where(flags[4 + p] != 0, t * 128, 1 << 20)
        row = lax.broadcasted_iota(jnp.int32, (256, 256), 0)
        col = lax.broadcasted_iota(jnp.int32, (256, 256), 1)
        visible = col <= (row & 127) + limit

        def scores(kv):
            q = jnp.concatenate(
                [q_ref[rows, (2 * kv + g) * 128 : (2 * kv + g + 1) * 128] for g in range(2)], axis=0
            )
            s = lax.dot_general(
                q,
                kbuf[p, :, kv * 128 : (kv + 1) * 128],
                (((1,), (1,)), ((), ())),
                preferred_element_type=F32,
            )
            return jnp.concatenate([s[:, :1792], jnp.where(visible, s[:, 1792:], NEG)], axis=1)

        for kv, s in enumerate([scores(0), scores(1)]):
            old = m_ref[kv, span, :]
            top = s[:, :128]
            for a in range(1, 16):
                top = jnp.maximum(top, s[:, a * 128 : (a + 1) * 128])
            new = jnp.maximum(old, jnp.max(top, axis=1, keepdims=True))
            keep = jnp.exp2((old - new) * EXP2_SCALE)
            w = jnp.exp2((s - jnp.concatenate([new] * 16, axis=1)) * EXP2_SCALE)
            part = w[:, :128]
            for a in range(1, 16):
                part = part + w[:, a * 128 : (a + 1) * 128]
            mixed = jnp.dot(
                w.astype(BF), vbuf[p, :, kv * 128 : (kv + 1) * 128], preferred_element_type=F32
            )
            m_ref[kv, span, :] = new
            l_ref[kv, span, :] = l_ref[kv, span, :] * keep + part
            acc_ref[kv, span, :] = acc_ref[kv, span, :] * keep + mixed

    def page(p, carry):
        for c in page_copies(p):
            c.wait()

        def tile(t, carry):
            @pl.when(flags[p * 2 + t] != 0)
            def _():
                attend_tile(p, t)

            return carry

        return lax.fori_loop(0, 2, tile, carry)

    lax.fori_loop(0, 2, page, 0)

    lane = lax.broadcasted_iota(jnp.int32, (128, 128), 1)
    halves = []
    for piece in pieces(gain_ref[...]):
        halves += [piece[:, :84], piece[:, 84:168]]
    halves += [jnp.zeros((1, 84), F32)] * 2
    gains = jnp.concatenate(
        [jnp.zeros((8, 16), F32), jnp.concatenate(halves, axis=0), jnp.zeros((8, 28), F32)], axis=1
    )
    gains = jnp.concatenate([gains] * 16, axis=0)

    def finish(t, carry):
        marks = gains
        out_rows = pl.ds(pl.multiple_of(t * 128, 128), 128)
        for h in range(4):
            kv = h // 2
            rows = pl.ds(pl.multiple_of(t * 256 + (h % 2) * 128, 128), 128)
            total = jnp.sum(l_ref[kv, rows, :], axis=1, keepdims=True)
            some = total > 0.0
            safe = jnp.where(some, total, 1.0)
            level = jnp.where(some, m_ref[kv, rows, :][:, :1] * EXP2_SCALE + jnp.log2(safe), NEG)
            o_ref[out_rows, h * 128 : (h + 1) * 128] = (acc_ref[kv, rows, :] * (1.0 / safe)).astype(BF)
            for n, piece in enumerate(pieces(level)):
                marks = jnp.where(lane == h + 4 * n, piece, marks)
        o_ref[out_rows, 512:640] = marks.astype(BF)
        return carry

    lax.fori_loop(0, 2, finish, 0)


def in_hbm(array):
    return pltpu.with_memory_space_constraint(array, pltpu.HBM)


def attend(page_map, selected, ids, gain, queries, keys, values):
    return pl.pallas_call(
        attend_kernel,
        out_shape=jax.ShapeDtypeStruct((256, 640), BF),
        in_specs=[HBM, HBM, SMEM, HBM, HBM, HBM, HBM],
        out_specs=VMEM,
        scratch_shapes=[
            pltpu.SMEM((64,), jnp.int32),
            pltpu.SMEM((2, 8), jnp.int32),
            pltpu.VMEM((1, 168), F32),
            pltpu.VMEM((256, 512), BF),
            pltpu.VMEM((2, 2048, 256), BF),
            pltpu.VMEM((2, 2048, 256), BF),
            pltpu.SemaphoreType.DMA((4,)),
            pltpu.SemaphoreType.DMA((2,)),
            pltpu.SemaphoreType.DMA((2,)),
            pltpu.SMEM((8,), jnp.int32),
            pltpu.VMEM((2, 512, 128), F32),
            pltpu.VMEM((2, 512, 128), F32),
            pltpu.VMEM((2, 512, 128), F32),
        ],
        compiler_params=pltpu.CompilerParams(vmem_limit_bytes=40 << 20),
        cost_estimate=pl.CostEstimate(
            flops=4 * 10**9, transcendentals=4 * 10**6, bytes_accessed=10 * 2**20
        ),
        name="attend",
    )(in_hbm(page_map), in_hbm(selected), ids, in_hbm(gain), in_hbm(queries), in_hbm(keys), in_hbm(values))


def merge_kernel(ids, x_ref, o_ref, gain_ref):
    x = x_ref[...].astype(F32)
    marks = x[:, :, 512:640].reshape(256, 128).astype(BF)
    source = lax.broadcasted_iota(jnp.int32, (128, 512), 0)
    target = lax.broadcasted_iota(jnp.int32, (128, 512), 1)
    spread = jnp.where((source < 12) & ((source & 3) == target // 128), 1.0, 0.0).astype(BF)
    level = jnp.dot(marks, spread, preferred_element_type=F32).reshape(32, 8, 512)
    top = jnp.max(level, axis=0, keepdims=True)
    weight = jnp.exp2(level - top)
    total = jnp.sum(weight, axis=0)
    mixed = jnp.sum(weight * x[:, :, :512], axis=0)
    share = (mixed / total).astype(BF)
    for k in range(NZ * NX):
        o_ref[k] = share
    for k in range(NX):
        gain = x_ref[ids[1] * NX + k, :, 512:640].astype(F32)
        for half in range(2):
            gain_ref[k : k + 1, half * 84 : half * 84 + 84] = (
                gain[half : half + 1, 16:100]
                + gain[half + 2 : half + 3, 16:100]
                + gain[half + 4 : half + 5, 16:100]
            )


def packed(rows):
    rest = rows[:, 128:168]
    return jnp.concatenate(
        [
            rows[:, :128],
            jnp.concatenate([rest[:16], rest[16:], jnp.zeros((16, 48), rows.dtype)], axis=1),
        ],
        axis=0,
    )


def project_kernel(a_ref, w_ref, o_ref):
    block = lax.dot_general(
        a_ref[...], w_ref[...], (((1,), (1,)), ((), ())), preferred_element_type=F32
    )
    for h in range(NZ):
        o_ref[h] = packed(block[h * 32 : (h + 1) * 32]).astype(BF)


def stream_kernel(x_ref, r_ref, o_ref):
    total = jnp.sum(x_ref[...].astype(F32), axis=0) + packed(r_ref[...].astype(F32))
    o_ref[...] = total.astype(BF)


def gate_up(a, squares, g_ref, u_ref):
    lane = lax.broadcasted_iota(jnp.int32, (128, 64), 1)
    marks = jnp.zeros((128, 64), F32)
    for n, piece in enumerate(pieces(squares)):
        marks = jnp.where(lane == n, piece, marks)
    gate = jnp.dot(a, g_ref[...], preferred_element_type=F32)
    up = jnp.dot(a, u_ref[...], preferred_element_type=F32)
    tail = jnp.concatenate([gate[:, 640:], up[:, 640:], marks], axis=1)
    return gate[:, :640].astype(BF), up[:, :640].astype(BF), tail.astype(BF)


def other_half_kernel(
    ids, x_ref, gain_ref, g_ref, u_ref, o_ref, normed_ref, squares_ref, own_ref, stream, normed
):
    for x in range(NX):
        block = x_ref[:, x, :, :].astype(F32)
        main = block[:, :32, :].reshape(256, 128)
        rest = jnp.concatenate([block[:, 32:48, 0:40], block[:, 32:48, 40:80]], axis=1)
        rest = rest.reshape(256, 40)
        first, second = slice(x * 168, x * 168 + 128), slice(x * 168 + 128, x * 168 + 168)
        stream[:, first] = main
        stream[:, second] = rest
        normed[:, first] = (main * gain_ref[x : x + 1, 0:128]).astype(BF)
        normed[:, second] = (rest * gain_ref[x : x + 1, 128:168]).astype(BF)
    theirs = pl.ds(pl.multiple_of((1 - ids[2]) * 128, 128), 128)
    mine = pl.ds(pl.multiple_of(ids[2] * 128, 128), 128)
    s = stream[theirs, :]
    o_ref[:, :640], o_ref[:, 640:1280], o_ref[:, 1280:] = gate_up(
        normed[theirs, :], jnp.sum(s * s, axis=1, keepdims=True), g_ref, u_ref
    )
    normed_ref[...] = normed[mine, :]
    s = stream[mine, :]
    squares_ref[...] = jnp.broadcast_to(jnp.sum(s * s, axis=1, keepdims=True), (128, 128))
    own_ref[...] = stream[pl.ds(pl.multiple_of(ids[0] * 8, 8), 8), :].astype(BF)


def own_half_kernel(a_ref, squares_ref, g_ref, u_ref, o_ref):
    o_ref[:, :640], o_ref[:, 640:1280], o_ref[:, 1280:] = gate_up(
        a_ref[...], squares_ref[:, :1], g_ref, u_ref
    )


def pair_kernel(a_ref, b_ref, o_ref):
    both = a_ref[...].astype(F32) + b_ref[...].astype(F32)
    o_ref[:, :1280] = both[:, :1280].astype(BF)
    tail = both[:, 1280:]
    lane = lax.broadcasted_iota(jnp.int32, (128, 128), 1)
    for n, piece in enumerate(pieces(tail[:, 64:65] + tail[:, 65:66] + tail[:, 66:67])):
        tail = jnp.where(lane == 64 + n, piece, tail)
    o_ref[:, 1280:] = tail.astype(BF)


def hidden_kernel(x_ref, o_ref):
    both = jnp.sum(x_ref[...].astype(F32), axis=0)
    squares = both[:, 1344:1345] + both[:, 1345:1346] + both[:, 1346:1347]
    factor = lax.rsqrt(squares / D + EPSILON)
    gate = jnp.concatenate([both[:, :640], both[:, 1280:1312]], axis=1) * factor
    up = jnp.concatenate([both[:, 640:1280], both[:, 1312:1344]], axis=1) * factor
    hidden = (jax.nn.gelu(gate, approximate=True) * up).astype(BF)
    for k in range(NY * NC):
        o_ref[k] = hidden


def down_kernel(a_ref, w_ref, o_ref):
    a = jnp.concatenate([a_ref[y * NC + c] for c in range(NC) for y in range(NY)], axis=0)
    o_ref[...] = jnp.dot(a, w_ref[...], preferred_element_type=F32).astype(BF)


def final_kernel(x_ref, s_ref, o_ref):
    o_ref[...] = (jnp.sum(x_ref[...].astype(F32), axis=0) + s_ref[...].astype(F32)).astype(BF)


def call(kernel, outs, specs, *args, scratch=()):
    outs = [jax.ShapeDtypeStruct(shape, dtype) for shape, dtype in outs]
    results = pl.pallas_call(
        kernel,
        out_shape=outs,
        in_specs=specs,
        out_specs=[VMEM] * len(outs),
        scratch_shapes=scratch,
        compiler_params=pltpu.CompilerParams(vmem_limit_bytes=32 << 20),
        name=kernel.__name__,
    )(*args)
    return results if len(outs) > 1 else results[0]


def exchange(parts, axis):
    return lax.all_to_all(parts, axis, split_axis=0, concat_axis=0, tiled=True)


def place(z, x, h):
    return (z * NX + x) * NY * NC + h


def shards(
    queries, keys, values, page_map, selected, residual_in, out_weight, norm_gain, gate_weight, up_weight, down_weight
):
    ctx = (lax.axis_index("z") * NX + lax.axis_index("x")).astype(jnp.int32)
    core = lax.axis_index("core").astype(jnp.int32)
    head = lax.axis_index("y").astype(jnp.int32) * NC + core
    ids = jnp.stack([ctx, head, core])
    sent = attend(page_map, selected, ids, norm_gain.reshape(1, 168), queries, keys, values)
    arrived = exchange(sent.reshape(32, 8, 640), CTX)
    shares, gain = call(
        merge_kernel, [((NZ * NX, 8, 512), BF), ((NX, 168), F32)], [SMEM, VMEM], ids, arrived
    )
    attention = exchange(shares, CTX).reshape(256, 512)
    partial = call(project_kernel, [((NZ, 48, 128), BF)], [VMEM, VMEM], attention, out_weight.T)
    projected = exchange(partial, HEADS)
    stream = call(stream_kernel, [((48, 128), BF)], [VMEM, VMEM], projected, residual_in)
    turned = lax.ppermute(
        stream,
        ALL,
        [(place(z, x, h), place(h, x, z)) for z in range(NZ) for x in range(NX) for h in range(NZ)],
    )
    rows = exchange(jnp.broadcast_to(turned, (NZ * NX, 48, 128)), CTX)
    half = ((128, 1408), BF)
    other, normed, squares, own_stream = call(
        other_half_kernel,
        [half, ((128, 672), BF), ((128, 128), F32), ((8, 672), BF)],
        [SMEM, VMEM, VMEM, VMEM, VMEM],
        ids,
        rows.reshape(NZ, NX, 48, 128),
        gain,
        gate_weight,
        up_weight,
        scratch=[pltpu.VMEM((256, 672), F32), pltpu.VMEM((256, 672), BF)],
    )
    received = lax.ppermute(other, "core", [(0, 1), (1, 0)])
    mine = call(own_half_kernel, [half], [VMEM] * 4, normed, squares, gate_weight, up_weight)
    pair = call(pair_kernel, [half], [VMEM, VMEM], mine, received)
    shared = exchange(pair.reshape(NY, 32, 1408), "y")
    hidden = exchange(call(hidden_kernel, [((NY * NC, 32, 672), BF)], [VMEM], shared), HEADS)
    down = call(
        down_kernel, [((256, 672), BF)], [VMEM, VMEM], hidden, down_weight
    )
    out_parts = exchange(down.reshape(32, 8, 672), CTX)
    return call(final_kernel, [((8, 672), BF)], [VMEM, VMEM], out_parts, own_stream)


def solution(mesh):
    fine = Mesh(mesh.devices.reshape(NZ, NX, NY, NC), ALL)
    in_specs = (
        P(None, HEADS),
        P(CTX, None, HEADS),
        P(CTX, None, HEADS),
        P(),
        P(),
        P(HEADS, CTX),
        P(HEADS, CTX),
        P(CTX),
        P(HEADS, CTX),
        P(HEADS, CTX),
        P(CTX, HEADS),
    )
    return jax.shard_map(shards, mesh=fine, in_specs=in_specs, out_specs=P(CTX, HEADS), check_vma=False)
```

```python
import functools
import math

import jax
import jax.numpy as jnp
from jax import lax
from jax.experimental import pallas as pl
from jax.experimental.pallas import tpu as pltpu
from jax.sharding import Mesh
from jax.sharding import PartitionSpec as P

D = 5376
HEAD = 128
LAST_PAGE = 63
BF = jnp.bfloat16
F32 = jnp.float32
NEG = -1e30
EXP2_SCALE = 168.0 ** (-0.5) * math.log2(math.e)
EPSILON = 1e-06
CTX = ("z", "x")
HEADS = ("y", "core")
ALL = ("z", "x", "y", "core")
NZ, NX, NY, NC = 8, 4, 4, 2

VMEM = pl.BlockSpec(memory_space=pltpu.VMEM)
SMEM = pl.BlockSpec(memory_space=pltpu.SMEM)
HBM = pl.BlockSpec(memory_space=pltpu.HBM)


def pieces(value):
    high = value.astype(BF).astype(F32)
    rest = value - high
    middle = rest.astype(BF).astype(F32)
    return high, middle, rest - middle


def attend_kernel(
    pm_hbm, sel_hbm, ids, gain_hbm, q_hbm, k_hbm, v_hbm, o_ref,
    pm, sel, gain_ref, q_ref, kbuf, vbuf, sems, ksem, vsem, flags, m_ref, l_ref, acc_ref,
):
    tables = (
        pltpu.make_async_copy(pm_hbm, pm, sems.at[0]),
        pltpu.make_async_copy(sel_hbm, sel, sems.at[1]),
    )
    late = (
        pltpu.make_async_copy(q_hbm, q_ref, sems.at[2]),
        pltpu.make_async_copy(gain_hbm, gain_ref, sems.at[3]),
    )

    def page_copies(p):
        return (
            pltpu.make_async_copy(k_hbm.at[p], kbuf.at[p], ksem.at[p]),
            pltpu.make_async_copy(v_hbm.at[p], vbuf.at[p], vsem.at[p]),
        )

    for c in tables + late + page_copies(0) + page_copies(1):
        c.start()
    m_ref[...] = jnp.full_like(m_ref, NEG)
    l_ref[...] = jnp.zeros_like(l_ref)
    acc_ref[...] = jnp.zeros_like(acc_ref)
    for n in range(6):
        flags[n] = jnp.int32(0)
    for c in tables:
        c.wait()

    def look(n, carry):
        logical = sel[n >> 3, n & 7]
        p = pm[logical] - ids[0] * 2

        @pl.when((p == 0) | (p == 1))
        def _():
            flags[p * 2 + (n >> 3)] = jnp.int32(1)

            @pl.when(logical == LAST_PAGE)
            def _():
                flags[4 + p] = jnp.int32(1)

        return carry

    lax.fori_loop(0, 16, look, 0)
    for c in late:
        c.wait()

    def attend_tile(p, t):
        span = pl.ds(pl.multiple_of(t * 256, 256), 256)
        rows = pl.ds(pl.multiple_of(t * 128, 128), 128)
        limit = jnp.where(flags[4 + p] != 0, t * 128, 1 << 20)
        row = lax.broadcasted_iota(jnp.int32, (256, 256), 0)
        col = lax.broadcasted_iota(jnp.int32, (256, 256), 1)
        visible = col <= (row & 127) + limit

        def scores(kv):
            q = jnp.concatenate(
                [q_ref[rows, (2 * kv + g) * 128 : (2 * kv + g + 1) * 128] for g in range(2)], axis=0
            )
            s = lax.dot_general(
                q,
                kbuf[p, :, kv * 128 : (kv + 1) * 128],
                (((1,), (1,)), ((), ())),
                preferred_element_type=F32,
            )
            return jnp.concatenate([s[:, :1792], jnp.where(visible, s[:, 1792:], NEG)], axis=1)

        for kv, s in enumerate([scores(0), scores(1)]):
            old = m_ref[kv, span, :]
            top = s[:, :128]
            for a in range(1, 16):
                top = jnp.maximum(top, s[:, a * 128 : (a + 1) * 128])
            new = jnp.maximum(old, jnp.max(top, axis=1, keepdims=True))
            keep = jnp.exp2((old - new) * EXP2_SCALE)
            w = jnp.exp2((s - jnp.concatenate([new] * 16, axis=1)) * EXP2_SCALE)
            part = w[:, :128]
            for a in range(1, 16):
                part = part + w[:, a * 128 : (a + 1) * 128]
            mixed = jnp.dot(
                w.astype(BF), vbuf[p, :, kv * 128 : (kv + 1) * 128], preferred_element_type=F32
            )
            m_ref[kv, span, :] = new
            l_ref[kv, span, :] = l_ref[kv, span, :] * keep + part
            acc_ref[kv, span, :] = acc_ref[kv, span, :] * keep + mixed

    def page(p, carry):
        for c in page_copies(p):
            c.wait()

        def tile(t, carry):
            @pl.when(flags[p * 2 + t] != 0)
            def _():
                attend_tile(p, t)

            return carry

        return lax.fori_loop(0, 2, tile, carry)

    lax.fori_loop(0, 2, page, 0)

    lane = lax.broadcasted_iota(jnp.int32, (128, 128), 1)
    halves = []
    for piece in pieces(gain_ref[...]):
        halves += [piece[:, :84], piece[:, 84:168]]
    halves += [jnp.zeros((1, 84), F32)] * 2
    gains = jnp.concatenate(
        [jnp.zeros((8, 16), F32), jnp.concatenate(halves, axis=0), jnp.zeros((8, 28), F32)], axis=1
    )
    gains = jnp.concatenate([gains] * 16, axis=0)

    def finish(t, carry):
        marks = gains
        out_rows = pl.ds(pl.multiple_of(t * 128, 128), 128)
        for h in range(4):
            kv = h // 2
            rows = pl.ds(pl.multiple_of(t * 256 + (h % 2) * 128, 128), 128)
            total = jnp.sum(l_ref[kv, rows, :], axis=1, keepdims=True)
            some = total > 0.0
            safe = jnp.where(some, total, 1.0)
            level = jnp.where(some, m_ref[kv, rows, :][:, :1] * EXP2_SCALE + jnp.log2(safe), NEG)
            o_ref[out_rows, h * 128 : (h + 1) * 128] = (acc_ref[kv, rows, :] * (1.0 / safe)).astype(BF)
            for n, piece in enumerate(pieces(level)):
                marks = jnp.where(lane == h + 4 * n, piece, marks)
        o_ref[out_rows, 512:640] = marks.astype(BF)
        return carry

    lax.fori_loop(0, 2, finish, 0)


def in_hbm(array):
    return pltpu.with_memory_space_constraint(array, pltpu.HBM)


def attend(page_map, selected, ids, gain, queries, keys, values):
    return pl.pallas_call(
        attend_kernel,
        out_shape=jax.ShapeDtypeStruct((256, 640), BF),
        in_specs=[HBM, HBM, SMEM, HBM, HBM, HBM, HBM],
        out_specs=VMEM,
        scratch_shapes=[
            pltpu.SMEM((64,), jnp.int32),
            pltpu.SMEM((2, 8), jnp.int32),
            pltpu.VMEM((1, 168), F32),
            pltpu.VMEM((256, 512), BF),
            pltpu.VMEM((2, 2048, 256), BF),
            pltpu.VMEM((2, 2048, 256), BF),
            pltpu.SemaphoreType.DMA((4,)),
            pltpu.SemaphoreType.DMA((2,)),
            pltpu.SemaphoreType.DMA((2,)),
            pltpu.SMEM((8,), jnp.int32),
            pltpu.VMEM((2, 512, 128), F32),
            pltpu.VMEM((2, 512, 128), F32),
            pltpu.VMEM((2, 512, 128), F32),
        ],
        compiler_params=pltpu.CompilerParams(vmem_limit_bytes=40 << 20),
        cost_estimate=pl.CostEstimate(
            flops=4 * 10**9, transcendentals=4 * 10**6, bytes_accessed=10 * 2**20
        ),
        name="attend",
    )(in_hbm(page_map), in_hbm(selected), ids, in_hbm(gain), in_hbm(queries), in_hbm(keys), in_hbm(values))


def merge_kernel(ids, x_ref, o_ref, gain_ref):
    x = x_ref[...].astype(F32)
    marks = x[:, :, 512:640].reshape(256, 128).astype(BF)
    source = lax.broadcasted_iota(jnp.int32, (128, 512), 0)
    target = lax.broadcasted_iota(jnp.int32, (128, 512), 1)
    spread = jnp.where((source < 12) & ((source & 3) == target // 128), 1.0, 0.0).astype(BF)
    level = jnp.dot(marks, spread, preferred_element_type=F32).reshape(32, 8, 512)
    top = jnp.max(level, axis=0, keepdims=True)
    weight = jnp.exp2(level - top)
    total = jnp.sum(weight, axis=0)
    mixed = jnp.sum(weight * x[:, :, :512], axis=0)
    share = (mixed / total).astype(BF)
    o_ref[...] = share
    for k in range(NX):
        gain = x_ref[ids[1] * NX + k, :, 512:640].astype(F32)
        for half in range(2):
            gain_ref[k : k + 1, half * 84 : half * 84 + 84] = (
                gain[half : half + 1, 16:100]
                + gain[half + 2 : half + 3, 16:100]
                + gain[half + 4 : half + 5, 16:100]
            )


def packed(rows):
    rest = rows[:, 128:168]
    return jnp.concatenate(
        [
            rows[:, :128],
            jnp.concatenate([rest[:16], rest[16:], jnp.zeros((16, 48), rows.dtype)], axis=1),
        ],
        axis=0,
    )


def project_kernel(a_ref, w_ref, o_ref):
    block = lax.dot_general(
        a_ref[...], w_ref[...], (((1,), (1,)), ((), ())), preferred_element_type=F32
    )
    for h in range(NZ):
        o_ref[h] = packed(block[h * 32 : (h + 1) * 32]).astype(BF)


def stream_kernel(x_ref, r_ref, o_ref):
    total = jnp.sum(x_ref[...].astype(F32), axis=0) + packed(r_ref[...].astype(F32))
    o_ref[...] = total.astype(BF)


def gate_up(a, squares, g_ref, u_ref):
    lane = lax.broadcasted_iota(jnp.int32, (128, 64), 1)
    marks = jnp.zeros((128, 64), F32)
    for n, piece in enumerate(pieces(jnp.sum(squares, axis=1, keepdims=True))):
        marks = jnp.where(lane == n, piece, marks)
    gate = jnp.dot(a, g_ref[...], preferred_element_type=F32)
    up = jnp.dot(a, u_ref[...], preferred_element_type=F32)
    tail = jnp.concatenate([gate[:, 640:], up[:, 640:], marks], axis=1)
    return gate[:, :640].astype(BF), up[:, :640].astype(BF), tail.astype(BF)


def unpacked(block):
    rest = jnp.concatenate([block[..., 32:48, 0:40], block[..., 32:48, 40:80]], axis=-2)
    return block[..., :32, :], rest


def other_half_kernel(
    ids, x_ref, gain_ref, g_ref, u_ref, o_ref, normed_ref, squares_ref, own_ref, own, squares, normed
):
    full = jnp.zeros((256, 128), F32)
    part = jnp.zeros((256, 40), F32)
    for x in range(NX):
        main, rest = unpacked(x_ref[:, x, :, :].astype(F32))
        main, rest = main.reshape(256, 128), rest.reshape(256, 40)
        first, second = slice(x * 168, x * 168 + 128), slice(x * 168 + 128, x * 168 + 168)
        full = full + main * main
        part = part + rest * rest
        normed[:, first] = (main * gain_ref[x : x + 1, 0:128]).astype(BF)
        normed[:, second] = (rest * gain_ref[x : x + 1, 128:168]).astype(BF)
        own[:, first], own[:, second] = unpacked(x_ref[ids[0] >> 2, x, :, :].astype(F32))
    squares[...] = full + jnp.concatenate([part, jnp.zeros((256, 88), F32)], axis=1)
    theirs = pl.ds(pl.multiple_of((1 - ids[2]) * 128, 128), 128)
    mine = pl.ds(pl.multiple_of(ids[2] * 128, 128), 128)
    o_ref[:, :640], o_ref[:, 640:1280], o_ref[:, 1280:] = gate_up(
        normed[theirs, :], squares[theirs, :], g_ref, u_ref
    )
    normed_ref[...] = normed[mine, :]
    squares_ref[...] = squares[mine, :]
    own_ref[...] = own[pl.ds(pl.multiple_of((ids[0] & 3) * 8, 8), 8), :].astype(BF)


def own_half_kernel(a_ref, squares_ref, g_ref, u_ref, o_ref):
    o_ref[:, :640], o_ref[:, 640:1280], o_ref[:, 1280:] = gate_up(
        a_ref[...], squares_ref[...], g_ref, u_ref
    )


def pair_kernel(a_ref, b_ref, o_ref):
    both = a_ref[...].astype(F32) + b_ref[...].astype(F32)
    o_ref[:, :1280] = both[:, :1280].astype(BF)
    tail = both[:, 1280:]
    lane = lax.broadcasted_iota(jnp.int32, (128, 128), 1)
    for n, piece in enumerate(pieces(tail[:, 64:65] + tail[:, 65:66] + tail[:, 66:67])):
        tail = jnp.where(lane == 64 + n, piece, tail)
    o_ref[:, 1280:] = tail.astype(BF)


def hidden_kernel(x_ref, o_ref):
    both = jnp.sum(x_ref[...].astype(F32), axis=0)
    squares = both[:, 1344:1345] + both[:, 1345:1346] + both[:, 1346:1347]
    factor = lax.rsqrt(squares / D + EPSILON)
    gate = jnp.concatenate([both[:, :640], both[:, 1280:1312]], axis=1) * factor
    up = jnp.concatenate([both[:, 640:1280], both[:, 1312:1344]], axis=1) * factor
    hidden = (jax.nn.gelu(gate, approximate=True) * up).astype(BF)
    for k in range(NY * NC):
        o_ref[k] = hidden


def down_kernel(a_ref, w_ref, o_ref):
    a = jnp.concatenate([a_ref[y * NC + c] for c in range(NC) for y in range(NY)], axis=0)
    o_ref[...] = jnp.dot(a, w_ref[...], preferred_element_type=F32).astype(BF)


def final_kernel(x_ref, s_ref, o_ref):
    o_ref[...] = (jnp.sum(x_ref[...].astype(F32), axis=0) + s_ref[...].astype(F32)).astype(BF)


def call(kernel, outs, specs, *args, scratch=()):
    outs = [jax.ShapeDtypeStruct(shape, dtype) for shape, dtype in outs]
    results = pl.pallas_call(
        kernel,
        out_shape=outs,
        in_specs=specs,
        out_specs=[VMEM] * len(outs),
        scratch_shapes=scratch,
        compiler_params=pltpu.CompilerParams(vmem_limit_bytes=32 << 20),
        name=kernel.__name__,
    )(*args)
    return results if len(outs) > 1 else results[0]


def exchange(parts, axis):
    return lax.all_to_all(parts, axis, split_axis=0, concat_axis=0, tiled=True)


def place(z, x, h):
    return (z * NX + x) * NY * NC + h


def shards(
    queries, keys, values, page_map, selected, residual_in, out_weight, norm_gain, gate_weight, up_weight, down_weight
):
    ctx = (lax.axis_index("z") * NX + lax.axis_index("x")).astype(jnp.int32)
    core = lax.axis_index("core").astype(jnp.int32)
    head = lax.axis_index("y").astype(jnp.int32) * NC + core
    ids = jnp.stack([ctx, head, core])
    sent = attend(page_map, selected, ids, norm_gain.reshape(1, 168), queries, keys, values)
    arrived = exchange(sent.reshape(32, 8, 640), CTX)
    share, gain = call(
        merge_kernel, [((8, 512), BF), ((NX, 168), F32)], [SMEM, VMEM], ids, arrived
    )
    attention = exchange(jnp.broadcast_to(share, (NZ * NX, 8, 512)), CTX).reshape(256, 512)
    partial = call(project_kernel, [((NZ, 48, 128), BF)], [VMEM, VMEM], attention, out_weight.T)
    projected = exchange(partial, HEADS)
    stream = call(stream_kernel, [((48, 128), BF)], [VMEM, VMEM], projected, residual_in)
    turned = lax.ppermute(
        stream,
        ALL,
        [(place(z, x, h), place(h, x, z)) for z in range(NZ) for x in range(NX) for h in range(NZ)],
    )
    rows = exchange(jnp.broadcast_to(turned, (NZ * NX, 48, 128)), CTX)
    half = ((128, 1408), BF)
    other, normed, squares, own_stream = call(
        other_half_kernel,
        [half, ((128, 672), BF), ((128, 128), F32), ((8, 672), BF)],
        [SMEM, VMEM, VMEM, VMEM, VMEM],
        ids,
        rows.reshape(NZ, NX, 48, 128),
        gain,
        gate_weight,
        up_weight,
        scratch=[pltpu.VMEM((32, 672), F32), pltpu.VMEM((256, 128), F32), pltpu.VMEM((256, 672), BF)],
    )
    received = lax.ppermute(other, "core", [(0, 1), (1, 0)])
    mine = call(own_half_kernel, [half], [VMEM] * 4, normed, squares, gate_weight, up_weight)
    pair = call(pair_kernel, [half], [VMEM, VMEM], mine, received)
    shared = exchange(pair.reshape(NY, 32, 1408), "y")
    hidden = exchange(call(hidden_kernel, [((NY * NC, 32, 672), BF)], [VMEM], shared), HEADS)
    down = call(
        down_kernel, [((256, 672), BF)], [VMEM, VMEM], hidden, down_weight
    )
    out_parts = exchange(down.reshape(32, 8, 672), CTX)
    return call(final_kernel, [((8, 672), BF)], [VMEM, VMEM], out_parts, own_stream)


def solution(mesh):
    fine = Mesh(mesh.devices.reshape(NZ, NX, NY, NC), ALL)
    in_specs = (
        P(None, HEADS),
        P(CTX, None, HEADS),
        P(CTX, None, HEADS),
        P(),
        P(),
        P(HEADS, CTX),
        P(HEADS, CTX),
        P(CTX),
        P(HEADS, CTX),
        P(HEADS, CTX),
        P(CTX, HEADS),
    )
    return jax.shard_map(shards, mesh=fine, in_specs=in_specs, out_specs=P(CTX, HEADS), check_vma=False)
```

```python
import functools
import math

import jax
import jax.numpy as jnp
from jax import lax
from jax.experimental import pallas as pl
from jax.experimental.pallas import tpu as pltpu
from jax.sharding import Mesh
from jax.sharding import PartitionSpec as P

D = 5376
HEAD = 128
LAST_PAGE = 63
BF = jnp.bfloat16
F32 = jnp.float32
NEG = -1e30
EXP2_SCALE = 168.0 ** (-0.5) * math.log2(math.e)
EPSILON = 1e-06
CTX = ("z", "x")
HEADS = ("y", "core")
ALL = ("z", "x", "y", "core")
NZ, NX, NY, NC = 8, 4, 4, 2

VMEM = pl.BlockSpec(memory_space=pltpu.VMEM)
HBM = pl.BlockSpec(memory_space=pltpu.HBM)


def pieces(value):
    high = value.astype(BF).astype(F32)
    rest = value - high
    middle = rest.astype(BF).astype(F32)
    return high, middle, rest - middle


def attend_kernel(
    pm_hbm, sel_hbm, gain_hbm, q_hbm, k_hbm, v_hbm, o_ref,
    pm, sel, gain_ref, q_ref, kbuf, vbuf, sems, ksem, vsem, flags, m_ref, l_ref, acc_ref,
):
    tables = (
        pltpu.make_async_copy(pm_hbm, pm, sems.at[0]),
        pltpu.make_async_copy(sel_hbm, sel, sems.at[1]),
    )
    late = (
        pltpu.make_async_copy(q_hbm, q_ref, sems.at[2]),
        pltpu.make_async_copy(gain_hbm, gain_ref, sems.at[3]),
    )

    def page_copies(p):
        return (
            pltpu.make_async_copy(k_hbm.at[p], kbuf.at[p], ksem.at[p]),
            pltpu.make_async_copy(v_hbm.at[p], vbuf.at[p], vsem.at[p]),
        )

    for c in tables + late + page_copies(0) + page_copies(1):
        c.start()
    m_ref[...] = jnp.full_like(m_ref, NEG)
    l_ref[...] = jnp.zeros_like(l_ref)
    acc_ref[...] = jnp.zeros_like(acc_ref)
    for n in range(6):
        flags[n] = jnp.int32(0)
    for c in tables:
        c.wait()

    first_slot = (lax.axis_index("z") * NX + lax.axis_index("x")) * 2

    def look(n, carry):
        logical = sel[n >> 3, n & 7]
        p = pm[logical] - first_slot

        @pl.when((p == 0) | (p == 1))
        def _():
            flags[p * 2 + (n >> 3)] = jnp.int32(1)

            @pl.when(logical == LAST_PAGE)
            def _():
                flags[4 + p] = jnp.int32(1)

        return carry

    lax.fori_loop(0, 16, look, 0)
    for c in late:
        c.wait()

    def attend_tile(p, t):
        span = pl.ds(pl.multiple_of(t * 256, 256), 256)
        rows = pl.ds(pl.multiple_of(t * 128, 128), 128)
        limit = jnp.where(flags[4 + p] != 0, t * 128, 1 << 20)
        row = lax.broadcasted_iota(jnp.int32, (256, 256), 0)
        col = lax.broadcasted_iota(jnp.int32, (256, 256), 1)
        visible = col <= (row & 127) + limit

        def scores(kv):
            q = jnp.concatenate(
                [q_ref[rows, (2 * kv + g) * 128 : (2 * kv + g + 1) * 128] for g in range(2)], axis=0
            )
            s = lax.dot_general(
                q,
                kbuf[p, :, kv * 128 : (kv + 1) * 128],
                (((1,), (1,)), ((), ())),
                preferred_element_type=F32,
            )
            return jnp.concatenate([s[:, :1792], jnp.where(visible, s[:, 1792:], NEG)], axis=1)

        for kv, s in enumerate([scores(0), scores(1)]):
            old = m_ref[kv, span, :]
            top = s[:, :128]
            for a in range(1, 16):
                top = jnp.maximum(top, s[:, a * 128 : (a + 1) * 128])
            new = jnp.maximum(old, jnp.max(top, axis=1, keepdims=True))
            keep = jnp.exp2((old - new) * EXP2_SCALE)
            w = jnp.exp2((s - jnp.concatenate([new] * 16, axis=1)) * EXP2_SCALE)
            part = w[:, :128]
            for a in range(1, 16):
                part = part + w[:, a * 128 : (a + 1) * 128]
            mixed = jnp.dot(
                w.astype(BF), vbuf[p, :, kv * 128 : (kv + 1) * 128], preferred_element_type=F32
            )
            m_ref[kv, span, :] = new
            l_ref[kv, span, :] = l_ref[kv, span, :] * keep + part
            acc_ref[kv, span, :] = acc_ref[kv, span, :] * keep + mixed

    def page(p, carry):
        for c in page_copies(p):
            c.wait()

        def tile(t, carry):
            @pl.when(flags[p * 2 + t] != 0)
            def _():
                attend_tile(p, t)

            return carry

        return lax.fori_loop(0, 2, tile, carry)

    lax.fori_loop(0, 2, page, 0)

    lane = lax.broadcasted_iota(jnp.int32, (128, 128), 1)
    halves = []
    for piece in pieces(gain_ref[...]):
        halves += [piece[:, :84], piece[:, 84:168]]
    halves += [jnp.zeros((1, 84), F32)] * 2
    gains = jnp.concatenate(
        [jnp.zeros((8, 16), F32), jnp.concatenate(halves, axis=0), jnp.zeros((8, 28), F32)], axis=1
    )
    gains = jnp.concatenate([gains] * 16, axis=0)

    def finish(t, carry):
        marks = gains
        out_rows = pl.ds(pl.multiple_of(t * 128, 128), 128)
        for h in range(4):
            kv = h // 2
            rows = pl.ds(pl.multiple_of(t * 256 + (h % 2) * 128, 128), 128)
            total = jnp.sum(l_ref[kv, rows, :], axis=1, keepdims=True)
            some = total > 0.0
            safe = jnp.where(some, total, 1.0)
            level = jnp.where(some, m_ref[kv, rows, :][:, :1] * EXP2_SCALE + jnp.log2(safe), NEG)
            o_ref[out_rows, h * 128 : (h + 1) * 128] = (acc_ref[kv, rows, :] * (1.0 / safe)).astype(BF)
            for n, piece in enumerate(pieces(level)):
                marks = jnp.where(lane == h + 4 * n, piece, marks)
        o_ref[out_rows, 512:640] = marks.astype(BF)
        return carry

    lax.fori_loop(0, 2, finish, 0)


def in_hbm(array):
    return pltpu.with_memory_space_constraint(array, pltpu.HBM)


def attend(page_map, selected, gain, queries, keys, values):
    return pl.pallas_call(
        attend_kernel,
        out_shape=jax.ShapeDtypeStruct((256, 640), BF),
        in_specs=[HBM] * 6,
        out_specs=VMEM,
        scratch_shapes=[
            pltpu.SMEM((64,), jnp.int32),
            pltpu.SMEM((2, 8), jnp.int32),
            pltpu.VMEM((1, 168), F32),
            pltpu.VMEM((256, 512), BF),
            pltpu.VMEM((2, 2048, 256), BF),
            pltpu.VMEM((2, 2048, 256), BF),
            pltpu.SemaphoreType.DMA((4,)),
            pltpu.SemaphoreType.DMA((2,)),
            pltpu.SemaphoreType.DMA((2,)),
            pltpu.SMEM((8,), jnp.int32),
            pltpu.VMEM((2, 512, 128), F32),
            pltpu.VMEM((2, 512, 128), F32),
            pltpu.VMEM((2, 512, 128), F32),
        ],
        compiler_params=pltpu.CompilerParams(vmem_limit_bytes=40 << 20),
        cost_estimate=pl.CostEstimate(
            flops=4 * 10**9, transcendentals=4 * 10**6, bytes_accessed=10 * 2**20
        ),
        name="attend",
    )(in_hbm(page_map), in_hbm(selected), in_hbm(gain), in_hbm(queries), in_hbm(keys), in_hbm(values))


def merge_kernel(x_ref, o_ref, gain_ref):
    marks = x_ref[:, :, 512:640].astype(F32).reshape(256, 128).astype(BF)
    source = lax.broadcasted_iota(jnp.int32, (128, 128), 0)
    for h in range(4):
        spread = jnp.where((source < 12) & ((source & 3) == h), 1.0, 0.0).astype(BF)
        level = jnp.dot(marks, spread, preferred_element_type=F32).reshape(32, 8, 128)
        weight = jnp.exp2(level - jnp.max(level, axis=0, keepdims=True))
        mixed = jnp.sum(weight * x_ref[:, :, h * 128 : (h + 1) * 128].astype(F32), axis=0)
        o_ref[:, h * 128 : (h + 1) * 128] = (mixed / jnp.sum(weight, axis=0)).astype(BF)
    head = lax.axis_index("y") * NC + lax.axis_index("core")
    for k in range(NX):
        gain = x_ref[head * NX + k, :, 512:640].astype(F32)
        for half in range(2):
            gain_ref[k : k + 1, half * 84 : half * 84 + 84] = (
                gain[half : half + 1, 16:100]
                + gain[half + 2 : half + 3, 16:100]
                + gain[half + 4 : half + 5, 16:100]
            )


def packed(rows):
    rest = rows[:, 128:168]
    return jnp.concatenate(
        [
            rows[:, :128],
            jnp.concatenate([rest[:16], rest[16:], jnp.zeros((16, 48), rows.dtype)], axis=1),
        ],
        axis=0,
    )


def project_kernel(a_ref, w_ref, o_ref):
    block = lax.dot_general(
        a_ref[...], w_ref[...], (((1,), (1,)), ((), ())), preferred_element_type=F32
    )
    for h in range(NZ):
        o_ref[h] = packed(block[h * 32 : (h + 1) * 32]).astype(BF)


def stream_kernel(x_ref, r_ref, o_ref):
    total = jnp.sum(x_ref[...].astype(F32), axis=0) + packed(r_ref[...].astype(F32))
    o_ref[...] = total.astype(BF)


def gate_up(a, squares, g_ref, u_ref):
    lane = lax.broadcasted_iota(jnp.int32, (128, 64), 1)
    marks = jnp.zeros((128, 64), F32)
    for n, piece in enumerate(pieces(jnp.sum(squares, axis=1, keepdims=True))):
        marks = jnp.where(lane == n, piece, marks)
    gate = jnp.dot(a, g_ref[...], preferred_element_type=F32)
    up = jnp.dot(a, u_ref[...], preferred_element_type=F32)
    tail = jnp.concatenate([gate[:, 640:], up[:, 640:], marks], axis=1)
    return gate[:, :640].astype(BF), up[:, :640].astype(BF), tail.astype(BF)


def unpacked(block):
    rest = jnp.concatenate([block[..., 32:48, 0:40], block[..., 32:48, 40:80]], axis=-2)
    return block[..., :32, :], rest


def other_half_kernel(
    x_ref, gain_ref, g_ref, u_ref, o_ref, normed_ref, squares_ref, own_ref, own, squares, normed
):
    core = lax.axis_index("core")
    full = jnp.zeros((256, 128), F32)
    part = jnp.zeros((256, 40), F32)
    for x in range(NX):
        main, rest = unpacked(x_ref[:, x, :, :].astype(F32))
        main, rest = main.reshape(256, 128), rest.reshape(256, 40)
        first, second = slice(x * 168, x * 168 + 128), slice(x * 168 + 128, x * 168 + 168)
        full = full + main * main
        part = part + rest * rest
        normed[:, first] = (main * gain_ref[x : x + 1, 0:128]).astype(BF)
        normed[:, second] = (rest * gain_ref[x : x + 1, 128:168]).astype(BF)
        own[:, first], own[:, second] = unpacked(x_ref[lax.axis_index("z"), x, :, :].astype(F32))
    squares[...] = full + jnp.concatenate([part, jnp.zeros((256, 88), F32)], axis=1)
    theirs = pl.ds(pl.multiple_of((1 - core) * 128, 128), 128)
    mine = pl.ds(pl.multiple_of(core * 128, 128), 128)
    o_ref[:, :640], o_ref[:, 640:1280], o_ref[:, 1280:] = gate_up(
        normed[theirs, :], squares[theirs, :], g_ref, u_ref
    )
    normed_ref[...] = normed[mine, :]
    squares_ref[...] = squares[mine, :]
    own_ref[...] = own[pl.ds(pl.multiple_of(lax.axis_index("x") * 8, 8), 8), :].astype(BF)


def own_half_kernel(a_ref, squares_ref, g_ref, u_ref, o_ref):
    o_ref[:, :640], o_ref[:, 640:1280], o_ref[:, 1280:] = gate_up(
        a_ref[...], squares_ref[...], g_ref, u_ref
    )


def pair_kernel(a_ref, b_ref, o_ref):
    both = a_ref[...].astype(F32) + b_ref[...].astype(F32)
    o_ref[:, :1280] = both[:, :1280].astype(BF)
    tail = both[:, 1280:]
    lane = lax.broadcasted_iota(jnp.int32, (128, 128), 1)
    for n, piece in enumerate(pieces(tail[:, 64:65] + tail[:, 65:66] + tail[:, 66:67])):
        tail = jnp.where(lane == 64 + n, piece, tail)
    o_ref[:, 1280:] = tail.astype(BF)


def hidden_kernel(x_ref, o_ref):
    both = jnp.sum(x_ref[...].astype(F32), axis=0)
    squares = both[:, 1344:1345] + both[:, 1345:1346] + both[:, 1346:1347]
    factor = lax.rsqrt(squares / D + EPSILON)
    gate = jnp.concatenate([both[:, :640], both[:, 1280:1312]], axis=1) * factor
    up = jnp.concatenate([both[:, 640:1280], both[:, 1312:1344]], axis=1) * factor
    hidden = (jax.nn.gelu(gate, approximate=True) * up).astype(BF)
    for k in range(NY * NC):
        o_ref[k] = hidden


def down_kernel(a_ref, w_ref, o_ref):
    a = jnp.concatenate([a_ref[y * NC + c] for c in range(NC) for y in range(NY)], axis=0)
    o_ref[...] = jnp.dot(a, w_ref[...], preferred_element_type=F32).astype(BF)


def final_kernel(x_ref, s_ref, o_ref):
    o_ref[...] = (jnp.sum(x_ref[...].astype(F32), axis=0) + s_ref[...].astype(F32)).astype(BF)


def call(kernel, outs, specs, *args, scratch=()):
    outs = [jax.ShapeDtypeStruct(shape, dtype) for shape, dtype in outs]
    results = pl.pallas_call(
        kernel,
        out_shape=outs,
        in_specs=specs,
        out_specs=[VMEM] * len(outs),
        scratch_shapes=scratch,
        compiler_params=pltpu.CompilerParams(vmem_limit_bytes=32 << 20),
        name=kernel.__name__,
    )(*args)
    return results if len(outs) > 1 else results[0]


def exchange(parts, axis):
    return lax.all_to_all(parts, axis, split_axis=0, concat_axis=0, tiled=True)


def place(z, x, h):
    return (z * NX + x) * NY * NC + h


def shards(
    queries, keys, values, page_map, selected, residual_in, out_weight, norm_gain, gate_weight, up_weight, down_weight
):
    sent = attend(page_map, selected, norm_gain.reshape(1, 168), queries, keys, values)
    arrived = exchange(sent.reshape(32, 8, 640), CTX)
    share, gain = call(
        merge_kernel, [((8, 512), BF), ((NX, 168), F32)], [VMEM], arrived
    )
    attention = exchange(jnp.broadcast_to(share, (NZ * NX, 8, 512)), CTX).reshape(256, 512)
    partial = call(project_kernel, [((NZ, 48, 128), BF)], [VMEM, VMEM], attention, out_weight.T)
    projected = exchange(partial, HEADS)
    stream = call(stream_kernel, [((48, 128), BF)], [VMEM, VMEM], projected, residual_in)
    turned = lax.ppermute(
        stream,
        ALL,
        [(place(z, x, h), place(h, x, z)) for z in range(NZ) for x in range(NX) for h in range(NZ)],
    )
    rows = exchange(jnp.broadcast_to(turned, (NZ * NX, 48, 128)), CTX)
    half = ((128, 1408), BF)
    other, normed, squares, own_stream = call(
        other_half_kernel,
        [half, ((128, 672), BF), ((128, 128), F32), ((8, 672), BF)],
        [VMEM, VMEM, VMEM, VMEM],
        rows.reshape(NZ, NX, 48, 128),
        gain,
        gate_weight,
        up_weight,
        scratch=[pltpu.VMEM((32, 672), F32), pltpu.VMEM((256, 128), F32), pltpu.VMEM((256, 672), BF)],
    )
    received = lax.ppermute(other, "core", [(0, 1), (1, 0)])
    mine = call(own_half_kernel, [half], [VMEM] * 4, normed, squares, gate_weight, up_weight)
    pair = call(pair_kernel, [half], [VMEM, VMEM], mine, received)
    shared = exchange(pair.reshape(NY, 32, 1408), "y")
    hidden = exchange(call(hidden_kernel, [((NY * NC, 32, 672), BF)], [VMEM], shared), HEADS)
    down = call(
        down_kernel, [((256, 672), BF)], [VMEM, VMEM], hidden, down_weight
    )
    out_parts = exchange(down.reshape(32, 8, 672), CTX)
    return call(final_kernel, [((8, 672), BF)], [VMEM, VMEM], out_parts, own_stream)


def solution(mesh):
    fine = Mesh(mesh.devices.reshape(NZ, NX, NY, NC), ALL)
    in_specs = (
        P(None, HEADS),
        P(CTX, None, HEADS),
        P(CTX, None, HEADS),
        P(),
        P(),
        P(HEADS, CTX),
        P(HEADS, CTX),
        P(CTX),
        P(HEADS, CTX),
        P(HEADS, CTX),
        P(CTX, HEADS),
    )
    return jax.shard_map(shards, mesh=fine, in_specs=in_specs, out_specs=P(CTX, HEADS), check_vma=False)
```

```python
import functools
import math

import jax
import jax.numpy as jnp
from jax import lax
from jax.experimental import pallas as pl
from jax.experimental.pallas import tpu as pltpu
from jax.sharding import Mesh
from jax.sharding import PartitionSpec as P

D = 5376
HEAD = 128
LAST_PAGE = 63
BF = jnp.bfloat16
F32 = jnp.float32
NEG = -1e30
EXP2_SCALE = 168.0 ** (-0.5) * math.log2(math.e)
EPSILON = 1e-06
CTX = ("z", "x")
HEADS = ("y", "core")
ALL = ("z", "x", "y", "core")
NZ, NX, NY, NC = 8, 4, 4, 2

VMEM = pl.BlockSpec(memory_space=pltpu.VMEM)
HBM = pl.BlockSpec(memory_space=pltpu.HBM)


def pieces(value):
    high = value.astype(BF).astype(F32)
    rest = value - high
    middle = rest.astype(BF).astype(F32)
    return high, middle, rest - middle


def attend_kernel(
    pm_hbm, sel_hbm, gain_hbm, q_hbm, k_hbm, v_hbm, o_ref,
    pm, sel, gain_ref, q_ref, kbuf, vbuf, sems, ksem, vsem, flags, gains_ref, m_ref, l_ref, acc_ref,
):
    tables = (
        pltpu.make_async_copy(pm_hbm, pm, sems.at[0]),
        pltpu.make_async_copy(sel_hbm, sel, sems.at[1]),
    )
    late = (
        pltpu.make_async_copy(q_hbm, q_ref, sems.at[2]),
        pltpu.make_async_copy(gain_hbm, gain_ref, sems.at[3]),
    )

    def page_copies(p):
        return (
            pltpu.make_async_copy(k_hbm.at[p], kbuf.at[p], ksem.at[p]),
            pltpu.make_async_copy(v_hbm.at[p], vbuf.at[p], vsem.at[p]),
        )

    for c in tables + late + page_copies(0) + page_copies(1):
        c.start()
    m_ref[...] = jnp.full_like(m_ref, NEG)
    l_ref[...] = jnp.zeros_like(l_ref)
    acc_ref[...] = jnp.zeros_like(acc_ref)
    for n in range(6):
        flags[n] = jnp.int32(0)
    for c in tables:
        c.wait()

    first_slot = (lax.axis_index("z") * NX + lax.axis_index("x")) * 2

    def look(n, carry):
        logical = sel[n >> 3, n & 7]
        p = pm[logical] - first_slot

        @pl.when((p == 0) | (p == 1))
        def _():
            flags[p * 2 + (n >> 3)] = jnp.int32(1)

            @pl.when(logical == LAST_PAGE)
            def _():
                flags[4 + p] = jnp.int32(1)

        return carry

    lax.fori_loop(0, 16, look, 0)
    for c in late:
        c.wait()
    halves = []
    for piece in pieces(gain_ref[...]):
        halves += [piece[:, :84], piece[:, 84:168]]
    halves += [jnp.zeros((1, 84), F32)] * 2
    gains_ref[...] = jnp.concatenate(
        [jnp.zeros((8, 16), F32), jnp.concatenate(halves, axis=0), jnp.zeros((8, 28), F32)], axis=1
    )

    def attend_tile(p, t):
        span = pl.ds(pl.multiple_of(t * 256, 256), 256)
        rows = pl.ds(pl.multiple_of(t * 128, 128), 128)
        limit = jnp.where(flags[4 + p] != 0, t * 128, 1 << 20)
        row = lax.broadcasted_iota(jnp.int32, (256, 256), 0)
        col = lax.broadcasted_iota(jnp.int32, (256, 256), 1)
        visible = col <= (row & 127) + limit

        def scores(kv):
            q = jnp.concatenate(
                [q_ref[rows, (2 * kv + g) * 128 : (2 * kv + g + 1) * 128] for g in range(2)], axis=0
            )
            s = lax.dot_general(
                q,
                kbuf[p, :, kv * 128 : (kv + 1) * 128],
                (((1,), (1,)), ((), ())),
                preferred_element_type=F32,
            )
            return jnp.concatenate([s[:, :1792], jnp.where(visible, s[:, 1792:], NEG)], axis=1)

        for kv, s in enumerate([scores(0), scores(1)]):
            old = m_ref[kv, span, :]
            top = s[:, :128]
            for a in range(1, 16):
                top = jnp.maximum(top, s[:, a * 128 : (a + 1) * 128])
            new = jnp.maximum(old, jnp.max(top, axis=1, keepdims=True))
            keep = jnp.exp2((old - new) * EXP2_SCALE)
            w = jnp.exp2((s - jnp.concatenate([new] * 16, axis=1)) * EXP2_SCALE)
            part = w[:, :128]
            for a in range(1, 16):
                part = part + w[:, a * 128 : (a + 1) * 128]
            mixed = jnp.dot(
                w.astype(BF), vbuf[p, :, kv * 128 : (kv + 1) * 128], preferred_element_type=F32
            )
            m_ref[kv, span, :] = new
            l_ref[kv, span, :] = l_ref[kv, span, :] * keep + part
            acc_ref[kv, span, :] = acc_ref[kv, span, :] * keep + mixed

    def page(p, carry):
        for c in page_copies(p):
            c.wait()

        def tile(t, carry):
            @pl.when(flags[p * 2 + t] != 0)
            def _():
                attend_tile(p, t)

            return carry

        return lax.fori_loop(0, 2, tile, carry)

    lax.fori_loop(0, 2, page, 0)

    lane = lax.broadcasted_iota(jnp.int32, (128, 128), 1)

    def finish(t, carry):
        marks = jnp.concatenate([gains_ref[...]] * 16, axis=0)
        out_rows = pl.ds(pl.multiple_of(t * 128, 128), 128)
        for h in range(4):
            kv = h // 2
            rows = pl.ds(pl.multiple_of(t * 256 + (h % 2) * 128, 128), 128)
            total = jnp.sum(l_ref[kv, rows, :], axis=1, keepdims=True)
            some = total > 0.0
            safe = jnp.where(some, total, 1.0)
            level = jnp.where(some, m_ref[kv, rows, :][:, :1] * EXP2_SCALE + jnp.log2(safe), NEG)
            o_ref[out_rows, h * 128 : (h + 1) * 128] = (acc_ref[kv, rows, :] * (1.0 / safe)).astype(BF)
            for n, piece in enumerate(pieces(level)):
                marks = jnp.where(lane == h + 4 * n, piece, marks)
        o_ref[out_rows, 512:640] = marks.astype(BF)
        return carry

    lax.fori_loop(0, 2, finish, 0)


def in_hbm(array):
    return pltpu.with_memory_space_constraint(array, pltpu.HBM)


def attend(page_map, selected, gain, queries, keys, values):
    return pl.pallas_call(
        attend_kernel,
        out_shape=jax.ShapeDtypeStruct((256, 640), BF),
        in_specs=[HBM] * 6,
        out_specs=VMEM,
        scratch_shapes=[
            pltpu.SMEM((64,), jnp.int32),
            pltpu.SMEM((2, 8), jnp.int32),
            pltpu.VMEM((1, 168), F32),
            pltpu.VMEM((256, 512), BF),
            pltpu.VMEM((2, 2048, 256), BF),
            pltpu.VMEM((2, 2048, 256), BF),
            pltpu.SemaphoreType.DMA((4,)),
            pltpu.SemaphoreType.DMA((2,)),
            pltpu.SemaphoreType.DMA((2,)),
            pltpu.SMEM((8,), jnp.int32),
            pltpu.VMEM((8, 128), F32),
            pltpu.VMEM((2, 512, 128), F32),
            pltpu.VMEM((2, 512, 128), F32),
            pltpu.VMEM((2, 512, 128), F32),
        ],
        compiler_params=pltpu.CompilerParams(vmem_limit_bytes=40 << 20),
        cost_estimate=pl.CostEstimate(
            flops=4 * 10**9, transcendentals=4 * 10**6, bytes_accessed=10 * 2**20
        ),
        name="attend",
    )(in_hbm(page_map), in_hbm(selected), in_hbm(gain), in_hbm(queries), in_hbm(keys), in_hbm(values))


def merge_kernel(x_ref, o_ref, gain_ref):
    marks = x_ref[:, :, 512:640].astype(F32).reshape(256, 128).astype(BF)
    source = lax.broadcasted_iota(jnp.int32, (128, 128), 0)
    for h in range(4):
        spread = jnp.where((source < 12) & ((source & 3) == h), 1.0, 0.0).astype(BF)
        level = jnp.dot(marks, spread, preferred_element_type=F32).reshape(32, 8, 128)
        weight = jnp.exp2(level - jnp.max(level, axis=0, keepdims=True))
        mixed = jnp.sum(weight * x_ref[:, :, h * 128 : (h + 1) * 128].astype(F32), axis=0)
        o_ref[:, h * 128 : (h + 1) * 128] = (mixed / jnp.sum(weight, axis=0)).astype(BF)
    head = lax.axis_index("y") * NC + lax.axis_index("core")
    for k in range(NX):
        gain = x_ref[head * NX + k, :, 512:640].astype(F32)
        for half in range(2):
            gain_ref[k : k + 1, half * 84 : half * 84 + 84] = (
                gain[half : half + 1, 16:100]
                + gain[half + 2 : half + 3, 16:100]
                + gain[half + 4 : half + 5, 16:100]
            )


def packed(rows):
    rest = rows[:, 128:168]
    return jnp.concatenate(
        [
            rows[:, :128],
            jnp.concatenate([rest[:16], rest[16:], jnp.zeros((16, 48), rows.dtype)], axis=1),
        ],
        axis=0,
    )


def project_kernel(a_ref, w_ref, o_ref):
    block = lax.dot_general(
        a_ref[...], w_ref[...], (((1,), (1,)), ((), ())), preferred_element_type=F32
    )
    for h in range(NZ):
        o_ref[h] = packed(block[h * 32 : (h + 1) * 32]).astype(BF)


def stream_kernel(x_ref, r_ref, o_ref):
    total = jnp.sum(x_ref[...].astype(F32), axis=0) + packed(r_ref[...].astype(F32))
    o_ref[...] = total.astype(BF)


def gate_up(a, squares, g_ref, u_ref):
    lane = lax.broadcasted_iota(jnp.int32, (128, 64), 1)
    marks = jnp.zeros((128, 64), F32)
    for n, piece in enumerate(pieces(jnp.sum(squares, axis=1, keepdims=True))):
        marks = jnp.where(lane == n, piece, marks)
    gate = jnp.dot(a, g_ref[...], preferred_element_type=F32)
    up = jnp.dot(a, u_ref[...], preferred_element_type=F32)
    tail = jnp.concatenate([gate[:, 640:], up[:, 640:], marks], axis=1)
    return gate[:, :640].astype(BF), up[:, :640].astype(BF), tail.astype(BF)


def unpacked(block):
    rest = jnp.concatenate([block[..., 32:48, 0:40], block[..., 32:48, 40:80]], axis=-2)
    return block[..., :32, :], rest


def other_half_kernel(
    x_ref, gain_ref, g_ref, u_ref, o_ref, normed_ref, squares_ref, own_ref, own, squares, normed
):
    core = lax.axis_index("core")
    full = jnp.zeros((256, 128), F32)
    part = jnp.zeros((256, 40), F32)
    for x in range(NX):
        main, rest = unpacked(x_ref[:, x, :, :].astype(F32))
        main, rest = main.reshape(256, 128), rest.reshape(256, 40)
        first, second = slice(x * 168, x * 168 + 128), slice(x * 168 + 128, x * 168 + 168)
        full = full + main * main
        part = part + rest * rest
        normed[:, first] = (main * gain_ref[x : x + 1, 0:128]).astype(BF)
        normed[:, second] = (rest * gain_ref[x : x + 1, 128:168]).astype(BF)
        own[:, first], own[:, second] = unpacked(x_ref[lax.axis_index("z"), x, :, :].astype(F32))
    squares[...] = full + jnp.concatenate([part, jnp.zeros((256, 88), F32)], axis=1)
    theirs = pl.ds(pl.multiple_of((1 - core) * 128, 128), 128)
    mine = pl.ds(pl.multiple_of(core * 128, 128), 128)
    o_ref[:, :640], o_ref[:, 640:1280], o_ref[:, 1280:] = gate_up(
        normed[theirs, :], squares[theirs, :], g_ref, u_ref
    )
    normed_ref[...] = normed[mine, :]
    squares_ref[...] = squares[mine, :]
    own_ref[...] = own[pl.ds(pl.multiple_of(lax.axis_index("x") * 8, 8), 8), :].astype(BF)


def own_half_kernel(a_ref, squares_ref, g_ref, u_ref, o_ref):
    o_ref[:, :640], o_ref[:, 640:1280], o_ref[:, 1280:] = gate_up(
        a_ref[...], squares_ref[...], g_ref, u_ref
    )


def pair_kernel(a_ref, b_ref, o_ref):
    both = a_ref[...].astype(F32) + b_ref[...].astype(F32)
    o_ref[:, :1280] = both[:, :1280].astype(BF)
    tail = both[:, 1280:]
    lane = lax.broadcasted_iota(jnp.int32, (128, 128), 1)
    for n, piece in enumerate(pieces(tail[:, 64:65] + tail[:, 65:66] + tail[:, 66:67])):
        tail = jnp.where(lane == 64 + n, piece, tail)
    o_ref[:, 1280:] = tail.astype(BF)


def hidden_kernel(x_ref, o_ref):
    both = jnp.sum(x_ref[...].astype(F32), axis=0)
    squares = both[:, 1344:1345] + both[:, 1345:1346] + both[:, 1346:1347]
    factor = lax.rsqrt(squares / D + EPSILON)
    gate = jnp.concatenate([both[:, :640], both[:, 1280:1312]], axis=1) * factor
    up = jnp.concatenate([both[:, 640:1280], both[:, 1312:1344]], axis=1) * factor
    hidden = (jax.nn.gelu(gate, approximate=True) * up).astype(BF)
    for k in range(NY * NC):
        o_ref[k] = hidden


def down_kernel(a_ref, w_ref, o_ref):
    a = jnp.concatenate([a_ref[y * NC + c] for c in range(NC) for y in range(NY)], axis=0)
    o_ref[...] = jnp.dot(a, w_ref[...], preferred_element_type=F32).astype(BF)


def final_kernel(x_ref, s_ref, o_ref):
    o_ref[...] = (jnp.sum(x_ref[...].astype(F32), axis=0) + s_ref[...].astype(F32)).astype(BF)


def call(kernel, outs, specs, *args, scratch=()):
    outs = [jax.ShapeDtypeStruct(shape, dtype) for shape, dtype in outs]
    results = pl.pallas_call(
        kernel,
        out_shape=outs,
        in_specs=specs,
        out_specs=[VMEM] * len(outs),
        scratch_shapes=scratch,
        compiler_params=pltpu.CompilerParams(vmem_limit_bytes=32 << 20),
        name=kernel.__name__,
    )(*args)
    return results if len(outs) > 1 else results[0]


def exchange(parts, axis):
    return lax.all_to_all(parts, axis, split_axis=0, concat_axis=0, tiled=True)


def place(z, x, h):
    return (z * NX + x) * NY * NC + h


def shards(
    queries, keys, values, page_map, selected, residual_in, out_weight, norm_gain, gate_weight, up_weight, down_weight
):
    sent = attend(page_map, selected, norm_gain.reshape(1, 168), queries, keys, values)
    arrived = exchange(sent.reshape(32, 8, 640), CTX)
    share, gain = call(
        merge_kernel, [((8, 512), BF), ((NX, 168), F32)], [VMEM], arrived
    )
    attention = exchange(jnp.broadcast_to(share, (NZ * NX, 8, 512)), CTX).reshape(256, 512)
    partial = call(project_kernel, [((NZ, 48, 128), BF)], [VMEM, VMEM], attention, out_weight.T)
    projected = exchange(partial, HEADS)
    stream = call(stream_kernel, [((48, 128), BF)], [VMEM, VMEM], projected, residual_in)
    turned = lax.ppermute(
        stream,
        ALL,
        [(place(z, x, h), place(h, x, z)) for z in range(NZ) for x in range(NX) for h in range(NZ)],
    )
    rows = exchange(jnp.broadcast_to(turned, (NZ * NX, 48, 128)), CTX)
    half = ((128, 1408), BF)
    other, normed, squares, own_stream = call(
        other_half_kernel,
        [half, ((128, 672), BF), ((128, 128), F32), ((8, 672), BF)],
        [VMEM, VMEM, VMEM, VMEM],
        rows.reshape(NZ, NX, 48, 128),
        gain,
        gate_weight,
        up_weight,
        scratch=[pltpu.VMEM((32, 672), F32), pltpu.VMEM((256, 128), F32), pltpu.VMEM((256, 672), BF)],
    )
    received = lax.ppermute(other, "core", [(0, 1), (1, 0)])
    mine = call(own_half_kernel, [half], [VMEM] * 4, normed, squares, gate_weight, up_weight)
    pair = call(pair_kernel, [half], [VMEM, VMEM], mine, received)
    shared = exchange(pair.reshape(NY, 32, 1408), "y")
    hidden = exchange(call(hidden_kernel, [((NY * NC, 32, 672), BF)], [VMEM], shared), HEADS)
    down = call(
        down_kernel, [((256, 672), BF)], [VMEM, VMEM], hidden, down_weight
    )
    out_parts = exchange(down.reshape(32, 8, 672), CTX)
    return call(final_kernel, [((8, 672), BF)], [VMEM, VMEM], out_parts, own_stream)


def solution(mesh):
    fine = Mesh(mesh.devices.reshape(NZ, NX, NY, NC), ALL)
    in_specs = (
        P(None, HEADS),
        P(CTX, None, HEADS),
        P(CTX, None, HEADS),
        P(),
        P(),
        P(HEADS, CTX),
        P(HEADS, CTX),
        P(CTX),
        P(HEADS, CTX),
        P(HEADS, CTX),
        P(CTX, HEADS),
    )
    return jax.shard_map(shards, mesh=fine, in_specs=in_specs, out_specs=P(CTX, HEADS), check_vma=False)
```

```python
import functools
import math

import jax
import jax.numpy as jnp
from jax import lax
from jax.experimental import pallas as pl
from jax.experimental.pallas import tpu as pltpu
from jax.sharding import Mesh
from jax.sharding import PartitionSpec as P

D = 5376
HEAD = 128
LAST_PAGE = 63
BF = jnp.bfloat16
F32 = jnp.float32
NEG = -1e30
EXP2_SCALE = 168.0 ** (-0.5) * math.log2(math.e)
EPSILON = 1e-06
CTX = ("z", "x")
HEADS = ("y", "core")
ALL = ("z", "x", "y", "core")
NZ, NX, NY, NC = 8, 4, 4, 2

VMEM = pl.BlockSpec(memory_space=pltpu.VMEM)
HBM = pl.BlockSpec(memory_space=pltpu.HBM)


def pieces(value):
    high = value.astype(BF).astype(F32)
    rest = value - high
    middle = rest.astype(BF).astype(F32)
    return high, middle, rest - middle


def attend_kernel(
    pm_hbm, sel_hbm, gain_hbm, q_hbm, k_hbm, v_hbm, o_ref,
    pm, sel, gain_ref, q_ref, kbuf, vbuf, sems, ksem, vsem, flags, gains_ref, m_ref, l_ref, acc_ref,
):
    tables = (
        pltpu.make_async_copy(pm_hbm, pm, sems.at[0]),
        pltpu.make_async_copy(sel_hbm, sel, sems.at[1]),
    )
    late = (
        pltpu.make_async_copy(q_hbm, q_ref, sems.at[2]),
        pltpu.make_async_copy(gain_hbm, gain_ref, sems.at[3]),
    )

    def page_copies(p):
        return (
            pltpu.make_async_copy(k_hbm.at[p], kbuf.at[p], ksem.at[p]),
            pltpu.make_async_copy(v_hbm.at[p], vbuf.at[p], vsem.at[p]),
        )

    for c in tables + late + page_copies(0) + page_copies(1):
        c.start()
    m_ref[...] = jnp.full_like(m_ref, NEG)
    l_ref[...] = jnp.zeros_like(l_ref)
    acc_ref[...] = jnp.zeros_like(acc_ref)
    for n in range(6):
        flags[n] = jnp.int32(0)
    for c in tables:
        c.wait()

    first_slot = (lax.axis_index("z") * NX + lax.axis_index("x")) * 2

    def look(n, carry):
        logical = sel[n >> 3, n & 7]
        p = pm[logical] - first_slot

        @pl.when((p == 0) | (p == 1))
        def _():
            flags[p * 2 + (n >> 3)] = jnp.int32(1)

            @pl.when(logical == LAST_PAGE)
            def _():
                flags[4 + p] = jnp.int32(1)

        return carry

    lax.fori_loop(0, 16, look, 0)
    for c in late:
        c.wait()
    halves = []
    for piece in pieces(gain_ref[...]):
        halves += [piece[:, :84], piece[:, 84:168]]
    halves += [jnp.zeros((1, 84), F32)] * 2
    gains_ref[...] = jnp.concatenate(
        [jnp.zeros((8, 16), F32), jnp.concatenate(halves, axis=0), jnp.zeros((8, 28), F32)], axis=1
    )

    def attend_tile(p, t):
        span = pl.ds(pl.multiple_of(t * 256, 256), 256)
        rows = pl.ds(pl.multiple_of(t * 128, 128), 128)
        limit = jnp.where(flags[4 + p] != 0, t * 128, 1 << 20)
        row = lax.broadcasted_iota(jnp.int32, (256, 256), 0)
        col = lax.broadcasted_iota(jnp.int32, (256, 256), 1)
        visible = col <= (row & 127) + limit

        def scores(kv):
            q = jnp.concatenate(
                [q_ref[rows, (2 * kv + g) * 128 : (2 * kv + g + 1) * 128] for g in range(2)], axis=0
            )
            s = lax.dot_general(
                q,
                kbuf[p, :, kv * 128 : (kv + 1) * 128],
                (((1,), (1,)), ((), ())),
                preferred_element_type=F32,
            )
            return jnp.concatenate([s[:, :1792], jnp.where(visible, s[:, 1792:], NEG)], axis=1)

        for kv, s in enumerate([scores(0), scores(1)]):
            old = m_ref[kv, span, :]
            top = s[:, :128]
            for a in range(1, 16):
                top = jnp.maximum(top, s[:, a * 128 : (a + 1) * 128])
            new = jnp.maximum(old, jnp.max(top, axis=1, keepdims=True))
            keep = jnp.exp2((old - new) * EXP2_SCALE)
            w = jnp.exp2((s - jnp.concatenate([new] * 16, axis=1)) * EXP2_SCALE)
            part = w[:, :128]
            for a in range(1, 16):
                part = part + w[:, a * 128 : (a + 1) * 128]
            mixed = jnp.dot(
                w.astype(BF), vbuf[p, :, kv * 128 : (kv + 1) * 128], preferred_element_type=F32
            )
            m_ref[kv, span, :] = new
            l_ref[kv, span, :] = l_ref[kv, span, :] * keep + part
            acc_ref[kv, span, :] = acc_ref[kv, span, :] * keep + mixed

    def page(p, carry):
        for c in page_copies(p):
            c.wait()

        def tile(t, carry):
            @pl.when(flags[p * 2 + t] != 0)
            def _():
                attend_tile(p, t)

            return carry

        return lax.fori_loop(0, 2, tile, carry)

    lax.fori_loop(0, 2, page, 0)

    lane = lax.broadcasted_iota(jnp.int32, (128, 128), 1)

    def finish(t, carry):
        marks = jnp.concatenate([gains_ref[...]] * 16, axis=0)
        out_rows = pl.ds(pl.multiple_of(t * 128, 128), 128)
        for h in range(4):
            kv = h // 2
            rows = pl.ds(pl.multiple_of(t * 256 + (h % 2) * 128, 128), 128)
            total = jnp.sum(l_ref[kv, rows, :], axis=1, keepdims=True)
            some = total > 0.0
            safe = jnp.where(some, total, 1.0)
            level = jnp.where(some, m_ref[kv, rows, :][:, :1] * EXP2_SCALE + jnp.log2(safe), NEG)
            o_ref[out_rows, h * 128 : (h + 1) * 128] = (acc_ref[kv, rows, :] * (1.0 / safe)).astype(BF)
            for n, piece in enumerate(pieces(level)):
                marks = jnp.where(lane == h + 4 * n, piece, marks)
        o_ref[out_rows, 512:640] = marks.astype(BF)
        return carry

    lax.fori_loop(0, 2, finish, 0)


def in_hbm(array):
    return pltpu.with_memory_space_constraint(array, pltpu.HBM)


def attend(page_map, selected, gain, queries, keys, values):
    return pl.pallas_call(
        attend_kernel,
        out_shape=jax.ShapeDtypeStruct((256, 640), BF),
        in_specs=[HBM] * 6,
        out_specs=VMEM,
        scratch_shapes=[
            pltpu.SMEM((64,), jnp.int32),
            pltpu.SMEM((2, 8), jnp.int32),
            pltpu.VMEM((1, 168), F32),
            pltpu.VMEM((256, 512), BF),
            pltpu.VMEM((2, 2048, 256), BF),
            pltpu.VMEM((2, 2048, 256), BF),
            pltpu.SemaphoreType.DMA((4,)),
            pltpu.SemaphoreType.DMA((2,)),
            pltpu.SemaphoreType.DMA((2,)),
            pltpu.SMEM((8,), jnp.int32),
            pltpu.VMEM((8, 128), F32),
            pltpu.VMEM((2, 512, 128), F32),
            pltpu.VMEM((2, 512, 128), F32),
            pltpu.VMEM((2, 512, 128), F32),
        ],
        compiler_params=pltpu.CompilerParams(vmem_limit_bytes=40 << 20),
        cost_estimate=pl.CostEstimate(
            flops=4 * 10**9, transcendentals=4 * 10**6, bytes_accessed=10 * 2**20
        ),
        name="attend",
    )(in_hbm(page_map), in_hbm(selected), in_hbm(gain), in_hbm(queries), in_hbm(keys), in_hbm(values))


def merge_kernel(x_ref, o_ref, gain_ref):
    marks = x_ref[:, :, 512:640].astype(F32).reshape(256, 128).astype(BF)
    source = lax.broadcasted_iota(jnp.int32, (128, 128), 0)
    for h in range(4):
        spread = jnp.where((source < 12) & ((source & 3) == h), 1.0, 0.0).astype(BF)
        level = jnp.dot(marks, spread, preferred_element_type=F32).reshape(32, 8, 128)
        weight = jnp.exp2(level - jnp.max(level, axis=0, keepdims=True))
        mixed = jnp.sum(weight * x_ref[:, :, h * 128 : (h + 1) * 128].astype(F32), axis=0)
        o_ref[:, h * 128 : (h + 1) * 128] = (mixed / jnp.sum(weight, axis=0)).astype(BF)
    head = lax.axis_index("y") * NC + lax.axis_index("core")
    for k in range(NX):
        gain = x_ref[head * NX + k, :, 512:640].astype(F32)
        for half in range(2):
            gain_ref[k : k + 1, half * 84 : half * 84 + 84] = (
                gain[half : half + 1, 16:100]
                + gain[half + 2 : half + 3, 16:100]
                + gain[half + 4 : half + 5, 16:100]
            )


def packed(rows):
    rest = rows[:, 128:168]
    return jnp.concatenate(
        [
            rows[:, :128],
            jnp.concatenate([rest[:16], rest[16:], jnp.zeros((16, 48), rows.dtype)], axis=1),
        ],
        axis=0,
    )


def project_kernel(a_ref, w_ref, o_ref):
    block = lax.dot_general(
        a_ref[...], w_ref[...], (((1,), (1,)), ((), ())), preferred_element_type=F32
    )
    for h in range(NZ):
        o_ref[h] = packed(block[h * 32 : (h + 1) * 32]).astype(BF)


def stream_kernel(x_ref, r_ref, o_ref):
    total = jnp.sum(x_ref[...].astype(F32), axis=0) + packed(r_ref[...].astype(F32))
    o_ref[...] = total.astype(BF)


def gate_up(a, squares, g_ref, u_ref):
    lane = lax.broadcasted_iota(jnp.int32, (128, 64), 1)
    marks = jnp.zeros((128, 64), F32)
    for n, piece in enumerate(pieces(jnp.sum(squares, axis=1, keepdims=True))):
        marks = jnp.where(lane == n, piece, marks)
    gate = jnp.dot(a, g_ref[...], preferred_element_type=F32)
    up = jnp.dot(a, u_ref[...], preferred_element_type=F32)
    tail = jnp.concatenate([gate[:, 640:], up[:, 640:], marks], axis=1)
    return gate[:, :640].astype(BF), up[:, :640].astype(BF), tail.astype(BF)


def unpacked(block):
    rest = jnp.concatenate([block[..., 32:48, 0:40], block[..., 32:48, 40:80]], axis=-2)
    return block[..., :32, :], rest


def other_half_kernel(
    x_ref, gain_ref, g_ref, u_ref, o_ref, normed_ref, squares_ref, own_ref, own, squares, normed
):
    core = lax.axis_index("core")
    full = jnp.zeros((256, 128), F32)
    part = jnp.zeros((256, 40), F32)
    for x in range(NX):
        main, rest = unpacked(x_ref[:, x, :, :].astype(F32))
        main, rest = main.reshape(256, 128), rest.reshape(256, 40)
        first, second = slice(x * 168, x * 168 + 128), slice(x * 168 + 128, x * 168 + 168)
        full = full + main * main
        part = part + rest * rest
        normed[:, first] = (main * gain_ref[x : x + 1, 0:128]).astype(BF)
        normed[:, second] = (rest * gain_ref[x : x + 1, 128:168]).astype(BF)
        own[:, first], own[:, second] = unpacked(x_ref[lax.axis_index("z"), x, :, :].astype(F32))
    squares[...] = full + jnp.concatenate([part, jnp.zeros((256, 88), F32)], axis=1)
    theirs = pl.ds(pl.multiple_of((1 - core) * 128, 128), 128)
    mine = pl.ds(pl.multiple_of(core * 128, 128), 128)
    o_ref[:, :640], o_ref[:, 640:1280], o_ref[:, 1280:] = gate_up(
        normed[theirs, :], squares[theirs, :], g_ref, u_ref
    )
    normed_ref[...] = normed[mine, :]
    squares_ref[...] = squares[mine, :]
    own_ref[...] = own[pl.ds(pl.multiple_of(lax.axis_index("x") * 8, 8), 8), :].astype(BF)


def own_half_kernel(a_ref, squares_ref, g_ref, u_ref, o_ref):
    o_ref[:, :640], o_ref[:, 640:1280], o_ref[:, 1280:] = gate_up(
        a_ref[...], squares_ref[...], g_ref, u_ref
    )


def pair_kernel(a_ref, b_ref, o_ref):
    both = a_ref[...].astype(F32) + b_ref[...].astype(F32)
    o_ref[:, :1280] = both[:, :1280].astype(BF)
    tail = both[:, 1280:]
    lane = lax.broadcasted_iota(jnp.int32, (128, 128), 1)
    for n, piece in enumerate(pieces(tail[:, 64:65] + tail[:, 65:66] + tail[:, 66:67])):
        tail = jnp.where(lane == 64 + n, piece, tail)
    o_ref[:, 1280:] = tail.astype(BF)


def hidden_kernel(x_ref, o_ref):
    both = jnp.sum(x_ref[...].astype(F32), axis=0)
    squares = both[:, 1344:1345] + both[:, 1345:1346] + both[:, 1346:1347]
    factor = lax.rsqrt(squares / D + EPSILON)
    gate = jnp.concatenate([both[:, :640], both[:, 1280:1312]], axis=1) * factor
    up = jnp.concatenate([both[:, 640:1280], both[:, 1312:1344]], axis=1) * factor
    hidden = jax.nn.gelu(gate, approximate=True) * up
    tail = jnp.concatenate([hidden[g * 8 : (g + 1) * 8, 640:] for g in range(4)], axis=1)
    blocks = [hidden[:, j * 128 : (j + 1) * 128] for j in range(5)]
    rows = jnp.concatenate(blocks + [tail], axis=0).astype(BF)
    for k in range(NY * NC):
        o_ref[k] = rows


def down_kernel(a_ref, w_ref, o_ref):
    mains, tails = [], []
    for c in range(NC):
        for y in range(NY):
            rows = a_ref[y * NC + c].astype(F32)
            mains.append(
                jnp.concatenate([rows[j * 32 : (j + 1) * 32] for j in range(5)], axis=1).astype(BF)
            )
            tails += [rows[160:, g * 32 : (g + 1) * 32] for g in range(4)]
    main = jnp.concatenate(mains, axis=0)
    tail = jnp.concatenate(tails, axis=0).astype(BF)
    total = jnp.dot(main, w_ref[:640, :], preferred_element_type=F32)
    total = total + jnp.dot(tail, w_ref[640:, :], preferred_element_type=F32)
    o_ref[...] = total.astype(BF)


def final_kernel(x_ref, s_ref, o_ref):
    o_ref[...] = (jnp.sum(x_ref[...].astype(F32), axis=0) + s_ref[...].astype(F32)).astype(BF)


def call(kernel, outs, specs, *args, scratch=()):
    outs = [jax.ShapeDtypeStruct(shape, dtype) for shape, dtype in outs]
    results = pl.pallas_call(
        kernel,
        out_shape=outs,
        in_specs=specs,
        out_specs=[VMEM] * len(outs),
        scratch_shapes=scratch,
        compiler_params=pltpu.CompilerParams(vmem_limit_bytes=32 << 20),
        name=kernel.__name__,
    )(*args)
    return results if len(outs) > 1 else results[0]


def exchange(parts, axis):
    return lax.all_to_all(parts, axis, split_axis=0, concat_axis=0, tiled=True)


def place(z, x, h):
    return (z * NX + x) * NY * NC + h


def shards(
    queries, keys, values, page_map, selected, residual_in, out_weight, norm_gain, gate_weight, up_weight, down_weight
):
    sent = attend(page_map, selected, norm_gain.reshape(1, 168), queries, keys, values)
    arrived = exchange(sent.reshape(32, 8, 640), CTX)
    share, gain = call(
        merge_kernel, [((8, 512), BF), ((NX, 168), F32)], [VMEM], arrived
    )
    attention = exchange(jnp.broadcast_to(share, (NZ * NX, 8, 512)), CTX).reshape(256, 512)
    partial = call(project_kernel, [((NZ, 48, 128), BF)], [VMEM, VMEM], attention, out_weight.T)
    projected = exchange(partial, HEADS)
    stream = call(stream_kernel, [((48, 128), BF)], [VMEM, VMEM], projected, residual_in)
    turned = lax.ppermute(
        stream,
        ALL,
        [(place(z, x, h), place(h, x, z)) for z in range(NZ) for x in range(NX) for h in range(NZ)],
    )
    rows = exchange(jnp.broadcast_to(turned, (NZ * NX, 48, 128)), CTX)
    half = ((128, 1408), BF)
    other, normed, squares, own_stream = call(
        other_half_kernel,
        [half, ((128, 672), BF), ((128, 128), F32), ((8, 672), BF)],
        [VMEM, VMEM, VMEM, VMEM],
        rows.reshape(NZ, NX, 48, 128),
        gain,
        gate_weight,
        up_weight,
        scratch=[pltpu.VMEM((32, 672), F32), pltpu.VMEM((256, 128), F32), pltpu.VMEM((256, 672), BF)],
    )
    received = lax.ppermute(other, "core", [(0, 1), (1, 0)])
    mine = call(own_half_kernel, [half], [VMEM] * 4, normed, squares, gate_weight, up_weight)
    pair = call(pair_kernel, [half], [VMEM, VMEM], mine, received)
    shared = exchange(pair.reshape(NY, 32, 1408), "y")
    hidden = exchange(call(hidden_kernel, [((NY * NC, 168, 128), BF)], [VMEM], shared), HEADS)
    down = call(
        down_kernel, [((256, 672), BF)], [VMEM, VMEM], hidden, down_weight
    )
    out_parts = exchange(down.reshape(32, 8, 672), CTX)
    return call(final_kernel, [((8, 672), BF)], [VMEM, VMEM], out_parts, own_stream)


def solution(mesh):
    fine = Mesh(mesh.devices.reshape(NZ, NX, NY, NC), ALL)
    in_specs = (
        P(None, HEADS),
        P(CTX, None, HEADS),
        P(CTX, None, HEADS),
        P(),
        P(),
        P(HEADS, CTX),
        P(HEADS, CTX),
        P(CTX),
        P(HEADS, CTX),
        P(HEADS, CTX),
        P(CTX, HEADS),
    )
    return jax.shard_map(shards, mesh=fine, in_specs=in_specs, out_specs=P(CTX, HEADS), check_vma=False)
```

```python
import functools
import math

import jax
import jax.numpy as jnp
from jax import lax
from jax.experimental import pallas as pl
from jax.experimental.pallas import tpu as pltpu
from jax.sharding import Mesh
from jax.sharding import PartitionSpec as P

D = 5376
HEAD = 128
LAST_PAGE = 63
BF = jnp.bfloat16
F32 = jnp.float32
NEG = -1e30
EXP2_SCALE = 168.0 ** (-0.5) * math.log2(math.e)
EPSILON = 1e-06
CTX = ("z", "x")
HEADS = ("y", "core")
ALL = ("z", "x", "y", "core")
NZ, NX, NY, NC = 8, 4, 4, 2

VMEM = pl.BlockSpec(memory_space=pltpu.VMEM)
HBM = pl.BlockSpec(memory_space=pltpu.HBM)


def pieces(value):
    high = value.astype(BF).astype(F32)
    rest = value - high
    middle = rest.astype(BF).astype(F32)
    return high, middle, rest - middle


def attend_kernel(
    pm_hbm, sel_hbm, gain_hbm, q_hbm, k_hbm, v_hbm, o_ref,
    pm, sel, gain_ref, q_ref, kbuf, vbuf, sems, ksem, vsem, flags, gains_ref, m_ref, l_ref, acc_ref,
):
    tables = (
        pltpu.make_async_copy(pm_hbm, pm, sems.at[0]),
        pltpu.make_async_copy(sel_hbm, sel, sems.at[1]),
    )
    late = (
        pltpu.make_async_copy(q_hbm, q_ref, sems.at[2]),
        pltpu.make_async_copy(gain_hbm, gain_ref, sems.at[3]),
    )

    def page_copies(p):
        return (
            pltpu.make_async_copy(k_hbm.at[p], kbuf.at[p], ksem.at[p]),
            pltpu.make_async_copy(v_hbm.at[p], vbuf.at[p], vsem.at[p]),
        )

    for c in tables + late + page_copies(0) + page_copies(1):
        c.start()
    m_ref[...] = jnp.full_like(m_ref, NEG)
    l_ref[...] = jnp.zeros_like(l_ref)
    acc_ref[...] = jnp.zeros_like(acc_ref)
    for n in range(6):
        flags[n] = jnp.int32(0)
    for c in tables:
        c.wait()

    first_slot = (lax.axis_index("z") * NX + lax.axis_index("x")) * 2

    def look(n, carry):
        logical = sel[n >> 3, n & 7]
        p = pm[logical] - first_slot

        @pl.when((p == 0) | (p == 1))
        def _():
            flags[p * 2 + (n >> 3)] = jnp.int32(1)

            @pl.when(logical == LAST_PAGE)
            def _():
                flags[4 + p] = jnp.int32(1)

        return carry

    lax.fori_loop(0, 16, look, 0)
    for c in late:
        c.wait()
    halves = []
    for piece in pieces(gain_ref[...]):
        halves += [piece[:, :84], piece[:, 84:168]]
    halves += [jnp.zeros((1, 84), F32)] * 2
    gains_ref[...] = jnp.concatenate(
        [jnp.zeros((8, 16), F32), jnp.concatenate(halves, axis=0), jnp.zeros((8, 28), F32)], axis=1
    )

    def attend_tile(p, t):
        span = pl.ds(pl.multiple_of(t * 256, 256), 256)
        rows = pl.ds(pl.multiple_of(t * 128, 128), 128)
        limit = jnp.where(flags[4 + p] != 0, t * 128, 1 << 20)
        row = lax.broadcasted_iota(jnp.int32, (256, 256), 0)
        col = lax.broadcasted_iota(jnp.int32, (256, 256), 1)
        visible = col <= (row & 127) + limit

        def scores(kv):
            q = jnp.concatenate(
                [q_ref[rows, (2 * kv + g) * 128 : (2 * kv + g + 1) * 128] for g in range(2)], axis=0
            )
            s = lax.dot_general(
                q,
                kbuf[p, :, kv * 128 : (kv + 1) * 128],
                (((1,), (1,)), ((), ())),
                preferred_element_type=F32,
            )
            return jnp.concatenate([s[:, :1792], jnp.where(visible, s[:, 1792:], NEG)], axis=1)

        for kv, s in enumerate([scores(0), scores(1)]):
            old = m_ref[kv, span, :]
            top = s[:, :128]
            for a in range(1, 16):
                top = jnp.maximum(top, s[:, a * 128 : (a + 1) * 128])
            new = jnp.maximum(old, jnp.max(top, axis=1, keepdims=True))
            keep = jnp.exp2((old - new) * EXP2_SCALE)
            w = jnp.exp2((s - jnp.concatenate([new] * 16, axis=1)) * EXP2_SCALE)
            part = w[:, :128]
            for a in range(1, 16):
                part = part + w[:, a * 128 : (a + 1) * 128]
            mixed = jnp.dot(
                w.astype(BF), vbuf[p, :, kv * 128 : (kv + 1) * 128], preferred_element_type=F32
            )
            m_ref[kv, span, :] = new
            l_ref[kv, span, :] = l_ref[kv, span, :] * keep + part
            acc_ref[kv, span, :] = acc_ref[kv, span, :] * keep + mixed

    def page(p, carry):
        for c in page_copies(p):
            c.wait()

        def tile(t, carry):
            @pl.when(flags[p * 2 + t] != 0)
            def _():
                attend_tile(p, t)

            return carry

        return lax.fori_loop(0, 2, tile, carry)

    lax.fori_loop(0, 2, page, 0)

    lane = lax.broadcasted_iota(jnp.int32, (128, 128), 1)

    def finish(t, carry):
        marks = jnp.concatenate([gains_ref[...]] * 16, axis=0)
        out_rows = pl.ds(pl.multiple_of(t * 128, 128), 128)
        for h in range(4):
            kv = h // 2
            rows = pl.ds(pl.multiple_of(t * 256 + (h % 2) * 128, 128), 128)
            total = jnp.sum(l_ref[kv, rows, :], axis=1, keepdims=True)
            some = total > 0.0
            safe = jnp.where(some, total, 1.0)
            level = jnp.where(some, m_ref[kv, rows, :][:, :1] * EXP2_SCALE + jnp.log2(safe), NEG)
            o_ref[out_rows, h * 128 : (h + 1) * 128] = (acc_ref[kv, rows, :] * (1.0 / safe)).astype(BF)
            for n, piece in enumerate(pieces(level)):
                marks = jnp.where(lane == h + 4 * n, piece, marks)
        o_ref[out_rows, 512:640] = marks.astype(BF)
        return carry

    lax.fori_loop(0, 2, finish, 0)


def in_hbm(array):
    return pltpu.with_memory_space_constraint(array, pltpu.HBM)


def attend(page_map, selected, gain, queries, keys, values):
    return pl.pallas_call(
        attend_kernel,
        out_shape=jax.ShapeDtypeStruct((256, 640), BF),
        in_specs=[HBM] * 6,
        out_specs=VMEM,
        scratch_shapes=[
            pltpu.SMEM((64,), jnp.int32),
            pltpu.SMEM((2, 8), jnp.int32),
            pltpu.VMEM((1, 168), F32),
            pltpu.VMEM((256, 512), BF),
            pltpu.VMEM((2, 2048, 256), BF),
            pltpu.VMEM((2, 2048, 256), BF),
            pltpu.SemaphoreType.DMA((4,)),
            pltpu.SemaphoreType.DMA((2,)),
            pltpu.SemaphoreType.DMA((2,)),
            pltpu.SMEM((8,), jnp.int32),
            pltpu.VMEM((8, 128), F32),
            pltpu.VMEM((2, 512, 128), F32),
            pltpu.VMEM((2, 512, 128), F32),
            pltpu.VMEM((2, 512, 128), F32),
        ],
        compiler_params=pltpu.CompilerParams(vmem_limit_bytes=40 << 20),
        cost_estimate=pl.CostEstimate(
            flops=4 * 10**9, transcendentals=4 * 10**6, bytes_accessed=10 * 2**20
        ),
        name="attend",
    )(in_hbm(page_map), in_hbm(selected), in_hbm(gain), in_hbm(queries), in_hbm(keys), in_hbm(values))


def merge_kernel(x_ref, o_ref, gain_ref):
    marks = x_ref[:, :, 512:640].astype(F32).reshape(256, 128).astype(BF)
    source = lax.broadcasted_iota(jnp.int32, (128, 128), 0)
    for h in range(4):
        spread = jnp.where((source < 12) & ((source & 3) == h), 1.0, 0.0).astype(BF)
        level = jnp.dot(marks, spread, preferred_element_type=F32).reshape(32, 8, 128)
        weight = jnp.exp2(level - jnp.max(level, axis=0, keepdims=True))
        mixed = jnp.sum(weight * x_ref[:, :, h * 128 : (h + 1) * 128].astype(F32), axis=0)
        o_ref[:, h * 128 : (h + 1) * 128] = (mixed / jnp.sum(weight, axis=0)).astype(BF)
    head = lax.axis_index("y") * NC + lax.axis_index("core")
    for k in range(NX):
        gain = x_ref[head * NX + k, :, 512:640].astype(F32)
        for half in range(2):
            gain_ref[k : k + 1, half * 84 : half * 84 + 84] = (
                gain[half : half + 1, 16:100]
                + gain[half + 2 : half + 3, 16:100]
                + gain[half + 4 : half + 5, 16:100]
            )


def packed(rows):
    rest = rows[:, 128:168]
    return jnp.concatenate(
        [
            rows[:, :128],
            jnp.concatenate([rest[:16], rest[16:], jnp.zeros((16, 48), rows.dtype)], axis=1),
        ],
        axis=0,
    )


def project_kernel(a_ref, w_ref, o_ref):
    block = lax.dot_general(
        a_ref[...], w_ref[...], (((1,), (1,)), ((), ())), preferred_element_type=F32
    )
    for h in range(NZ):
        o_ref[h] = packed(block[h * 32 : (h + 1) * 32]).astype(BF)


def stream_kernel(x_ref, r_ref, o_ref):
    total = jnp.sum(x_ref[...].astype(F32), axis=0) + packed(r_ref[...].astype(F32))
    o_ref[...] = total.astype(BF)


def gate_up(a, squares, g_ref, u_ref):
    lane = lax.broadcasted_iota(jnp.int32, (128, 64), 1)
    marks = jnp.zeros((128, 64), F32)
    for n, piece in enumerate(pieces(jnp.sum(squares, axis=1, keepdims=True))):
        marks = jnp.where(lane == n, piece, marks)
    gate = jnp.dot(a, g_ref[...], preferred_element_type=F32)
    up = jnp.dot(a, u_ref[...], preferred_element_type=F32)
    tail = jnp.concatenate([gate[:, 640:], up[:, 640:], marks], axis=1)
    return gate[:, :640].astype(BF), up[:, :640].astype(BF), tail.astype(BF)


def unpacked(block):
    rest = jnp.concatenate([block[..., 32:48, 0:40], block[..., 32:48, 40:80]], axis=-2)
    return block[..., :32, :], rest


def other_half_kernel(
    x_ref, gain_ref, g_ref, u_ref, o_ref, normed_ref, squares_ref, own_ref, own, squares, normed
):
    core = lax.axis_index("core")
    full = jnp.zeros((256, 128), F32)
    part = jnp.zeros((256, 40), F32)
    for x in range(NX):
        main, rest = unpacked(x_ref[:, x, :, :].astype(F32))
        main, rest = main.reshape(256, 128), rest.reshape(256, 40)
        first, second = slice(x * 168, x * 168 + 128), slice(x * 168 + 128, x * 168 + 168)
        full = full + main * main
        part = part + rest * rest
        normed[:, first] = (main * gain_ref[x : x + 1, 0:128]).astype(BF)
        normed[:, second] = (rest * gain_ref[x : x + 1, 128:168]).astype(BF)
        own[:, first], own[:, second] = unpacked(x_ref[lax.axis_index("z"), x, :, :].astype(F32))
    squares[...] = full + jnp.concatenate([part, jnp.zeros((256, 88), F32)], axis=1)
    theirs = pl.ds(pl.multiple_of((1 - core) * 128, 128), 128)
    mine = pl.ds(pl.multiple_of(core * 128, 128), 128)
    o_ref[:, :640], o_ref[:, 640:1280], o_ref[:, 1280:] = gate_up(
        normed[theirs, :], squares[theirs, :], g_ref, u_ref
    )
    normed_ref[...] = normed[mine, :]
    squares_ref[...] = squares[mine, :]
    own_ref[...] = own[pl.ds(pl.multiple_of(lax.axis_index("x") * 8, 8), 8), :].astype(BF)


def own_half_kernel(a_ref, squares_ref, g_ref, u_ref, o_ref):
    o_ref[:, :640], o_ref[:, 640:1280], o_ref[:, 1280:] = gate_up(
        a_ref[...], squares_ref[...], g_ref, u_ref
    )


def pair_kernel(a_ref, b_ref, o_ref):
    both = a_ref[...].astype(F32) + b_ref[...].astype(F32)
    o_ref[:, :1280] = both[:, :1280].astype(BF)
    tail = both[:, 1280:]
    lane = lax.broadcasted_iota(jnp.int32, (128, 128), 1)
    for n, piece in enumerate(pieces(tail[:, 64:65] + tail[:, 65:66] + tail[:, 66:67])):
        tail = jnp.where(lane == 64 + n, piece, tail)
    o_ref[:, 1280:] = tail.astype(BF)


def hidden_kernel(x_ref, o_ref):
    both = jnp.sum(x_ref[...].astype(F32), axis=0)
    squares = both[:, 1344:1345] + both[:, 1345:1346] + both[:, 1346:1347]
    factor = lax.rsqrt(squares / D + EPSILON)
    gate = jnp.concatenate([both[:, :640], both[:, 1280:1312]], axis=1) * factor
    up = jnp.concatenate([both[:, 640:1280], both[:, 1312:1344]], axis=1) * factor
    hidden = jax.nn.gelu(gate, approximate=True) * up
    tail = jnp.concatenate([hidden[g * 8 : (g + 1) * 8, 640:] for g in range(4)], axis=1)
    blocks = [hidden[:, j * 128 : (j + 1) * 128] for j in range(5)]
    rows = jnp.concatenate(blocks + [tail], axis=0).astype(BF)
    for k in range(NY * NC):
        o_ref[k] = rows


def down_kernel(a_ref, w_ref, o_ref):
    mains, tails = [], []
    for c in range(NC):
        for y in range(NY):
            k = y * NC + c
            blocks = [a_ref[k, j * 32 : (j + 1) * 32, :] for j in range(5)]
            mains.append(jnp.concatenate(blocks, axis=1))
            rest = a_ref[k, 160:168, :].astype(F32)
            tails += [rest[:, g * 32 : (g + 1) * 32] for g in range(4)]
    main = jnp.concatenate(mains, axis=0)
    tail = jnp.concatenate(tails, axis=0).astype(BF)
    total = jnp.dot(main, w_ref[:640, :], preferred_element_type=F32)
    total = total + jnp.dot(tail, w_ref[640:, :], preferred_element_type=F32)
    o_ref[...] = total.astype(BF)


def final_kernel(x_ref, s_ref, o_ref):
    o_ref[...] = (jnp.sum(x_ref[...].astype(F32), axis=0) + s_ref[...].astype(F32)).astype(BF)


def call(kernel, outs, specs, *args, scratch=()):
    outs = [jax.ShapeDtypeStruct(shape, dtype) for shape, dtype in outs]
    results = pl.pallas_call(
        kernel,
        out_shape=outs,
        in_specs=specs,
        out_specs=[VMEM] * len(outs),
        scratch_shapes=scratch,
        compiler_params=pltpu.CompilerParams(vmem_limit_bytes=32 << 20),
        name=kernel.__name__,
    )(*args)
    return results if len(outs) > 1 else results[0]


def exchange(parts, axis):
    return lax.all_to_all(parts, axis, split_axis=0, concat_axis=0, tiled=True)


def place(z, x, h):
    return (z * NX + x) * NY * NC + h


def shards(
    queries, keys, values, page_map, selected, residual_in, out_weight, norm_gain, gate_weight, up_weight, down_weight
):
    sent = attend(page_map, selected, norm_gain.reshape(1, 168), queries, keys, values)
    arrived = exchange(sent.reshape(32, 8, 640), CTX)
    share, gain = call(
        merge_kernel, [((8, 512), BF), ((NX, 168), F32)], [VMEM], arrived
    )
    attention = exchange(jnp.broadcast_to(share, (NZ * NX, 8, 512)), CTX).reshape(256, 512)
    partial = call(project_kernel, [((NZ, 48, 128), BF)], [VMEM, VMEM], attention, out_weight.T)
    projected = exchange(partial, HEADS)
    stream = call(stream_kernel, [((48, 128), BF)], [VMEM, VMEM], projected, residual_in)
    turned = lax.ppermute(
        stream,
        ALL,
        [(place(z, x, h), place(h, x, z)) for z in range(NZ) for x in range(NX) for h in range(NZ)],
    )
    rows = exchange(jnp.broadcast_to(turned, (NZ * NX, 48, 128)), CTX)
    half = ((128, 1408), BF)
    other, normed, squares, own_stream = call(
        other_half_kernel,
        [half, ((128, 672), BF), ((128, 128), F32), ((8, 672), BF)],
        [VMEM, VMEM, VMEM, VMEM],
        rows.reshape(NZ, NX, 48, 128),
        gain,
        gate_weight,
        up_weight,
        scratch=[pltpu.VMEM((32, 672), F32), pltpu.VMEM((256, 128), F32), pltpu.VMEM((256, 672), BF)],
    )
    received = lax.ppermute(other, "core", [(0, 1), (1, 0)])
    mine = call(own_half_kernel, [half], [VMEM] * 4, normed, squares, gate_weight, up_weight)
    pair = call(pair_kernel, [half], [VMEM, VMEM], mine, received)
    shared = exchange(pair.reshape(NY, 32, 1408), "y")
    hidden = exchange(call(hidden_kernel, [((NY * NC, 168, 128), BF)], [VMEM], shared), HEADS)
    down = call(
        down_kernel, [((256, 672), BF)], [VMEM, VMEM], hidden, down_weight
    )
    out_parts = exchange(down.reshape(32, 8, 672), CTX)
    return call(final_kernel, [((8, 672), BF)], [VMEM, VMEM], out_parts, own_stream)


def solution(mesh):
    fine = Mesh(mesh.devices.reshape(NZ, NX, NY, NC), ALL)
    in_specs = (
        P(None, HEADS),
        P(CTX, None, HEADS),
        P(CTX, None, HEADS),
        P(),
        P(),
        P(HEADS, CTX),
        P(HEADS, CTX),
        P(CTX),
        P(HEADS, CTX),
        P(HEADS, CTX),
        P(CTX, HEADS),
    )
    return jax.shard_map(shards, mesh=fine, in_specs=in_specs, out_specs=P(CTX, HEADS), check_vma=False)
```
